256 devices in a mesh: px: 16 (over y, x), py: 16 (over z, core).
Axes of the slice: x: 4, y: 4, z: 8, core: 2. Of those that a mesh axis runs over, the one named last changes fastest.
Arguments:
- source: float32 [8, 512, 2048], P(None, 'px', 'py'), may hold values from -12 to 12
- coefficient: float32 [8, 512, 2048], P(None, 'px', 'py'), may hold values from 0.25 to 4
- strip_rows: int32 [16], replicated, may hold values from 1 to 72, 128 in all
Outputs:
- solution: float32 [8, 512, 2048], P(None, 'px', 'py')
The draws below stay inside these ranges and needn't reach their ends.
Inputs may be any that keep to these rules, and one draw needn't show every extreme that they name: `strip_rows`: the entries sum to 128 and the largest is exactly 72.
All inputs are finite; a program needn't handle non-finite values.
Results may differ from the reference program's by a relative error of at most 0.00027.
Values sent between devices are 32-bit elements; how exact they have to be, the bound alone decides.
A program may use at most 128 MiB of HBM per device.

```python
import math
import jax
import jax.numpy as jnp
import numpy as np

NZ = 8
CYCLES = 2
PRE = 2
POST = 2
COARSE_SWEEPS = 6
NX = 512
NY = 2048
NX2 = 128
MOST = 72
STRIPS = 16


def draw_source(key, part):
    return 3.0 * jax.random.truncated_normal(key, -4.0, 4.0, (NZ, NX, NY), jnp.float32)


def block_levels(own_key, shape, split, smallest, top_value):
    factor_of, own = 1.0, jax.random.fold_in(own_key, 6)
    for axis_at, blocks in split:
        draws = jnp.exp(jax.random.uniform(jax.random.fold_in(own, axis_at), (blocks,), jnp.float32, smallest / len(split), top_value / len(split)))
        factor_of = factor_of * jnp.repeat(draws, shape[axis_at] // blocks).reshape([-1 if axis == axis_at else 1 for axis in range(len(shape))])
    return factor_of


def profile(count, total, most, skew):
    loads = [(1 << 20) // math.isqrt(grade ** skew) + 1 for grade in range(2, count + 1)]
    surplus, holding = total - most - (count - 1), [1] * (count - 1)
    while surplus > 0:
        movable = [i for i in range(count - 1) if holding[i] < most]
        mass, budget = sum([loads[i] for i in movable]), surplus
        for i in movable:
            addition = min(most - holding[i], max(1, budget * loads[i] // mass), surplus)
            holding[i] = holding[i] + addition
            surplus = surplus - addition
    return np.array([most] + holding)


def uneven(own_key, amount, total, bound, skew):
    if amount == 2:
        one = jax.random.randint(own_key, (), max(1, total - bound), min(bound, total - 1) + 1)
        return jnp.stack([one, total - one])
    lengths = jnp.asarray(profile(amount, total, bound, skew), jnp.int32)
    couples = (amount - 1) // 2
    source_of, sink = lengths[1:1 + 2 * couples:2], lengths[2:2 + 2 * couples:2]
    room = jnp.minimum(source_of - 1, bound - sink)
    passed = jax.random.randint(jax.random.fold_in(own_key, 1), (couples,), 0, 1 << 20) % (room + 1)
    lengths = lengths.at[1:1 + 2 * couples:2].set(source_of - passed).at[2:2 + 2 * couples:2].set(sink + passed)
    return lengths[jax.random.permutation(jax.random.fold_in(own_key, 2), amount)]


def setup_inputs(seed: int = 0) -> dict:
    keys = jax.random.split(jax.random.key(seed), 4)
    source = draw_source(jax.random.fold_in(keys[3], 71), 0)
    coefficient = jnp.clip(jnp.exp(math.log(4.0) - 2.7725887 * jax.random.uniform(keys[1], (NZ, NX, NY), jnp.float32) ** block_levels(keys[1], (NZ, NX, NY), ((1, 16), (2, 16)), -0.2, 0.2)), 0.25, 4.0)
    strip_rows = uneven(keys[2], STRIPS, NX2, MOST, 2).astype(jnp.int32)
    return dict(source=source, coefficient=coefficient, strip_rows=strip_rows)


relaxation = 0.8
z_coupling = 0.25


def pad_plain(values):
    return jnp.pad(values, ((0, 0), (1, 1), (1, 1)))


def face_arrays(conduct, z_factor):
    padded = pad_plain(conduct)
    face_west = 0.5 * (conduct + padded[:, :-2, 1:-1])
    face_east = 0.5 * (conduct + padded[:, 2:, 1:-1])
    face_south = 0.5 * (conduct + padded[:, 1:-1, :-2])
    face_north = 0.5 * (conduct + padded[:, 1:-1, 2:])
    vertical = z_factor * 0.5 * (conduct[:-1] + conduct[1:])
    zero_layer = jnp.zeros_like(conduct[:1])
    face_down = jnp.concatenate([zero_layer, vertical], axis=0)
    face_up = jnp.concatenate([vertical, zero_layer], axis=0)
    diagonal = face_west + face_east + face_south + face_north + face_down + face_up
    return [face_west, face_east, face_south, face_north, face_down, face_up, diagonal]


def update(values, values_pad, faces, source_term):
    face_west, face_east, face_south, face_north, face_down, face_up, diagonal, inverse = faces
    zero_layer = jnp.zeros_like(values[:1])
    value_down = jnp.concatenate([zero_layer, values[:-1]], axis=0)
    value_up = jnp.concatenate([values[1:], zero_layer], axis=0)
    beside = (face_west * values_pad[:, :-2, 1:-1] + face_east * values_pad[:, 2:, 1:-1]
              + face_south * values_pad[:, 1:-1, :-2] + face_north * values_pad[:, 1:-1, 2:]
              + face_down * value_down + face_up * value_up)
    return source_term - diagonal * values + beside


def relax_sweep(values, values_pad, faces, source_term):
    return values + relaxation * faces[7] * update(values, values_pad, faces, source_term)


def smooth(values, source_term, faces, count):
    for sweep_index in range(count):
        values = relax_sweep(values, pad_plain(values), faces, source_term)
    return values


def coarsen(values):
    layers, row_count, col_count = values.shape
    return 0.25 * values.reshape(layers, row_count // 2, 2, col_count // 2, 2).sum(axis=(2, 4))


def restrict(values):
    layers, row_count, col_count = values.shape
    return values.reshape(layers, row_count // 2, 2, col_count // 2, 2).sum(axis=(2, 4))


def prolong(values):
    return jnp.repeat(jnp.repeat(values, 2, axis=1), 2, axis=2)


def strip_ids(strip_rows, rows_global):
    ends = jnp.cumsum(strip_rows)
    return jnp.sum((rows_global[:, None] >= ends[None, :]).astype(jnp.int32), axis=1)


def level_faces(conduct, z_factor):
    faces = face_arrays(conduct, z_factor)
    faces.append(1.0 / faces[6])
    return faces


def reference(source, coefficient, strip_rows):
    mid_conduct = coarsen(coefficient)
    low_conduct = coarsen(mid_conduct)
    fine_faces = level_faces(coefficient, z_coupling)
    mid_faces = level_faces(mid_conduct, 4.0 * z_coupling)
    low_faces = face_arrays(low_conduct, 16.0 * z_coupling)
    row_ids = strip_ids(strip_rows, jnp.arange(NX2, dtype=jnp.int32))
    same_next = (row_ids[:-1] == row_ids[1:]).astype(jnp.float32)
    zero_one = jnp.zeros((1,), jnp.float32)
    keep_west = jnp.concatenate([zero_one, same_next])
    keep_east = jnp.concatenate([same_next, zero_one])
    low_faces[0] = low_faces[0] * keep_west[None, :, None]
    low_faces[1] = low_faces[1] * keep_east[None, :, None]
    low_faces.append(1.0 / low_faces[6])
    onehot = (row_ids[:, None] == jnp.arange(STRIPS, dtype=jnp.int32)[None, :]).astype(jnp.float32)
    diag_rows = jnp.sum(low_faces[6], axis=(0, 2))
    diag_total = jnp.sum(onehot * diag_rows[:, None], axis=0)
    solution = jnp.zeros_like(source)
    for cycle_index in range(CYCLES):
        solution = smooth(solution, source, fine_faces, PRE)
        mid_source = restrict(update(solution, pad_plain(solution), fine_faces, source))
        middle = smooth(jnp.zeros_like(mid_source), mid_source, mid_faces, PRE)
        low_source = restrict(update(middle, pad_plain(middle), mid_faces, mid_source))
        correction = smooth(jnp.zeros_like(low_source), low_source, low_faces, COARSE_SWEEPS)
        left_over = update(correction, pad_plain(correction), low_faces, low_source)
        res_rows = jnp.sum(left_over, axis=(0, 2))
        res_total = jnp.sum(onehot * res_rows[:, None], axis=0)
        shift_strip = res_total / diag_total
        shift_rows = jnp.sum(onehot * shift_strip[None, :], axis=1)
        correction = correction + shift_rows[None, :, None]
        middle = smooth(middle + prolong(correction), mid_source, mid_faces, POST)
        solution = smooth(solution + prolong(middle), source, fine_faces, POST)
    return solution
```

```python
import jax
import jax.numpy as jnp
from jax import lax
from jax.experimental import pallas as pl
from jax.experimental.pallas import tpu as pltpu
from jax.sharding import PartitionSpec as P

CYCLES = 2
COARSE_SWEEPS = 6
relaxation = 0.8
z_coupling = 0.25

MESH = pl.DeviceIdType.MESH

NZ = 8
ROWS = 32
LANES = 128
EDGE = 16
HALO = 12
FINE = ROWS + 2 * HALO
MID = FINE // 2
OWN2 = ROWS // 4
LOW = 3 * OWN2
SHIFTED = OWN2 + 8


def lanes_of(rows):
    return lax.broadcasted_iota(jnp.int32, (rows, NZ, LANES), 2)


def layers_of(rows):
    return lax.broadcasted_iota(jnp.int32, (rows, NZ, LANES), 1)


def beside_lanes(pair, step, tiles):
    lane = lanes_of(pair[0].shape[0])
    back = [pltpu.roll(part, step, 2) for part in pair]
    ahead = [pltpu.roll(part, LANES - step, 2) for part in pair]
    before, after = lane < step, lane >= LANES - step
    south = [jnp.where(before, back[1 - t], back[t]) for t in tiles]
    north = [jnp.where(after, ahead[1 - t], ahead[t]) for t in tiles]
    return south, north


def weighted(values, weights, row, rows, step, tiles=(0, 1)):
    pair = [values[t, pl.ds(row + 1, rows)] for t in (0, 1)]
    south, north = beside_lanes(pair, step, tiles)
    totals = []
    for at, t in enumerate(tiles):
        here = pl.ds(row, rows)
        total = weights[0, t, here] * values[t, pl.ds(row, rows)]
        total += weights[1, t, here] * values[t, pl.ds(row + 2, rows)]
        total += weights[2, t, here] * south[at]
        total += weights[3, t, here] * north[at]
        total += weights[4, t, here] * pltpu.roll(pair[t], 1, 1)
        total += weights[5, t, here] * pltpu.roll(pair[t], NZ - 1, 1)
        totals.append(total)
    return [pair[t] for t in tiles], totals


def loop(count, body):
    def step(index, nothing):
        body(index)
        return nothing

    lax.fori_loop(0, count, step, 0)


def sweep(values, new, weights, right, first, count, rows, step):
    def body(index):
        row = first + index * rows
        old, total = weighted(values, weights, row, rows, step)
        for t in (0, 1):
            base = (1.0 - relaxation) * old[t] + total[t]
            if right is not None:
                base += right[t, pl.ds(row, rows)]
            new[t, pl.ds(row + 1, rows)] = base

    loop(count, body)


def make_weights(conduct, weights, row, rows, step, z_factor, keep=None):
    pair = [conduct[t, pl.ds(row + 1, rows)] for t in (0, 1)]
    south, north = beside_lanes(pair, step, (0, 1))
    layer = layers_of(rows)
    inverses, diagonals = [], []
    for t in (0, 1):
        own = pair[t]
        faces = [
            0.5 * (own + conduct[t, pl.ds(row, rows)]),
            0.5 * (own + conduct[t, pl.ds(row + 2, rows)]),
            0.5 * (own + south[t]),
            0.5 * (own + north[t]),
            jnp.where(layer > 0, (0.5 * z_factor) * (own + pltpu.roll(own, 1, 1)), 0.0),
            jnp.where(layer < NZ - 1, (0.5 * z_factor) * (own + pltpu.roll(own, NZ - 1, 1)), 0.0),
        ]
        diagonal = faces[0] + faces[1] + faces[2] + faces[3] + faces[4] + faces[5]
        inside = own > 0.0
        inverse = jnp.where(inside, relaxation / jnp.where(inside, diagonal, 1.0), 0.0)
        if keep is not None:
            faces[0] = faces[0] * keep[pl.ds(row, rows)]
            faces[1] = faces[1] * keep[pl.ds(row + 1, rows)]
        for side in range(6):
            weights[side, t, pl.ds(row, rows)] = inverse * faces[side]
        inverses.append(inverse)
        diagonals.append(diagonal)
    return inverses, diagonals


def pair_rows(values):
    rows = values.shape[0]
    return jnp.sum(values.reshape(rows // 2, 2, NZ, LANES), axis=1)


def pair_lanes(values, step):
    lane = lanes_of(values.shape[0])
    other = jnp.where(
        (lane // step) % 2 == 0, pltpu.roll(values, LANES - step, 2), pltpu.roll(values, step, 2)
    )
    return values + other


def twice_rows(values):
    rows = values.shape[0]
    wide = jnp.broadcast_to(values[:, None], (rows, 2, NZ, LANES))
    return wide.reshape(2 * rows, NZ, LANES)


def roll_lanes(tile, amount):
    amount = amount % LANES
    return tile if amount == 0 else pltpu.roll(tile, amount, 1)


def pack_edges(block, group, right_side):
    lane = lax.broadcasted_iota(jnp.int32, (NZ, LANES), 1)
    packed = None
    for j in range(8):
        moved = roll_lanes(block[8 * group + j], EDGE * j + (EDGE if right_side else 0))
        packed = moved if packed is None else jnp.where(lane // EDGE == j, moved, packed)
    return packed


def unpack_edges(left, right, j):
    lane = lax.broadcasted_iota(jnp.int32, (NZ, LANES), 1)
    from_right = roll_lanes(right, -EDGE * j)
    from_left = roll_lanes(left, -EDGE * (j + 1))
    return jnp.where(lane < EDGE, from_right, jnp.where(lane >= LANES - EDGE, from_left, 0.0))


def pack_quads(rows):
    lane = lax.broadcasted_iota(jnp.int32, (NZ, LANES), 1) % 4
    out = rows[3]
    for m in range(3):
        out = jnp.where(lane == m, rows[m], out)
    return out


def unpack_quad(packed, m):
    lane = lax.broadcasted_iota(jnp.int32, (NZ, LANES), 1) % 4
    one = roll_lanes(jnp.where(lane == m, packed, 0.0), -m)
    one = one + roll_lanes(one, 1)
    return one + roll_lanes(one, 2)


class Exchange:
    def __init__(self, depth, extra):
        self.depth, self.extra = depth, extra
        sizes = [depth + extra] * 2 + [4 + extra] * 2 + [2 + extra] * 4
        self.at = [sum(sizes[:i]) for i in range(9)]

    def stage_rows(self, send, block):
        send[0:self.depth] = block[ROWS - self.depth:ROWS]
        send[self.depth + self.extra:2 * self.depth + self.extra] = block[0:self.depth]

    def stage_edges(self, edges, block):
        for side in (0, 1):
            for group in range(4):
                at = group if group < 2 else group + self.extra
                edges[side, at] = pack_edges(block, group, side == 1)

    def stage_extra(self, send, edges, at, tile):
        send[self.depth + at] = tile
        for side in (0, 1):
            edges[side, 2 + at] = tile

    def start(self, send, edges, got, send_sem, got_sem, near):
        n, x, at = self.depth, self.extra, self.at
        top, bottom = pl.ds(0, 2 + x), pl.ds(2, 2 + x)
        moves = [
            (send.at[pl.ds(0, n + x)], 0, (1, 0)),
            (send.at[pl.ds(n, n + x)], 1, (-1, 0)),
            (edges.at[1], 2, (0, 1)),
            (edges.at[0], 3, (0, -1)),
            (edges.at[1, bottom], 4, (1, 1)),
            (edges.at[0, bottom], 5, (1, -1)),
            (edges.at[1, top], 6, (-1, 1)),
            (edges.at[0, top], 7, (-1, -1)),
        ]
        for source, slot, way in moves:
            pltpu.make_async_remote_copy(
                src_ref=source,
                dst_ref=got.at[pl.ds(at[slot], at[slot + 1] - at[slot])],
                send_sem=send_sem,
                recv_sem=got_sem,
                device_id=near(*way),
                device_id_type=MESH,
            ).start()

    def unpack(self, got, put_rows, put_beside):
        n, x, at = self.depth, self.extra, self.at
        put_rows(HALO - n, n, got[at[0]:at[0] + n])
        put_rows(HALO + ROWS, n, got[at[1] + x:at[1] + x + n])
        for i in range(FINE):
            if i < HALO:
                source = ROWS - HALO + i
                offset = at[4] + x - 2, at[5] + x - 2
            elif i < HALO + ROWS:
                source = i - HALO
                shift = x if source >= ROWS // 2 else 0
                offset = at[2] + shift, at[3] + shift
            else:
                source = i - HALO - ROWS
                offset = at[6], at[7]
            group, j = divmod(source, 8)
            put_beside(i, unpack_edges(got[offset[0] + group], got[offset[1] + group], j))

    def extras(self, got, a, b, q):
        n, x, at = self.depth, self.extra, self.at
        where = {
            (-1, 0): at[0] + n,
            (1, 0): at[1],
            (0, -1): at[2] + 2,
            (0, 1): at[3] + 2,
            (-1, -1): at[4],
            (-1, 1): at[5],
            (1, -1): at[6] + 2,
            (1, 1): at[7] + 2,
        }
        return got[where[(a, b)] + q]


AROUND = [(a, b) for a in (-1, 0, 1) for b in (-1, 0, 1) if (a, b) != (0, 0)]
FOR_K = Exchange(HALO, 2)
FOR_F = Exchange(HALO - 2, 0)
FOR_S = Exchange(HALO - 1, 0)


def kernel(strip_ref, source_ref, coefficient_ref, out_ref,
           k_own, f_own, s_own, k_send, f_send, s_send, k_edge, f_edge, s_edge,
           k_got, f_got, s_got,
           k0, c0, g0, d0, va, vb, k1, c1, i1, g1, d1, ua, ub, k2, c2, i2, g2, ea, eb,
           weight, diag_sum, keep, shifts, pick, l_own, l_send, l_got, one_send, one_got, two_send,
           two_got, sems):
    px, py = lax.axis_index("px"), lax.axis_index("py")
    size_x, size_y = lax.axis_size("px"), lax.axis_size("py")
    strips = strip_ref.shape[0]

    def near(a, b):
        return (lax.rem(px + a + size_x, size_x), lax.rem(py + b + size_y, size_y))

    peers = [(0, b) for b in range(1, size_y)] + [(a, 0) for a in range(1, size_x)]
    peers += [way for way in AROUND if way[0] and way[1]]
    barrier = pltpu.get_barrier_semaphore()
    for way in peers:
        pl.semaphore_signal(barrier, inc=1, device_id=near(*way), device_id_type=MESH)

    def arrived(buffer, sem):
        pltpu.make_async_copy(buffer, buffer, sem).wait()

    for r in range(ROWS):
        k_own[r] = coefficient_ref[pl.ds(r, NZ, stride=ROWS), :]
        f_own[r] = source_ref[pl.ds(r, NZ, stride=ROWS), :]

    zero = jnp.zeros((NZ, LANES), jnp.float32)
    FOR_K.stage_rows(k_send, k_own)
    FOR_K.stage_edges(k_edge, k_own)
    for q in (0, 1):
        mids = 0.25 * pair_lanes(pair_rows(k_own[16 * q:16 * q + 16]), 1)
        lows = 0.25 * pair_lanes(pair_rows(mids), 2)
        k2[0, 1 + OWN2 + 4 * q:1 + OWN2 + 4 * q + 4] = lows
        FOR_K.stage_extra(k_send, k_edge, q, pack_quads([lows[m] for m in range(4)]))
    FOR_F.stage_rows(f_send, f_own)
    FOR_F.stage_edges(f_edge, f_own)
    pl.semaphore_wait(barrier, len(peers))
    FOR_K.start(k_send, k_edge, k_got, sems.at[0], sems.at[1], near)
    FOR_F.start(f_send, f_edge, f_got, sems.at[2], sems.at[3], near)

    ends, total = [], jnp.int32(0)
    for c in range(strips):
        total = total + strip_ref[c]
        ends.append(total)
    sub = lax.broadcasted_iota(jnp.int32, (8, LANES), 0)
    lane = lax.broadcasted_iota(jnp.int32, (8, LANES), 1)

    def strip_of(rows):
        found = jnp.zeros_like(rows)
        for end in ends:
            found = found + jnp.where(rows >= end, 1, 0)
        return found

    for tile in range(4):
        rows = OWN2 * px - OWN2 + 8 * tile + sub
        kept = jnp.ones((8, LANES), jnp.float32)
        for end in ends:
            kept = jnp.where(rows == end, 0.0, kept)
        for i in range(8 if tile < 3 else 1):
            keep[8 * tile + i] = jnp.broadcast_to(kept[i:i + 1], (NZ, LANES))
    lane_strip = strip_of(lane)
    for tile in (0, 1):
        rows = jnp.clip(OWN2 * px - 4 + 8 * tile + sub, 0, OWN2 * size_x - 1)
        pick[tile] = jnp.where(strip_of(rows) == lane_strip, 1.0, 0.0)

    for ref, end in ((k0, FINE), (va, FINE), (vb, FINE), (k1, MID), (ua, MID), (ub, MID),
                     (k2, LOW), (ea, LOW), (eb, LOW)):
        for t in (0, 1):
            ref[t, 0] = zero
            ref[t, end + 1] = zero

    wide_lane = lax.broadcasted_iota(jnp.int32, (NZ, LANES), 1)
    inner_x = (px > 0, px < size_x - 1)
    inner_y = jnp.where(
        wide_lane < LANES // 2,
        jnp.where(py < size_y - 1, 1.0, 0.0), jnp.where(py > 0, 1.0, 0.0)
    )
    row_in = [jnp.where(flag, 1.0, 0.0) for flag in inner_x]

    def put_k_rows(first, rows, values):
        k0[0, 1 + first:1 + first + rows] = values * row_in[0 if first < HALO else 1]

    def put_k_beside(i, tile):
        tile = tile * inner_y
        if i < HALO or i >= HALO + ROWS:
            tile = tile * row_in[0 if i < HALO else 1]
        k0[1, 1 + i] = tile

    k0[0, 1 + HALO:1 + HALO + ROWS] = k_own[...]
    arrived(k_got, sems.at[1])
    FOR_K.unpack(k_got, put_k_rows, put_k_beside)

    def low_tiles(get, put):
        for at, a in enumerate((-1, 0, 1)):
            for q in (0, 1):
                if a != 0:
                    tile = get(a, 0, q)
                    for m in range(4):
                        put(0, OWN2 * at + 4 * q + m, a, unpack_quad(tile, m))
                tile = jnp.where(wide_lane < LANES // 2, get(a, 1, q), get(a, -1, q))
                for m in range(4):
                    put(1, OWN2 * at + 4 * q + m, a, unpack_quad(tile, m))

    def put_k2(t, row, a, tile):
        if t == 1:
            tile = tile * inner_y
        if a != 0:
            tile = tile * row_in[0 if a < 0 else 1]
        k2[t, 1 + row] = tile

    low_tiles(lambda a, b, q: FOR_K.extras(k_got, a, b, q), put_k2)

    def weights_2(index):
        row = index * 8
        inverse, diagonal = make_weights(k2, c2, row, 8, 4, 16.0 * z_coupling, keep)
        for t in (0, 1):
            i2[t, pl.ds(row, 8)] = inverse[t]
            ea[t, pl.ds(row + 1, 8)] = jnp.where(k2[t, pl.ds(row + 1, 8)] > 0.0, 1.0, 0.0)

        @pl.when(index == 1)
        def _():
            diag_sum[...] = jnp.sum(diagonal[0], axis=1)

    loop(3, weights_2)

    def weights_0(index):
        row = index * 8
        inverse, diagonal = make_weights(k0, c0, row, 8, 1, z_coupling)
        for t in (0, 1):
            g0[t, pl.ds(row, 8)] = inverse[t]
            d0[t, pl.ds(row, 8)] = (1.0 / relaxation) * diagonal[t]
            half = pl.multiple_of(index * 4, 4)
            k1[t, pl.ds(half + 1, 4)] = 0.25 * pair_lanes(
                pair_rows(k0[t, pl.ds(row + 1, 8)]), 1)

    loop(FINE // 8, weights_0)

    def weights_1(index):
        row = index * 7
        inverse, diagonal = make_weights(k1, c1, row, 7, 2, 4.0 * z_coupling)
        for t in (0, 1):
            i1[t, pl.ds(row, 7)] = inverse[t]
            d1[t, pl.ds(row, 7)] = (1.0 / relaxation) * diagonal[t]

    loop(MID // 7, weights_1)

    for turn in range(COARSE_SWEEPS):
        here, there = (ea, eb) if turn % 2 == 0 else (eb, ea)
        sweep(here, there, c2, None, 0, 3, 8, 4)
    done = ea if COARSE_SWEEPS % 2 == 0 else eb
    weight[...] = done[0, 1 + OWN2:1 + 2 * OWN2]

    va[0, 1 + HALO:1 + HALO + ROWS] = f_own[...]

    def put_f_rows(first, rows, values):
        va[0, 1 + first:1 + first + rows] = values

    def put_f_beside(i, tile):
        va[1, 1 + i] = tile

    for i in (0, 1, FINE - 2, FINE - 1):
        va[0, 1 + i] = zero
    arrived(f_got, sems.at[3])
    FOR_F.unpack(f_got, put_f_rows, put_f_beside)

    def first_sweep(index):
        row = index * 8
        for t in (0, 1):
            start = g0[t, pl.ds(row, 8)] * va[t, pl.ds(row + 1, 8)]
            g0[t, pl.ds(row, 8)] = start
            va[t, pl.ds(row + 1, 8)] = start

    loop(FINE // 8, first_sweep)

    dens = None
    used = 4
    for cycle in range(CYCLES):
        if cycle > 0:
            sweep(va, vb, c0, g0, 0, FINE // 8, 8, 1)
            sweep(vb, va, c0, g0, 0, FINE // 8, 8, 1)
            fine, spare = va, vb
        else:
            sweep(va, vb, c0, g0, 0, FINE // 8, 8, 1)
            fine, spare = vb, va

        def down(index, fine=fine):
            row = index * 8
            old, total = weighted(fine, c0, row, 8, 1)
            for t in (0, 1):
                here = pl.ds(row, 8)
                rest = d0[t, here] * (g0[t, here] - relaxation * old[t] + total[t])
                half = pl.multiple_of(index * 4, 4)
                start = i1[t, pl.ds(half, 4)] * pair_lanes(pair_rows(rest), 1)
                g1[t, pl.ds(half, 4)] = start
                ua[t, pl.ds(half + 1, 4)] = start

        loop(FINE // 8, down)
        sweep(ua, ub, c1, g1, 0, MID // 7, 7, 2)

        def lower(index):
            row = HALO // 2 + index * 8
            old, total = weighted(ub, c1, row, 8, 2, (0,))
            here = pl.ds(row, 8)
            rest = d1[0, here] * (g1[0, here] - relaxation * old[0] + total[0])
            l_own[pl.ds(index * 4, 4)] = pair_lanes(pair_rows(rest), 2)

        loop(2, lower)

        sums = jnp.sum(weight[...] * l_own[...], axis=1)
        if cycle == 0:
            sums = jnp.where(lane % 4 == 0, sums, jnp.where(lane % 4 == 1, diag_sum[...], 0.0))
        one_send[cycle] = sums
        wide = 2 if cycle == 0 else 1

        def spread(source, got, sem, ways):
            for slot, way in enumerate(ways):
                pltpu.make_async_remote_copy(
                    src_ref=source,
                    dst_ref=got.at[slot],
                    send_sem=sems.at[sem],
                    recv_sem=sems.at[sem + 1],
                    device_id=near(*way),
                    device_id_type=MESH,
                ).start()

        one_in = one_got.at[cycle]
        spread(one_send.at[cycle], one_in, used, [(0, b) for b in range(1, size_y)])
        for q in (0, 1):
            l_send[cycle, q] = pack_quads([l_own[4 * q + m] for m in range(4)])
        low_in = l_got.at[cycle]
        spread(l_send.at[cycle], low_in, used + 2, [(-a, -b) for a, b in AROUND])
        arrived(one_in, sems.at[used + 1])
        sums = one_send[cycle] + jnp.sum(one_got[cycle], axis=0)
        mine = lane == OWN2 * px + sub
        for part in range(wide):
            column = jnp.sum(jnp.where(lane % 4 == part, sums, 0.0), axis=1, keepdims=True)
            two_send[cycle, part] = jnp.where(mine, column, 0.0)
        two_in = two_got.at[cycle, :, pl.ds(0, wide)] if wide == 1 else two_got.at[cycle]
        two_out = two_send.at[cycle, pl.ds(0, wide)]
        spread(two_out, two_in, used + 4, [(a, 0) for a in range(1, size_x)])

        arrived(low_in, sems.at[used + 3])

        def put_low(t, row, a, tile):
            start = i2[t, row] * tile
            g2[t, row] = start
            ea[t, 1 + row] = start

        low_tiles(lambda a, b, q: l_got[cycle, AROUND.index((a, b)), q], put_low)
        for r in range(OWN2):
            put_low(0, OWN2 + r, 0, l_own[r])
        for turn in range(COARSE_SWEEPS - 1):
            here, there = (ea, eb) if turn % 2 == 0 else (eb, ea)
            sweep(here, there, c2, g2, 0, 3, 8, 4)
        low = eb if COARSE_SWEEPS % 2 == 0 else ea

        arrived(two_in, sems.at[used + 5])
        parts = []
        for part in range(wide):
            both = two_send[cycle, part] + jnp.sum(two_got[cycle, :, part], axis=0)
            row_sums = jnp.broadcast_to(jnp.sum(both, axis=0, keepdims=True), (8, LANES))
            parts.append([jnp.sum(pick[tile] * row_sums, axis=1, keepdims=True) for tile in (0, 1)])
        if cycle == 0:
            dens = parts[1]
        for tile in (0, 1):
            shift = jnp.broadcast_to(parts[0][tile] / dens[tile], (8, LANES))
            for i in range(8):
                shifts[8 * tile + i] = jnp.broadcast_to(shift[i:i + 1], (NZ, LANES))

        def up_1(index):
            row = 2 + index * 8
            from_low = HALO // 4 + index * 4 + 3
            for t in (0, 1):
                here = pl.ds(from_low + 1, 4)
                inside = k2[t, here] > 0.0
                moved = jnp.where(inside, shifts[pl.ds(index * 4 + 2, 4)], 0.0)
                ua[t, pl.ds(row + 1, 8)] = ub[t, pl.ds(row + 1, 8)] + twice_rows(
                    low[t, here] + moved)

        loop(3, up_1)
        sweep(ua, ub, c1, g1, 2, 3, 8, 2)
        sweep(ub, ua, c1, g1, 2, 3, 8, 2)

        def up_0(index, fine=fine, spare=spare):
            row = 8 + index * 8
            for t in (0, 1):
                here = pl.ds(row + 1, 8)
                spare[t, here] = fine[t, here] + twice_rows(ua[t, pl.ds(4 + index * 4 + 1, 4)])

        loop(5, up_0)
        sweep(spare, fine, c0, g0, 8, 5, 8, 1)

        def last(index, fine=fine):
            row = HALO + index * 8
            old, total = weighted(fine, c0, row, 8, 1, (0,))
            done = g0[0, pl.ds(row, 8)] + (1.0 - relaxation) * old[0] + total[0]
            s_own[pl.ds(index * 8, 8)] = done

        loop(ROWS // 8, last)
        used += 6

        if cycle < CYCLES - 1:
            FOR_S.stage_rows(s_send, s_own)
            FOR_S.stage_edges(s_edge, s_own)
            FOR_S.start(s_send, s_edge, s_got, sems.at[used], sems.at[used + 1], near)
            va[0, 1 + HALO:1 + HALO + ROWS] = s_own[...]
            va[0, 1] = zero
            va[0, FINE] = zero

            def put_s_rows(first, rows, values):
                inside = k0[0, 1 + first:1 + first + rows] > 0.0
                va[0, 1 + first:1 + first + rows] = jnp.where(inside, values, 0.0)

            def put_s_beside(i, tile):
                va[1, 1 + i] = jnp.where(k0[1, 1 + i] > 0.0, tile, 0.0)

            arrived(s_got, sems.at[used + 1])
            FOR_S.unpack(s_got, put_s_rows, put_s_beside)
            used += 2

    for r in range(ROWS):
        out_ref[pl.ds(r, NZ, stride=ROWS), :] = s_own[r]

    arrived(k_got, sems.at[0])
    arrived(f_got, sems.at[2])
    arrived(one_got.at[0], sems.at[4])
    arrived(l_got.at[0], sems.at[6])
    arrived(two_got.at[0], sems.at[8])
    arrived(s_got, sems.at[10])
    arrived(one_got.at[1], sems.at[12])
    arrived(l_got.at[1], sems.at[14])
    arrived(two_got.at[1, :, pl.ds(0, 1)], sems.at[16])


def vmem(*shape):
    return pltpu.VMEM(shape + (NZ, LANES), jnp.float32)


def shards(source, coefficient, strip_rows):
    size_x, size_y = lax.axis_size("px"), lax.axis_size("py")
    flat = (NZ * ROWS, LANES)
    scratch = [vmem(ROWS), vmem(ROWS), vmem(ROWS)]
    scratch += [vmem(2 * e.depth + e.extra) for e in (FOR_K, FOR_F, FOR_S)]
    scratch += [vmem(2, 4 + e.extra) for e in (FOR_K, FOR_F, FOR_S)]
    scratch += [vmem(e.at[8]) for e in (FOR_K, FOR_F, FOR_S)]
    scratch += [vmem(2, FINE + 2), vmem(6, 2, FINE), vmem(2, FINE), vmem(2, FINE)]
    scratch += [vmem(2, FINE + 2), vmem(2, FINE + 2)]
    scratch += [vmem(2, MID + 2), vmem(6, 2, MID), vmem(2, MID), vmem(2, MID), vmem(2, MID)]
    scratch += [vmem(2, MID + 2), vmem(2, MID + 2)]
    scratch += [vmem(2, LOW + 2), vmem(6, 2, LOW), vmem(2, LOW), vmem(2, LOW)]
    scratch += [vmem(2, LOW + 2), vmem(2, LOW + 2)]
    scratch += [vmem(OWN2), pltpu.VMEM((8, LANES), jnp.float32), vmem(LOW + 1), vmem(SHIFTED)]
    scratch += [vmem(2), vmem(OWN2), vmem(2, 2), vmem(2, 8, 2), vmem(2), vmem(2, size_y - 1)]
    scratch += [vmem(2, 2), vmem(2, size_x - 1, 2)]
    scratch += [pltpu.SemaphoreType.DMA((18,))]
    whole = pl.BlockSpec(memory_space=pltpu.VMEM)
    done = pl.pallas_call(
        kernel,
        out_shape=jax.ShapeDtypeStruct(flat, jnp.float32),
        in_specs=[pl.BlockSpec(memory_space=pltpu.SMEM), whole, whole],
        out_specs=whole,
        scratch_shapes=scratch,
        compiler_params=pltpu.CompilerParams(
            collective_id=0, has_side_effects=True, vmem_limit_bytes=32 << 20
        ),
        name="cycles",
    )(strip_rows, source.reshape(flat), coefficient.reshape(flat))
    return done.reshape(source.shape)


def solution(mesh):
    placed = (P(None, "px", "py"), P(None, "px", "py"), P())
    return jax.shard_map(
        shards, mesh=mesh, in_specs=placed, out_specs=P(None, "px", "py"), check_vma=False
    )
```

```python
import jax
import jax.numpy as jnp
from jax import lax
from jax.experimental import pallas as pl
from jax.experimental.pallas import tpu as pltpu
from jax.sharding import PartitionSpec as P

CYCLES = 2
COARSE_SWEEPS = 6
relaxation = 0.8
z_coupling = 0.25

MESH = pl.DeviceIdType.MESH

NZ = 8
ROWS = 32
LANES = 128
EDGE = 16
HALO = 12
FINE = ROWS + 2 * HALO
MID = FINE // 2
OWN2 = ROWS // 4
LOW_TILES = 3 * OWN2 // 2
MID_LANE, MID_OWN = 32, 64
LOW_LANE, LOW_OWN, HALF = 8, 32, 64


def lanes_of(rows):
    return lax.broadcasted_iota(jnp.int32, (rows, NZ, LANES), 2)


def layers_of(rows):
    return lax.broadcasted_iota(jnp.int32, (rows, NZ, LANES), 1)


def beside_lanes(parts, tiles):
    back = [pltpu.roll(part, 1, 2) for part in parts]
    ahead = [pltpu.roll(part, LANES - 1, 2) for part in parts]
    if len(parts) == 1:
        return back, ahead
    lane = lanes_of(parts[0].shape[0])
    before, after = lane < 1, lane >= LANES - 1
    south = [jnp.where(before, back[1 - t], back[t]) for t in tiles]
    north = [jnp.where(after, ahead[1 - t], ahead[t]) for t in tiles]
    return south, north


def six_sum(weights, t, here, west, own, east, south, north):
    total = weights[0, t, here] * west + weights[1, t, here] * east
    total += weights[4, t, here] * pltpu.roll(own, 1, 1)
    total += weights[5, t, here] * pltpu.roll(own, NZ - 1, 1)
    total += weights[2, t, here] * south
    total += weights[3, t, here] * north
    return total


def weighted(values, weights, row, rows, tiles):
    parts = [values[t, row + 1:row + 1 + rows] for t in range(values.shape[0])]
    south, north = beside_lanes(parts, tiles)
    totals = []
    for at, t in enumerate(tiles):
        west, east = values[t, row:row + rows], values[t, row + 2:row + 2 + rows]
        totals.append(six_sum(weights, t, slice(row, row + rows), west, parts[t], east,
                              south[at], north[at]))
    return [parts[t] for t in tiles], totals


def sweep(values, new, weights, right, first, count, rows):
    tiles = range(values.shape[0])
    for index in range(count):
        row = first + index * rows
        old, total = weighted(values, weights, row, rows, tiles)
        for t in tiles:
            new[t, row + 1:row + 1 + rows] = (
                right[t, row:row + rows] + (1.0 - relaxation) * old[t] + total[t])


def scaled_faces(own, west, east, south, north, z_factor, keep=None):
    layer = layers_of(own.shape[0])
    half_z = 0.5 * z_factor
    faces = [
        0.5 * (own + west), 0.5 * (own + east), 0.5 * (own + south), 0.5 * (own + north),
        jnp.where(layer > 0, half_z * (own + pltpu.roll(own, 1, 1)), 0.0),
        jnp.where(layer < NZ - 1, half_z * (own + pltpu.roll(own, NZ - 1, 1)), 0.0),
    ]
    diagonal = faces[0] + faces[1] + faces[2] + faces[3] + faces[4] + faces[5]
    inside = own > 0.0
    inverse = jnp.where(inside, relaxation / jnp.where(inside, diagonal, 1.0), 0.0)
    if keep is not None:
        faces[0], faces[1] = faces[0] * keep[0], faces[1] * keep[1]
    return [inverse * face for face in faces], inverse, diagonal


def make_weights(conduct, weights, row, rows, z_factor):
    tiles = range(conduct.shape[0])
    parts = [conduct[t, row + 1:row + 1 + rows] for t in tiles]
    south, north = beside_lanes(parts, tiles)
    inverses, diagonals = [], []
    for t in tiles:
        west, east = conduct[t, row:row + rows], conduct[t, row + 2:row + 2 + rows]
        faces, inverse, diagonal = scaled_faces(
            parts[t], west, east, south[t], north[t], z_factor)
        for side in range(6):
            weights[side, t, row:row + rows] = faces[side]
        inverses.append(inverse)
        diagonals.append(diagonal)
    return inverses, diagonals


def low_rows_beside(values):
    first = pltpu.roll(values[LOW_TILES - 1:], HALF, 2)
    last = pltpu.roll(values[:1], HALF, 2)
    west = jnp.concatenate([first, values[:-1]], axis=0)
    east = jnp.concatenate([values[1:], last], axis=0)
    return west, east


def low_sum(values, weights):
    west, east = low_rows_beside(values)
    back, ahead = pltpu.roll(values, 1, 2), pltpu.roll(values, LANES - 1, 2)
    return six_sum(weights, 0, slice(0, LOW_TILES), west, values, east, back, ahead)


def pair_rows(values):
    rows = values.shape[0]
    return jnp.sum(values.reshape(rows // 2, 2, NZ, LANES), axis=1)


def twice_rows(values):
    rows = values.shape[0]
    wide = jnp.broadcast_to(values[:, None], (rows, 2, NZ, LANES))
    return wide.reshape(2 * rows, NZ, LANES)


def select_lanes(values, chosen):
    rows = values.shape[0]
    flat = jnp.dot(
        values.reshape(rows * NZ, LANES), chosen, precision=lax.Precision.HIGHEST,
        preferred_element_type=jnp.float32)
    return flat.reshape(rows, NZ, LANES)


def roll_lanes(tile, amount):
    amount = amount % LANES
    return tile if amount == 0 else pltpu.roll(tile, amount, 1)


def pack_edges(block, group, right_side):
    lane = lax.broadcasted_iota(jnp.int32, (NZ, LANES), 1)
    packed = None
    for j in range(8):
        moved = roll_lanes(block[8 * group + j], EDGE * j + (EDGE if right_side else 0))
        packed = moved if packed is None else jnp.where(lane // EDGE == j, moved, packed)
    return packed


def unpack_edges(left, right, j):
    lane = lax.broadcasted_iota(jnp.int32, (NZ, LANES), 1)
    from_right = roll_lanes(right, -EDGE * j)
    from_left = roll_lanes(left, -EDGE * (j + 1))
    return jnp.where(lane < EDGE, from_right, jnp.where(lane >= LANES - EDGE, from_left, 0.0))


def pack_low(rows):
    out = rows[0]
    for m in range(1, 4):
        out = out + roll_lanes(rows[m], LOW_OWN * m)
    return out


def unpack_low(get, scale_left, scale_right, scale_rows):
    lane = lax.broadcasted_iota(jnp.int32, (NZ, LANES), 1)
    rows = []
    for a in (-1, 0, 1):
        for q in (0, 1):
            own = get(a, 0, q)
            left, right = roll_lanes(get(a, -1, q), -LOW_OWN), roll_lanes(get(a, 1, q), LOW_OWN)
            if scale_left is not None:
                left, right = left * scale_left, right * scale_right
            if scale_rows is not None and a != 0:
                scale = scale_rows[0 if a < 0 else 1]
                own, left, right = own * scale, left * scale, right * scale
            for m in range(4):
                row = len(rows)
                away = (lane - LOW_OWN * m) % LANES
                tile = jnp.where(
                    away < LOW_OWN, own,
                    jnp.where(away < LOW_OWN + LOW_LANE, right,
                              jnp.where(away >= LANES - LOW_LANE, left, 0.0)))
                half = HALF if row >= LOW_TILES else 0
                rows.append(roll_lanes(tile, half + LOW_LANE - LOW_OWN * m))
    return jnp.stack([rows[i] + rows[i + LOW_TILES] for i in range(LOW_TILES)])


class Exchange:
    def __init__(self, depth):
        self.depth = depth
        sizes = [depth] * 2 + [4] * 2 + [2] * 4
        self.at = [sum(sizes[:i]) for i in range(9)]

    def stage(self, edges, block):
        for side in (0, 1):
            for group in range(4):
                edges[side, group] = pack_edges(block, group, side == 1)

    def start(self, block, edges, got, send_sem, got_sem, near):
        n, at = self.depth, self.at
        top, bottom = pl.ds(0, 2), pl.ds(2, 2)
        moves = [
            (block.at[pl.ds(ROWS - n, n)], 0, (1, 0)),
            (block.at[pl.ds(0, n)], 1, (-1, 0)),
            (edges.at[1], 2, (0, 1)),
            (edges.at[0], 3, (0, -1)),
            (edges.at[1, bottom], 4, (1, 1)),
            (edges.at[0, bottom], 5, (1, -1)),
            (edges.at[1, top], 6, (-1, 1)),
            (edges.at[0, top], 7, (-1, -1)),
        ]
        for source, slot, way in moves:
            pltpu.make_async_remote_copy(
                src_ref=source,
                dst_ref=got.at[pl.ds(at[slot], at[slot + 1] - at[slot])],
                send_sem=send_sem,
                recv_sem=got_sem,
                device_id=near(*way),
                device_id_type=MESH,
            ).start()

    def unpack(self, got, put_rows, put_beside):
        n, at = self.depth, self.at
        put_rows(HALO - n, n, got[at[0]:at[0] + n])
        put_rows(HALO + ROWS, n, got[at[1]:at[1] + n])
        for i in range(FINE):
            if i < HALO:
                source = ROWS - HALO + i
                offset = at[4] - 2, at[5] - 2
            elif i < HALO + ROWS:
                source = i - HALO
                offset = at[2], at[3]
            else:
                source = i - HALO - ROWS
                offset = at[6], at[7]
            group, j = divmod(source, 8)
            put_beside(i, unpack_edges(got[offset[0] + group], got[offset[1] + group], j))


AROUND = [(a, b) for a in (-1, 0, 1) for b in (-1, 0, 1) if (a, b) != (0, 0)]
FOR_K, FOR_F, FOR_S = Exchange(HALO), Exchange(HALO - 2), Exchange(HALO - 1)


def kernel(strip_ref, source_ref, coefficient_ref, out_ref,
           k_in, f_in, k_own, f_own, s_own, k_edge, f_edge, s_edge, k_got, f_got, s_got,
           k0, c0, g0, d0, va, vb, k1, c1, i1, g1, d1, ua, ub, k2, c2, i2,
           weight, shifts, pick, l_own, l_send, l_got, one_send, one_got, two_send, two_got,
           picked, sems):
    px, py = lax.axis_index("px"), lax.axis_index("py")
    size_x, size_y = lax.axis_size("px"), lax.axis_size("py")
    strips = strip_ref.shape[0]

    def near(a, b):
        return (lax.rem(px + a + size_x, size_x), lax.rem(py + b + size_y, size_y))

    k_copy = pltpu.make_async_copy(coefficient_ref, k_in, sems.at[0])
    f_copy = pltpu.make_async_copy(source_ref, f_in, sems.at[1])
    k_copy.start()
    f_copy.start()
    peers = [(0, b) for b in range(1, size_y)] + [(a, 0) for a in range(1, size_x)]
    peers += [way for way in AROUND if way[0] and way[1]]
    barrier = pltpu.get_barrier_semaphore()
    for way in peers:
        pl.semaphore_signal(barrier, inc=1, device_id=near(*way), device_id_type=MESH)

    def arrived(buffer, sem):
        pltpu.make_async_copy(buffer, buffer, sem).wait()

    def spread(source, got, sem, ways):
        for slot, way in enumerate(ways):
            pltpu.make_async_remote_copy(
                src_ref=source,
                dst_ref=got.at[slot],
                send_sem=sems.at[sem],
                recv_sem=sems.at[sem + 1],
                device_id=near(*way),
                device_id_type=MESH,
            ).start()

    one = lax.broadcasted_iota(jnp.int32, (LANES, LANES), 0)
    other = lax.broadcasted_iota(jnp.int32, (LANES, LANES), 1)

    def chosen(condition):
        return jnp.where(condition, 1.0, 0.0)

    def beside_pairs(wide, narrow):
        nearby = (wide < EDGE) & (narrow == MID_LANE + MID_OWN + wide // 2)
        return nearby | ((wide >= LANES - EDGE) & (narrow == MID_LANE - LANES // 2 + wide // 2))

    def low_of(mid, half):
        return half + LOW_LANE - MID_LANE // 2 + mid // 2

    mid_halo = 2 * LOW_LANE
    mid_in = (other >= MID_LANE - mid_halo) & (other < MID_LANE + MID_OWN + mid_halo)
    tables = [
        chosen(other == MID_LANE + one // 2), chosen(beside_pairs(one, other)),
        chosen(one == MID_LANE + other // 2), chosen(beside_pairs(other, one)),
        chosen((one >= MID_LANE) & (one < MID_LANE + MID_OWN)
               & (other == (one - MID_LANE) // 2)),
        chosen(mid_in & (one == low_of(other, 0))), chosen(mid_in & (one == low_of(other, HALF))),
        chosen(other == one // 4),
    ]
    for at, table in enumerate(tables):
        picked[at] = table

    ends, total = [], jnp.int32(0)
    for c in range(strips):
        total = total + strip_ref[c]
        ends.append(total)
    sub = lax.broadcasted_iota(jnp.int32, (8, LANES), 0)
    lane = lax.broadcasted_iota(jnp.int32, (8, LANES), 1)

    def strip_of(rows):
        found = jnp.zeros_like(rows)
        for end in ends:
            found = found + jnp.where(rows >= end, 1, 0)
        return found

    lane_strip = strip_of(lane)
    for tile in (0, 1):
        rows = jnp.clip(OWN2 * px - 4 + 8 * tile + sub, 0, OWN2 * size_x - 1)
        pick[tile] = jnp.where(strip_of(rows) == lane_strip, 1.0, 0.0)

    zero = jnp.zeros((NZ, LANES), jnp.float32)
    for ref, end in ((k0, FINE), (va, FINE), (vb, FINE), (k1, MID), (ua, MID), (ub, MID)):
        for t in range(ref.shape[0]):
            ref[t, 0] = zero
            ref[t, end + 1] = zero
    for i in (0, 1, FINE - 2, FINE - 1):
        va[0, 1 + i] = zero

    k_copy.wait()
    for r in range(ROWS):
        k_own[r] = k_in[pl.ds(r, NZ, stride=ROWS), :]
    lows = (1.0 / 16.0) * select_lanes(pair_rows(pair_rows(k_own[...])), picked[7])
    for q in (0, 1):
        l_send[2, q] = pack_low([lows[4 * q + m] for m in range(4)])
    FOR_K.stage(k_edge, k_own)
    f_copy.wait()
    for r in range(ROWS):
        f_own[r] = f_in[pl.ds(r, NZ, stride=ROWS), :]
    FOR_F.stage(f_edge, f_own)
    pl.semaphore_wait(barrier, len(peers))
    outward = [(-a, -b) for a, b in AROUND]
    spread(l_send.at[2], l_got.at[2], 2, outward)
    FOR_K.start(k_own, k_edge, k_got, sems.at[4], sems.at[5], near)
    FOR_F.start(f_own, f_edge, f_got, sems.at[6], sems.at[7], near)

    wide_lane = lax.broadcasted_iota(jnp.int32, (NZ, LANES), 1)
    in_left, in_right = jnp.where(py > 0, 1.0, 0.0), jnp.where(py < size_y - 1, 1.0, 0.0)
    inner_y = jnp.where(wide_lane < LANES // 2, in_right, in_left)
    row_in = [jnp.where(px > 0, 1.0, 0.0), jnp.where(px < size_x - 1, 1.0, 0.0)]

    kept = []
    for tile in range(4):
        rows = OWN2 * px - OWN2 + 8 * tile + sub
        flags = jnp.ones((8, LANES), jnp.float32)
        for end in ends:
            flags = jnp.where(rows == end, 0.0, flags)
        kept += [jnp.broadcast_to(flags[i:i + 1], (NZ, LANES)) for i in range(8)]
    lower_half = wide_lane < HALF
    keep = [
        jnp.stack([jnp.where(lower_half, kept[i + d], kept[i + d + LOW_TILES])
                   for i in range(LOW_TILES)]) for d in (0, 1)]

    def tiles_of(at):
        return lambda a, b, q: (
            l_send[at, q] if (a, b) == (0, 0) else l_got[at, AROUND.index((a, b)), q])

    arrived(l_got.at[2], sems.at[3])
    lows = unpack_low(tiles_of(2), in_left, in_right, row_in)
    k2[...] = lows
    west, east = low_rows_beside(lows)
    faces, inverse, diagonal = scaled_faces(
        lows, west, east, pltpu.roll(lows, 1, 2), pltpu.roll(lows, LANES - 1, 2),
        16.0 * z_coupling, keep)
    for side in range(6):
        c2[side, 0] = faces[side]
    i2[...] = inverse
    ones = jnp.where(lows > 0.0, 1.0, 0.0)
    for turn in range(COARSE_SWEEPS):
        ones = (1.0 - relaxation) * ones + low_sum(ones, c2)

    def own_low(values):
        out = []
        for r in range(OWN2, 2 * OWN2):
            half = HALF if r >= LOW_TILES else 0
            moved = roll_lanes(values[r % LOW_TILES], -half - LOW_LANE)
            out.append(jnp.where(wide_lane < LOW_OWN, moved, 0.0))
        return jnp.stack(out)

    weight[...] = own_low(ones)

    def in_row(values):
        column = jnp.sum(jnp.sum(values, axis=1), axis=1, keepdims=True)
        return jnp.sum(jnp.where(lane == OWN2 * px + sub, column, 0.0), axis=0, keepdims=True)

    one_send[0, 1] = in_row(own_low(diagonal))

    def put_k_rows(first, rows, values):
        k0[0, 1 + first:1 + first + rows] = values * row_in[0 if first < HALO else 1]

    def put_k_beside(i, tile):
        tile = tile * inner_y
        if i < HALO or i >= HALO + ROWS:
            tile = tile * row_in[0 if i < HALO else 1]
        k0[1, 1 + i] = tile

    k0[0, 1 + HALO:1 + HALO + ROWS] = k_own[...]
    arrived(k_got, sems.at[5])
    FOR_K.unpack(k_got, put_k_rows, put_k_beside)

    def restrict(parts):
        total = select_lanes(pair_rows(parts[0]), picked[0])
        return total + select_lanes(pair_rows(parts[1]), picked[1])

    for row in range(0, FINE, 8):
        inverse, diagonal = make_weights(k0, c0, row, 8, z_coupling)
        for t in (0, 1):
            g0[t, row:row + 8] = inverse[t]
            d0[t, row:row + 8] = (1.0 / relaxation) * diagonal[t]
        k1[0, row // 2 + 1:row // 2 + 5] = 0.25 * restrict(
            [k0[t, row + 1:row + 9] for t in (0, 1)])
    for row in range(0, MID, 7):
        inverse, diagonal = make_weights(k1, c1, row, 7, 4.0 * z_coupling)
        i1[0, row:row + 7] = inverse[0]
        d1[0, row:row + 7] = (1.0 / relaxation) * diagonal[0]

    va[0, 1 + HALO:1 + HALO + ROWS] = f_own[...]

    def put_f_rows(first, rows, values):
        va[0, 1 + first:1 + first + rows] = values

    def put_f_beside(i, tile):
        va[1, 1 + i] = tile

    arrived(f_got, sems.at[7])
    FOR_F.unpack(f_got, put_f_rows, put_f_beside)
    for row in range(0, FINE, 8):
        for t in (0, 1):
            start = g0[t, row:row + 8] * va[t, row + 1:row + 9]
            g0[t, row:row + 8] = start
            va[t, row + 1:row + 9] = start

    dens = None
    used = 8
    for cycle in range(CYCLES):
        if cycle > 0:
            sweep(va, vb, c0, g0, 0, FINE // 8, 8)
            sweep(vb, va, c0, g0, 0, FINE // 8, 8)
            fine, spare = va, vb
        else:
            sweep(va, vb, c0, g0, 0, FINE // 8, 8)
            fine, spare = vb, va

        for row in range(0, FINE, 8):
            old, total = weighted(fine, c0, row, 8, (0, 1))
            rest = [
                d0[t, row:row + 8] * (g0[t, row:row + 8] - relaxation * old[t] + total[t])
                for t in (0, 1)]
            half = row // 2
            start = i1[0, half:half + 4] * restrict(rest)
            g1[0, half:half + 4] = start
            ua[0, half + 1:half + 5] = start
        sweep(ua, ub, c1, g1, 0, MID // 7, 7)
        for part in (0, 1):
            row = HALO // 2 + 8 * part
            old, total = weighted(ub, c1, row, 8, (0,))
            rest = d1[0, row:row + 8] * (
                g1[0, row:row + 8] - relaxation * old[0] + total[0])
            l_own[4 * part:4 * part + 4] = select_lanes(pair_rows(rest), picked[4])

        one_send[cycle, 0] = in_row(weight[...] * l_own[...])
        wide = 2 if cycle == 0 else 1
        one_out, one_in = one_send.at[cycle, pl.ds(0, wide)], one_got.at[cycle, :, pl.ds(0, wide)]
        two_out, two_in = two_send.at[cycle, pl.ds(0, wide)], two_got.at[cycle, :, pl.ds(0, wide)]
        spread(one_out, one_in, used, [(0, b) for b in range(1, size_y)])
        for q in (0, 1):
            l_send[cycle, q] = pack_low([l_own[4 * q + m] for m in range(4)])
        spread(l_send.at[cycle], l_got.at[cycle], used + 2, outward)
        arrived(one_in, sems.at[used + 1])
        for part in range(wide):
            two_send[cycle, part] = one_send[cycle, part] + jnp.sum(one_got[cycle, :, part], axis=0)
        spread(two_out, two_in, used + 4, [(a, 0) for a in range(1, size_x)])

        arrived(l_got.at[cycle], sems.at[used + 3])
        right = i2[...] * unpack_low(tiles_of(cycle), None, None, None)
        low = right
        for turn in range(COARSE_SWEEPS - 1):
            low = right + (1.0 - relaxation) * low + low_sum(low, c2)

        arrived(two_in, sems.at[used + 5])
        parts = []
        for part in range(wide):
            both = two_send[cycle, part] + jnp.sum(two_got[cycle, :, part], axis=0)
            row_sums = jnp.broadcast_to(both, (8, LANES))
            parts.append([jnp.sum(pick[tile] * row_sums, axis=1, keepdims=True) for tile in (0, 1)])
        if cycle == 0:
            dens = parts[1]
        for tile in (0, 1):
            shift = jnp.broadcast_to(parts[0][tile] / dens[tile], (8, LANES))
            for i in range(8):
                shifts[8 * tile + i] = jnp.broadcast_to(shift[i:i + 1], (NZ, LANES))

        for part in (0, 1):
            tiles = slice(6, LOW_TILES) if part == 0 else slice(0, 6)
            moved = jnp.where(k2[tiles] > 0.0, shifts[2 + 6 * part:8 + 6 * part], 0.0)
            wave = select_lanes(low[tiles] + moved, picked[5 + part])
            at = 3 + 12 * part
            ua[0, at:at + 12] = ub[0, at:at + 12] + twice_rows(wave)
        sweep(ua, ub, c1, g1, 2, 3, 8)
        sweep(ub, ua, c1, g1, 2, 3, 8)

        for row in range(8, 48, 8):
            wave = ua[0, row // 2 + 1:row // 2 + 5]
            for t in (0, 1):
                spare[t, row + 1:row + 9] = fine[t, row + 1:row + 9] + twice_rows(
                    select_lanes(wave, picked[2 + t]))
        sweep(spare, fine, c0, g0, 8, 5, 8)
        for part in range(ROWS // 8):
            row = HALO + 8 * part
            old, total = weighted(fine, c0, row, 8, (0,))
            s_own[8 * part:8 * part + 8] = (
                g0[0, row:row + 8] + (1.0 - relaxation) * old[0] + total[0])
        used += 6

        if cycle < CYCLES - 1:
            FOR_S.stage(s_edge, s_own)
            FOR_S.start(s_own, s_edge, s_got, sems.at[used], sems.at[used + 1], near)
            va[0, 1 + HALO:1 + HALO + ROWS] = s_own[...]
            va[0, 1] = zero
            va[0, FINE] = zero

            def put_s_rows(first, rows, values):
                inside = k0[0, 1 + first:1 + first + rows] > 0.0
                va[0, 1 + first:1 + first + rows] = jnp.where(inside, values, 0.0)

            def put_s_beside(i, tile):
                va[1, 1 + i] = jnp.where(k0[1, 1 + i] > 0.0, tile, 0.0)

            arrived(s_got, sems.at[used + 1])
            FOR_S.unpack(s_got, put_s_rows, put_s_beside)
            arrived(s_got, sems.at[used])
            used += 2

    for r in range(ROWS):
        out_ref[pl.ds(r, NZ, stride=ROWS), :] = s_own[r]

    arrived(l_got.at[2], sems.at[2])
    arrived(k_got, sems.at[4])
    arrived(f_got, sems.at[6])
    for cycle, at in ((0, 8), (1, 16)):
        wide = pl.ds(0, 2 - cycle)
        arrived(one_got.at[cycle, :, wide], sems.at[at])
        arrived(l_got.at[cycle], sems.at[at + 2])
        arrived(two_got.at[cycle, :, wide], sems.at[at + 4])


def vmem(*shape):
    return pltpu.VMEM(shape + (NZ, LANES), jnp.float32)


def shards(source, coefficient, strip_rows):
    size_x, size_y = lax.axis_size("px"), lax.axis_size("py")
    flat = (NZ * ROWS, LANES)
    scratch = [pltpu.VMEM(flat, jnp.float32)] * 2
    scratch += [vmem(ROWS), vmem(ROWS), vmem(ROWS), vmem(2, 4), vmem(2, 4), vmem(2, 4)]
    scratch += [vmem(e.at[8]) for e in (FOR_K, FOR_F, FOR_S)]
    scratch += [vmem(2, FINE + 2), vmem(6, 2, FINE), vmem(2, FINE), vmem(2, FINE)]
    scratch += [vmem(2, FINE + 2), vmem(2, FINE + 2)]
    scratch += [vmem(1, MID + 2), vmem(6, 1, MID), vmem(1, MID), vmem(1, MID), vmem(1, MID)]
    scratch += [vmem(1, MID + 2), vmem(1, MID + 2)]
    scratch += [vmem(LOW_TILES), vmem(6, 1, LOW_TILES), vmem(LOW_TILES)]
    scratch += [vmem(OWN2), vmem(16), vmem(2), vmem(OWN2), vmem(3, 2), vmem(3, 8, 2)]
    row = lambda *shape: pltpu.VMEM(shape + (1, LANES), jnp.float32)
    scratch += [row(2, 2), row(2, size_y - 1, 2), row(2, 2), row(2, size_x - 1, 2)]
    scratch += [pltpu.VMEM((8, LANES, LANES), jnp.float32), pltpu.SemaphoreType.DMA((22,))]
    hbm = pl.BlockSpec(memory_space=pltpu.HBM)
    done = pl.pallas_call(
        kernel,
        out_shape=jax.ShapeDtypeStruct(flat, jnp.float32),
        in_specs=[pl.BlockSpec(memory_space=pltpu.SMEM), hbm, hbm],
        out_specs=pl.BlockSpec(memory_space=pltpu.VMEM),
        scratch_shapes=scratch,
        compiler_params=pltpu.CompilerParams(
            collective_id=0, has_side_effects=True, vmem_limit_bytes=32 << 20
        ),
        name="cycles",
    )(strip_rows, source.reshape(flat), coefficient.reshape(flat))
    return done.reshape(source.shape)


def solution(mesh):
    placed = (P(None, "px", "py"), P(None, "px", "py"), P())
    return jax.shard_map(
        shards, mesh=mesh, in_specs=placed, out_specs=P(None, "px", "py"), check_vma=False
    )
```

```python
import jax
import jax.numpy as jnp
from jax import lax
from jax.experimental import pallas as pl
from jax.experimental.pallas import tpu as pltpu
from jax.sharding import PartitionSpec as P

CYCLES = 2
COARSE_SWEEPS = 6
relaxation = 0.8
z_coupling = 0.25

MESH = pl.DeviceIdType.MESH

NZ = 8
ROWS = 32
LANES = 128
EDGE = 16
HALO = 14
FINE = ROWS + 2 * HALO
MID = FINE // 2
OWN2 = ROWS // 4
LOW_TILES = 3 * OWN2 // 2
MID_LANE, MID_OWN = 32, 64
LOW_LANE, LOW_OWN, HALF = 8, 32, 64
MID_HALO, MID_ROWS = HALO // 2, ROWS // 2


def lanes_of(rows):
    return lax.broadcasted_iota(jnp.int32, (rows, NZ, LANES), 2)


def layers_of(rows):
    return lax.broadcasted_iota(jnp.int32, (rows, NZ, LANES), 1)


def beside_lanes(parts, tiles):
    back = [pltpu.roll(part, 1, 2) for part in parts]
    ahead = [pltpu.roll(part, LANES - 1, 2) for part in parts]
    if len(parts) == 1:
        return back, ahead
    lane = lanes_of(parts[0].shape[0])
    before, after = lane < 1, lane >= LANES - 1
    south = [jnp.where(before, back[1 - t], back[t]) for t in tiles]
    north = [jnp.where(after, ahead[1 - t], ahead[t]) for t in tiles]
    return south, north


def six_sum(weights, t, here, west, own, east, south, north):
    total = weights[0, t, here] * west + weights[1, t, here] * east
    total += weights[4, t, here] * pltpu.roll(own, 1, 1)
    total += weights[5, t, here] * pltpu.roll(own, NZ - 1, 1)
    total += weights[2, t, here] * south
    total += weights[3, t, here] * north
    return total


def weighted(values, weights, row, rows, tiles):
    parts = [values[t, row + 1:row + 1 + rows] for t in range(values.shape[0])]
    south, north = beside_lanes(parts, tiles)
    totals = []
    for at, t in enumerate(tiles):
        west, east = values[t, row:row + rows], values[t, row + 2:row + 2 + rows]
        totals.append(six_sum(weights, t, slice(row, row + rows), west, parts[t], east,
                              south[at], north[at]))
    return [parts[t] for t in tiles], totals


def groups(first, end, rows=8):
    return [(row, min(rows, end - row)) for row in range(first, end, rows)]


def sweep(values, new, weights, right, first, end):
    tiles = range(values.shape[0])
    for row, rows in groups(first, end):
        old, total = weighted(values, weights, row, rows, tiles)
        for t in tiles:
            new[t, row + 1:row + 1 + rows] = (
                right[t, row:row + rows] + (1.0 - relaxation) * old[t] + total[t])


def scaled_faces(own, west, east, south, north, z_factor, keep=None):
    layer = layers_of(own.shape[0])
    half_z = 0.5 * z_factor
    faces = [
        0.5 * (own + west), 0.5 * (own + east), 0.5 * (own + south), 0.5 * (own + north),
        jnp.where(layer > 0, half_z * (own + pltpu.roll(own, 1, 1)), 0.0),
        jnp.where(layer < NZ - 1, half_z * (own + pltpu.roll(own, NZ - 1, 1)), 0.0),
    ]
    diagonal = faces[0] + faces[1] + faces[2] + faces[3] + faces[4] + faces[5]
    inside = own > 0.0
    inverse = jnp.where(inside, relaxation / jnp.where(inside, diagonal, 1.0), 0.0)
    if keep is not None:
        faces[0], faces[1] = faces[0] * keep[0], faces[1] * keep[1]
    return [inverse * face for face in faces], inverse, diagonal


def make_weights(conduct, weights, row, rows, z_factor):
    tiles = range(conduct.shape[0])
    parts = [conduct[t, row + 1:row + 1 + rows] for t in tiles]
    south, north = beside_lanes(parts, tiles)
    inverses, diagonals = [], []
    for t in tiles:
        west, east = conduct[t, row:row + rows], conduct[t, row + 2:row + 2 + rows]
        faces, inverse, diagonal = scaled_faces(
            parts[t], west, east, south[t], north[t], z_factor)
        for side in range(6):
            weights[side, t, row:row + rows] = faces[side]
        inverses.append(inverse)
        diagonals.append(diagonal)
    return inverses, diagonals


def low_rows_beside(values):
    first = pltpu.roll(values[LOW_TILES - 1:], HALF, 2)
    last = pltpu.roll(values[:1], HALF, 2)
    west = jnp.concatenate([first, values[:-1]], axis=0)
    east = jnp.concatenate([values[1:], last], axis=0)
    return west, east


def low_sum(values, weights):
    west, east = low_rows_beside(values)
    back, ahead = pltpu.roll(values, 1, 2), pltpu.roll(values, LANES - 1, 2)
    return six_sum(weights, 0, slice(0, LOW_TILES), west, values, east, back, ahead)


def pair_rows(values):
    rows = values.shape[0]
    return jnp.sum(values.reshape(rows // 2, 2, NZ, LANES), axis=1)


def twice_rows(values):
    rows = values.shape[0]
    wide = jnp.broadcast_to(values[:, None], (rows, 2, NZ, LANES))
    return wide.reshape(2 * rows, NZ, LANES)


def select_lanes(values, chosen):
    rows = values.shape[0]
    flat = jnp.dot(
        values.reshape(rows * NZ, LANES), chosen, precision=lax.Precision.HIGHEST,
        preferred_element_type=jnp.float32)
    return flat.reshape(rows, NZ, LANES)


def roll_lanes(tile, amount):
    amount = amount % LANES
    return tile if amount == 0 else pltpu.roll(tile, amount, 1)


def pack_edges(block, group, right_side):
    lane = lax.broadcasted_iota(jnp.int32, (NZ, LANES), 1)
    packed = None
    for j in range(8):
        moved = roll_lanes(block[8 * group + j], EDGE * j + (EDGE if right_side else 0))
        packed = moved if packed is None else jnp.where(lane // EDGE == j, moved, packed)
    return packed


def unpack_edges(left, right, j):
    lane = lax.broadcasted_iota(jnp.int32, (NZ, LANES), 1)
    from_right = roll_lanes(right, -EDGE * j)
    from_left = roll_lanes(left, -EDGE * (j + 1))
    return jnp.where(lane < EDGE, from_right, jnp.where(lane >= LANES - EDGE, from_left, 0.0))


def pack_low(rows):
    out = rows[0]
    for m in range(1, 4):
        out = out + roll_lanes(rows[m], LOW_OWN * m)
    return out


def unpack_low(get, scale_left, scale_right, scale_rows):
    lane = lax.broadcasted_iota(jnp.int32, (NZ, LANES), 1)
    rows = []
    for a in (-1, 0, 1):
        for q in (0, 1):
            own = get(a, 0, q)
            left, right = roll_lanes(get(a, -1, q), -LOW_OWN), roll_lanes(get(a, 1, q), LOW_OWN)
            if scale_left is not None:
                left, right = left * scale_left, right * scale_right
            if scale_rows is not None and a != 0:
                scale = scale_rows[0 if a < 0 else 1]
                own, left, right = own * scale, left * scale, right * scale
            for m in range(4):
                row = len(rows)
                away = (lane - LOW_OWN * m) % LANES
                tile = jnp.where(
                    away < LOW_OWN, own,
                    jnp.where(away < LOW_OWN + LOW_LANE, right,
                              jnp.where(away >= LANES - LOW_LANE, left, 0.0)))
                half = HALF if row >= LOW_TILES else 0
                rows.append(roll_lanes(tile, half + LOW_LANE - LOW_OWN * m))
    return jnp.stack([rows[i] + rows[i + LOW_TILES] for i in range(LOW_TILES)])


def pack_mid(rows):
    lane = lax.broadcasted_iota(jnp.int32, (NZ, LANES), 1)
    return [
        jnp.where(lane < HALF, roll_lanes(rows[2 * j], -MID_LANE),
                  roll_lanes(rows[2 * j + 1], MID_LANE)) for j in range(MID_ROWS // 2)]


MID_AT, MID_TILES = {}, 0
for side in [(a, b) for a in (-1, 0, 1) for b in (-1, 0, 1) if (a, b) != (0, 0)]:
    MID_AT[side] = MID_TILES
    MID_TILES += MID_ROWS // 2 if side[0] == 0 else MID_ROWS // 4


def start_mid(send, got, send_sem, got_sem, near):
    for a, b in AROUND:
        count = MID_ROWS // 2 if a == 0 else MID_ROWS // 4
        pltpu.make_async_remote_copy(
            src_ref=send.at[pl.ds(MID_ROWS // 4 if a < 0 else 0, count)],
            dst_ref=got.at[pl.ds(MID_AT[a, b], count)],
            send_sem=send_sem,
            recv_sem=got_sem,
            device_id=near(-a, -b),
            device_id_type=MESH,
        ).start()


def unpack_mid(got, which, put):
    lane = lax.broadcasted_iota(jnp.int32, (NZ, LANES), 1)
    own = (lane >= MID_LANE) & (lane < MID_LANE + MID_OWN)
    for row in range(MID):
        a = -1 if row < MID_HALO else 0 if row < MID_HALO + MID_ROWS else 1
        source = row - MID_HALO - MID_ROWS * a
        tile, half = divmod(source - (MID_ROWS // 2 if a < 0 else 0), 2)
        turn = MID_LANE if half == 0 else -MID_LANE
        left, right = got[MID_AT[a, -1] + tile, which], got[MID_AT[a, 1] + tile, which]
        beside = roll_lanes(jnp.where(lane % HALF < MID_LANE, right, left), -turn)
        if a != 0:
            beside = jnp.where(own, roll_lanes(got[MID_AT[a, 0] + tile, which], turn), beside)
        put(row, a, own, beside)


class Exchange:
    def __init__(self, depth):
        self.depth = depth
        sizes = [depth] * 2 + [4] * 2 + [2] * 4
        self.at = [sum(sizes[:i]) for i in range(9)]

    def stage(self, edges, block):
        for side in (0, 1):
            for group in range(4):
                edges[side, group] = pack_edges(block, group, side == 1)

    def start(self, block, edges, got, send_sem, got_sem, near):
        n, at = self.depth, self.at
        top, bottom = pl.ds(0, 2), pl.ds(2, 2)
        moves = [
            (block.at[pl.ds(ROWS - n, n)], 0, (1, 0)),
            (block.at[pl.ds(0, n)], 1, (-1, 0)),
            (edges.at[1], 2, (0, 1)),
            (edges.at[0], 3, (0, -1)),
            (edges.at[1, bottom], 4, (1, 1)),
            (edges.at[0, bottom], 5, (1, -1)),
            (edges.at[1, top], 6, (-1, 1)),
            (edges.at[0, top], 7, (-1, -1)),
        ]
        for source, slot, way in moves:
            pltpu.make_async_remote_copy(
                src_ref=source,
                dst_ref=got.at[pl.ds(at[slot], at[slot + 1] - at[slot])],
                send_sem=send_sem,
                recv_sem=got_sem,
                device_id=near(*way),
                device_id_type=MESH,
            ).start()

    def unpack(self, got, put_rows, put_beside):
        n, at = self.depth, self.at
        put_rows(HALO - n, n, got[at[0]:at[0] + n])
        put_rows(HALO + ROWS, n, got[at[1]:at[1] + n])
        for i in range(FINE):
            if i < HALO:
                source = ROWS - HALO + i
                offset = at[4] - 2, at[5] - 2
            elif i < HALO + ROWS:
                source = i - HALO
                offset = at[2], at[3]
            else:
                source = i - HALO - ROWS
                offset = at[6], at[7]
            group, j = divmod(source, 8)
            put_beside(i, unpack_edges(got[offset[0] + group], got[offset[1] + group], j))


AROUND = [(a, b) for a in (-1, 1) for b in (-1, 1)] + [(-1, 0), (1, 0), (0, -1), (0, 1)]
FOR_K, FOR_F = Exchange(HALO), Exchange(HALO - 4)
THIN = HALO - FOR_F.depth


def kernel(strip_hbm, source_ref, coefficient_ref, out_ref,
           strip_ref, k_in, f_in, k_own, f_own, s_own, k_edge, f_edge, k_got, f_got,
           k0, c0, g0, d0, va, vb, k1, c1, i1, g1, d1, ua, ub, k2, c2, i2,
           weight, shifts, pick, l_own, l_send, l_got, m_send, m_got, n_send, n_got, one_send, one_got, two_send, two_got,
           picked, sems):
    px, py = lax.axis_index("px"), lax.axis_index("py")
    size_x, size_y = lax.axis_size("px"), lax.axis_size("py")
    strips = strip_ref.shape[0]

    def near(a, b):
        return (lax.rem(px + a + size_x, size_x), lax.rem(py + b + size_y, size_y))

    k_copy = pltpu.make_async_copy(coefficient_ref, k_in, sems.at[0])
    f_copy = pltpu.make_async_copy(source_ref, f_in, sems.at[1])
    strip_copy = pltpu.make_async_copy(strip_hbm, strip_ref, sems.at[26])
    k_copy.start()
    strip_copy.start()
    f_copy.start()
    def around_ring(offset, size):
        return min(offset % size, -offset % size)

    along_y = sorted(range(1, size_y), key=lambda b: -around_ring(b, size_y))
    along_x = sorted(
        range(1, size_x),
        key=lambda a: -around_ring(a % 4, 4) - around_ring((a + 1) // 4, size_x // 4))
    to_y, to_x = [(0, b) for b in along_y], [(a, 0) for a in along_x]
    peers = to_y + to_x + [way for way in AROUND if way[0] and way[1]]
    barrier = pltpu.get_barrier_semaphore()
    for way in peers:
        pl.semaphore_signal(barrier, inc=1, device_id=near(*way), device_id_type=MESH)

    def arrived(buffer, sem):
        pltpu.make_async_copy(buffer, buffer, sem).wait()

    def spread(source, got, sem, ways):
        for slot, way in enumerate(ways):
            pltpu.make_async_remote_copy(
                src_ref=source,
                dst_ref=got.at[slot],
                send_sem=sems.at[sem],
                recv_sem=sems.at[sem + 1],
                device_id=near(*way),
                device_id_type=MESH,
            ).start()

    one = lax.broadcasted_iota(jnp.int32, (LANES, LANES), 0)
    other = lax.broadcasted_iota(jnp.int32, (LANES, LANES), 1)

    def chosen(condition):
        return jnp.where(condition, 1.0, 0.0)

    def beside_pairs(wide, narrow):
        nearby = (wide < EDGE) & (narrow == MID_LANE + MID_OWN + wide // 2)
        return nearby | ((wide >= LANES - EDGE) & (narrow == MID_LANE - LANES // 2 + wide // 2))

    def low_of(mid, half):
        return half + LOW_LANE - MID_LANE // 2 + mid // 2

    mid_halo = 2 * LOW_LANE
    mid_in = (other >= MID_LANE - mid_halo) & (other < MID_LANE + MID_OWN + mid_halo)
    tables = [
        chosen(other == MID_LANE + one // 2), chosen(beside_pairs(one, other)),
        chosen(one == MID_LANE + other // 2), chosen(beside_pairs(other, one)),
        chosen((one >= MID_LANE) & (one < MID_LANE + MID_OWN)
               & (other == (one - MID_LANE) // 2)),
        chosen(mid_in & (one == low_of(other, 0))), chosen(mid_in & (one == low_of(other, HALF))),
        chosen(other == one // 4),
    ]
    for at, table in enumerate(tables):
        picked[at] = table

    strip_copy.wait()
    ends, total = [], jnp.int32(0)
    for c in range(strips):
        total = total + strip_ref[c]
        ends.append(total)
    sub = lax.broadcasted_iota(jnp.int32, (8, LANES), 0)
    lane = lax.broadcasted_iota(jnp.int32, (8, LANES), 1)

    def strip_of(rows):
        found = jnp.zeros_like(rows)
        for end in ends:
            found = found + jnp.where(rows >= end, 1, 0)
        return found

    lane_strip = strip_of(lane)
    for tile in (0, 1):
        rows = jnp.clip(OWN2 * px - 4 + 8 * tile + sub, 0, OWN2 * size_x - 1)
        pick[tile] = jnp.where(strip_of(rows) == lane_strip, 1.0, 0.0)

    zero = jnp.zeros((NZ, LANES), jnp.float32)
    for ref, end in ((k0, FINE), (va, FINE), (vb, FINE), (k1, MID), (ua, MID), (ub, MID)):
        for t in range(ref.shape[0]):
            ref[t, 0] = zero
            ref[t, end + 1] = zero
    for i in range(THIN):
        va[0, 1 + i] = zero
        va[0, FINE - i] = zero
    for i in range(MID):
        ua[0, 1 + i] = zero

    k_copy.wait()
    for r in range(ROWS):
        k_own[r] = k_in[pl.ds(r, NZ, stride=ROWS), :]
    lows = (1.0 / 16.0) * select_lanes(pair_rows(pair_rows(k_own[...])), picked[7])
    for q in (0, 1):
        l_send[2, q] = pack_low([lows[4 * q + m] for m in range(4)])
    FOR_K.stage(k_edge, k_own)
    f_copy.wait()
    for r in range(ROWS):
        f_own[r] = f_in[pl.ds(r, NZ, stride=ROWS), :]
    FOR_F.stage(f_edge, f_own)
    pl.semaphore_wait(barrier, len(peers))
    outward = [(-a, -b) for a, b in AROUND]
    spread(l_send.at[2], l_got.at[2], 2, outward)
    FOR_K.start(k_own, k_edge, k_got, sems.at[4], sems.at[5], near)
    FOR_F.start(f_own, f_edge, f_got, sems.at[6], sems.at[7], near)

    wide_lane = lax.broadcasted_iota(jnp.int32, (NZ, LANES), 1)
    in_left, in_right = jnp.where(py > 0, 1.0, 0.0), jnp.where(py < size_y - 1, 1.0, 0.0)
    inner_y = jnp.where(wide_lane < LANES // 2, in_right, in_left)
    row_in = [jnp.where(px > 0, 1.0, 0.0), jnp.where(px < size_x - 1, 1.0, 0.0)]

    kept = []
    for tile in range(4):
        rows = OWN2 * px - OWN2 + 8 * tile + sub
        flags = jnp.ones((8, LANES), jnp.float32)
        for end in ends:
            flags = jnp.where(rows == end, 0.0, flags)
        kept += [jnp.broadcast_to(flags[i:i + 1], (NZ, LANES)) for i in range(8)]
    lower_half = wide_lane < HALF
    keep = [
        jnp.stack([jnp.where(lower_half, kept[i + d], kept[i + d + LOW_TILES])
                   for i in range(LOW_TILES)]) for d in (0, 1)]

    def tiles_of(at):
        return lambda a, b, q: (
            l_send[at, q] if (a, b) == (0, 0) else l_got[at, AROUND.index((a, b)), q])

    arrived(l_got.at[2], sems.at[3])
    lows = unpack_low(tiles_of(2), in_left, in_right, row_in)
    k2[...] = lows
    west, east = low_rows_beside(lows)
    faces, inverse, diagonal = scaled_faces(
        lows, west, east, pltpu.roll(lows, 1, 2), pltpu.roll(lows, LANES - 1, 2),
        16.0 * z_coupling, keep)
    for side in range(6):
        c2[side, 0] = faces[side]
    i2[...] = inverse
    ones = jnp.where(lows > 0.0, 1.0, 0.0)
    for turn in range(COARSE_SWEEPS):
        ones = (1.0 - relaxation) * ones + low_sum(ones, c2)

    def own_low(values):
        out = []
        for r in range(OWN2, 2 * OWN2):
            half = HALF if r >= LOW_TILES else 0
            moved = roll_lanes(values[r % LOW_TILES], -half - LOW_LANE)
            out.append(jnp.where(wide_lane < LOW_OWN, moved, 0.0))
        return jnp.stack(out)

    weight[...] = own_low(ones)

    def in_row(values):
        column = jnp.sum(jnp.sum(values, axis=1), axis=1, keepdims=True)
        return jnp.sum(jnp.where(lane == OWN2 * px + sub, column, 0.0), axis=0, keepdims=True)

    one_send[0, 1] = in_row(own_low(diagonal))

    def put_k_rows(first, rows, values):
        k0[0, 1 + first:1 + first + rows] = values * row_in[0 if first < HALO else 1]

    def put_k_beside(i, tile):
        tile = tile * inner_y
        if i < HALO or i >= HALO + ROWS:
            tile = tile * row_in[0 if i < HALO else 1]
        k0[1, 1 + i] = tile

    k0[0, 1 + HALO:1 + HALO + ROWS] = k_own[...]
    arrived(k_got, sems.at[5])
    FOR_K.unpack(k_got, put_k_rows, put_k_beside)

    def restrict(parts):
        total = select_lanes(pair_rows(parts[0]), picked[0])
        return total + select_lanes(pair_rows(parts[1]), picked[1])

    for row, rows in groups(0, FINE, 10):
        k1[0, row // 2 + 1:(row + rows) // 2 + 1] = 0.25 * restrict(
            [k0[t, row + 1:row + rows + 1] for t in (0, 1)])
    for row, rows in groups(THIN, FINE - THIN):
        inverse, diagonal = make_weights(k0, c0, row, rows, z_coupling)
        for t in (0, 1):
            g0[t, row:row + rows] = inverse[t]
            d0[t, row:row + rows] = (1.0 / relaxation) * diagonal[t]
    for row, rows in groups(0, MID, 10):
        inverse, diagonal = make_weights(k1, c1, row, rows, 4.0 * z_coupling)
        i1[0, row:row + rows] = inverse[0]
        d1[0, row:row + rows] = (1.0 / relaxation) * diagonal[0]

    va[0, 1 + HALO:1 + HALO + ROWS] = f_own[...]

    def put_f_rows(first, rows, values):
        va[0, 1 + first:1 + first + rows] = values

    def put_f_beside(i, tile):
        va[1, 1 + i] = tile

    arrived(f_got, sems.at[7])
    FOR_F.unpack(f_got, put_f_rows, put_f_beside)
    for row, rows in groups(THIN, FINE - THIN):
        for t in (0, 1):
            start = g0[t, row:row + rows] * va[t, row + 1:row + rows + 1]
            g0[t, row:row + rows] = start
            va[t, row + 1:row + rows + 1] = start

    def rows_0(halo):
        return HALO - halo, HALO + ROWS + halo

    def rows_1(halo):
        return MID_HALO - halo, MID_HALO + MID_ROWS + halo

    dens = None
    used = 8
    for cycle in range(CYCLES):
        if cycle > 0:
            sweep(va, vb, c0, g0, *rows_0(6))
            sweep(vb, va, c0, g0, *rows_0(6))
            fine, spare = va, vb
        else:
            sweep(va, vb, c0, g0, *rows_0(10))
            fine, spare = vb, va

        for row, rows in groups(*rows_0(4)):
            old, total = weighted(fine, c0, row, rows, (0, 1))
            here = slice(row, row + rows)
            rest = [
                d0[t, here] * (g0[t, here] - relaxation * old[t] + total[t]) for t in (0, 1)]
            half, count = row // 2, rows // 2
            start = i1[0, half:half + count] * restrict(rest)
            g1[0, half:half + count] = start
            ua[0, half + 1:half + count + 1] = start
        sweep(ua, ub, c1, g1, *rows_1(2))
        for part in (0, 1):
            row = MID_HALO + 8 * part
            old, total = weighted(ub, c1, row, 8, (0,))
            rest = d1[0, row:row + 8] * (
                g1[0, row:row + 8] - relaxation * old[0] + total[0])
            l_own[4 * part:4 * part + 4] = select_lanes(pair_rows(rest), picked[4])

        one_send[cycle, 0] = in_row(weight[...] * l_own[...])
        wide = 2 if cycle == 0 else 1
        one_out, one_in = one_send.at[cycle, pl.ds(0, wide)], one_got.at[cycle, :, pl.ds(0, wide)]
        two_out, two_in = two_send.at[cycle, pl.ds(0, wide)], two_got.at[cycle, :, pl.ds(0, wide)]
        spread(one_out, one_in, used, to_y)
        for q in (0, 1):
            l_send[cycle, q] = pack_low([l_own[4 * q + m] for m in range(4)])
        spread(l_send.at[cycle], l_got.at[cycle], used + 2, outward)
        mids_out, mids_in = (m_send, m_got) if cycle == 0 else (n_send, n_got)
        for j, tile in enumerate(pack_mid(ub[0, 1 + MID_HALO:1 + MID_HALO + MID_ROWS])):
            mids_out[j, 0] = tile
        if cycle == 0:
            for j, tile in enumerate(pack_mid(g1[0, MID_HALO:MID_HALO + MID_ROWS])):
                mids_out[j, 1] = tile
        start_mid(mids_out, mids_in, sems.at[used + 6], sems.at[used + 7], near)
        def pass_on():
            arrived(one_in, sems.at[used + 1])
            for part in range(wide):
                two_send[cycle, part] = one_send[cycle, part] + jnp.sum(one_got[cycle, :, part], axis=0)
            spread(two_out, two_in, used + 4, to_x)

        if cycle > 0:
            pass_on()

        arrived(l_got.at[cycle], sems.at[used + 3])
        right = i2[...] * unpack_low(tiles_of(cycle), None, None, None)
        low = right
        for turn in range(COARSE_SWEEPS - 1):
            low = right + (1.0 - relaxation) * low + low_sum(low, c2)
        if cycle == 0:
            mine = own_low(low)
            for q in (0, 1):
                l_send[3, q] = pack_low([mine[4 * q + m] for m in range(4)])
            spread(l_send.at[3], l_got.at[3], 24, outward)
            pass_on()

        def put_u(row, a, own, tile):
            tile = jnp.where(own, ub[0, 1 + row], tile) if a == 0 else tile
            ub[0, 1 + row] = jnp.where(k1[0, 1 + row] > 0.0, tile, 0.0)

        def put_g(row, a, own, tile):
            tile = jnp.where(own, g1[0, row], tile) if a == 0 else tile
            g1[0, row] = jnp.where(k1[0, 1 + row] > 0.0, tile, 0.0)

        arrived(mids_in, sems.at[used + 7])
        unpack_mid(mids_in, 0, put_u)
        if cycle == 0:
            unpack_mid(mids_in, 1, put_g)
            arrived(l_got.at[3], sems.at[25])
            low = jnp.where(k2[...] > 0.0, unpack_low(tiles_of(3), None, None, None), 0.0)

        arrived(two_in, sems.at[used + 5])
        parts = []
        for part in range(wide):
            both = two_send[cycle, part] + jnp.sum(two_got[cycle, :, part], axis=0)
            row_sums = jnp.broadcast_to(both, (8, LANES))
            parts.append([jnp.sum(pick[tile] * row_sums, axis=1, keepdims=True) for tile in (0, 1)])
        if cycle == 0:
            dens = parts[1]
        for tile in (0, 1):
            shift = jnp.broadcast_to(parts[0][tile] / dens[tile], (8, LANES))
            for i in range(8):
                shifts[8 * tile + i] = jnp.broadcast_to(shift[i:i + 1], (NZ, LANES))

        for part in (0, 1):
            tiles = slice(4, LOW_TILES) if part == 0 else slice(0, 8)
            moved = jnp.where(k2[tiles] > 0.0, shifts[8 * part:8 * part + 8], 0.0)
            wave = twice_rows(select_lanes(low[tiles] + moved, picked[5 + part]))
            at, count = (1, MID // 2) if part == 0 else (1 + MID // 2, MID // 2)
            ua[0, at:at + count] = ub[0, at:at + count] + (wave[1:] if part == 0 else wave[:-1])
        around = rows_1(6 if cycle == 0 else 2)
        sweep(ua, ub, c1, g1, *around)
        sweep(ub, ua, c1, g1, *around)

        for row, rows in groups(*rows_0(10 if cycle == 0 else 2)):
            wave = ua[0, row // 2 + 1:(row + rows) // 2 + 1]
            here = slice(row + 1, row + rows + 1)
            for t in (0, 1):
                spare[t, here] = fine[t, here] + twice_rows(select_lanes(wave, picked[2 + t]))
        if cycle < CYCLES - 1:
            sweep(spare, fine, c0, g0, *rows_0(8))
            sweep(fine, spare, c0, g0, *rows_0(8))
        else:
            sweep(spare, fine, c0, g0, *rows_0(1))
            for row, rows in groups(*rows_0(0)):
                old, total = weighted(fine, c0, row, rows, (0,))
                s_own[row - HALO:row - HALO + rows] = (
                    g0[0, row:row + rows] + (1.0 - relaxation) * old[0] + total[0])
        used += 8

    for r in range(ROWS):
        out_ref[pl.ds(r, NZ, stride=ROWS), :] = s_own[r]

    arrived(l_got.at[2], sems.at[2])
    arrived(k_got, sems.at[4])
    arrived(f_got, sems.at[6])
    arrived(l_got.at[3], sems.at[24])
    arrived(m_got, sems.at[14])
    arrived(n_got, sems.at[22])
    for cycle, at in ((0, 8), (1, 16)):
        wide = pl.ds(0, 2 - cycle)
        arrived(one_got.at[cycle, :, wide], sems.at[at])
        arrived(l_got.at[cycle], sems.at[at + 2])
        arrived(two_got.at[cycle, :, wide], sems.at[at + 4])


def vmem(*shape):
    return pltpu.VMEM(shape + (NZ, LANES), jnp.float32)


def shards(source, coefficient, strip_rows):
    size_x, size_y = lax.axis_size("px"), lax.axis_size("py")
    flat = (NZ * ROWS, LANES)
    scratch = [pltpu.SMEM(strip_rows.shape, jnp.int32)] + [pltpu.VMEM(flat, jnp.float32)] * 2
    scratch += [vmem(ROWS), vmem(ROWS), vmem(ROWS), vmem(2, 4), vmem(2, 4)]
    scratch += [vmem(e.at[8]) for e in (FOR_K, FOR_F)]
    scratch += [vmem(2, FINE + 2), vmem(6, 2, FINE), vmem(2, FINE), vmem(2, FINE)]
    scratch += [vmem(2, FINE + 2), vmem(2, FINE + 2)]
    scratch += [vmem(1, MID + 2), vmem(6, 1, MID), vmem(1, MID), vmem(1, MID), vmem(1, MID)]
    scratch += [vmem(1, MID + 2), vmem(1, MID + 2)]
    scratch += [vmem(LOW_TILES), vmem(6, 1, LOW_TILES), vmem(LOW_TILES)]
    scratch += [vmem(OWN2), vmem(16), vmem(2), vmem(OWN2), vmem(4, 2), vmem(4, 8, 2)]
    scratch += [vmem(MID_ROWS // 2, 2), vmem(MID_TILES, 2), vmem(MID_ROWS // 2, 1), vmem(MID_TILES, 1)]
    row = lambda *shape: pltpu.VMEM(shape + (1, LANES), jnp.float32)
    scratch += [row(2, 2), row(2, size_y - 1, 2), row(2, 2), row(2, size_x - 1, 2)]
    scratch += [pltpu.VMEM((8, LANES, LANES), jnp.float32), pltpu.SemaphoreType.DMA((27,))]
    hbm = pl.BlockSpec(memory_space=pltpu.HBM)
    done = pl.pallas_call(
        kernel,
        out_shape=jax.ShapeDtypeStruct(flat, jnp.float32),
        in_specs=[hbm, hbm, hbm],
        out_specs=pl.BlockSpec(memory_space=pltpu.VMEM),
        scratch_shapes=scratch,
        compiler_params=pltpu.CompilerParams(
            collective_id=0, has_side_effects=True, vmem_limit_bytes=32 << 20
        ),
        name="cycles",
    )(strip_rows, source.reshape(flat), coefficient.reshape(flat))
    return done.reshape(source.shape)


def solution(mesh):
    placed = (P(None, "px", "py"), P(None, "px", "py"), P())
    return jax.shard_map(
        shards, mesh=mesh, in_specs=placed, out_specs=P(None, "px", "py"), check_vma=False
    )
```

```python
import jax
import jax.numpy as jnp
from jax import lax
from jax.experimental import pallas as pl
from jax.experimental.pallas import tpu as pltpu
from jax.sharding import PartitionSpec as P

CYCLES = 2
COARSE_SWEEPS = 6
relaxation = 0.8
z_coupling = 0.25

MESH = pl.DeviceIdType.MESH

NZ = 8
ROWS = 32
LANES = 128
EDGE = 16
HALO = 14
FINE = ROWS + 2 * HALO
MID = FINE // 2
OWN2 = ROWS // 4
LOW_HALO = 10
LOW_TILES = (OWN2 + 2 * LOW_HALO) // 2
MID_LANE, MID_OWN = 32, 64
LOW_LANE, LOW_OWN, HALF = LOW_HALO, 32, 64
MID_HALO, MID_ROWS = HALO // 2, ROWS // 2


def lanes_of(rows):
    return lax.broadcasted_iota(jnp.int32, (rows, NZ, LANES), 2)


def layers_of(rows):
    return lax.broadcasted_iota(jnp.int32, (rows, NZ, LANES), 1)


def beside_lanes(parts, tiles):
    back = [pltpu.roll(part, 1, 2) for part in parts]
    ahead = [pltpu.roll(part, LANES - 1, 2) for part in parts]
    if len(parts) == 1:
        return back, ahead
    lane = lanes_of(parts[0].shape[0])
    before, after = lane < 1, lane >= LANES - 1
    south = [jnp.where(before, back[1 - t], back[t]) for t in tiles]
    north = [jnp.where(after, ahead[1 - t], ahead[t]) for t in tiles]
    return south, north


def six_sum(weights, t, here, west, own, east, south, north):
    total = weights[0, t, here] * west + weights[1, t, here] * east
    total += weights[4, t, here] * pltpu.roll(own, 1, 1)
    total += weights[5, t, here] * pltpu.roll(own, NZ - 1, 1)
    total += weights[2, t, here] * south
    total += weights[3, t, here] * north
    return total


def weighted(values, weights, row, rows, tiles):
    parts = [values[t, row + 1:row + 1 + rows] for t in range(values.shape[0])]
    south, north = beside_lanes(parts, tiles)
    totals = []
    for at, t in enumerate(tiles):
        west, east = values[t, row:row + rows], values[t, row + 2:row + 2 + rows]
        totals.append(six_sum(weights, t, slice(row, row + rows), west, parts[t], east,
                              south[at], north[at]))
    return [parts[t] for t in tiles], totals


def groups(first, end, rows=8):
    return [(row, min(rows, end - row)) for row in range(first, end, rows)]


def sweep(values, new, weights, right, first, end):
    tiles = range(values.shape[0])
    for row, rows in groups(first, end):
        old, total = weighted(values, weights, row, rows, tiles)
        for t in tiles:
            new[t, row + 1:row + 1 + rows] = (
                right[t, row:row + rows] + (1.0 - relaxation) * old[t] + total[t])


def scaled_faces(own, west, east, south, north, z_factor, keep=None):
    layer = layers_of(own.shape[0])
    half_z = 0.5 * z_factor
    faces = [
        0.5 * (own + west), 0.5 * (own + east), 0.5 * (own + south), 0.5 * (own + north),
        jnp.where(layer > 0, half_z * (own + pltpu.roll(own, 1, 1)), 0.0),
        jnp.where(layer < NZ - 1, half_z * (own + pltpu.roll(own, NZ - 1, 1)), 0.0),
    ]
    diagonal = faces[0] + faces[1] + faces[2] + faces[3] + faces[4] + faces[5]
    inside = own > 0.0
    inverse = jnp.where(inside, relaxation / jnp.where(inside, diagonal, 1.0), 0.0)
    if keep is not None:
        faces[0], faces[1] = faces[0] * keep[0], faces[1] * keep[1]
    return [inverse * face for face in faces], inverse, diagonal


def make_weights(conduct, weights, row, rows, z_factor):
    tiles = range(conduct.shape[0])
    parts = [conduct[t, row + 1:row + 1 + rows] for t in tiles]
    south, north = beside_lanes(parts, tiles)
    inverses, diagonals = [], []
    for t in tiles:
        west, east = conduct[t, row:row + rows], conduct[t, row + 2:row + 2 + rows]
        faces, inverse, diagonal = scaled_faces(
            parts[t], west, east, south[t], north[t], z_factor)
        for side in range(6):
            weights[side, t, row:row + rows] = faces[side]
        inverses.append(inverse)
        diagonals.append(diagonal)
    return inverses, diagonals


def low_rows_beside(values):
    first = pltpu.roll(values[LOW_TILES - 1:], HALF, 2)
    last = pltpu.roll(values[:1], HALF, 2)
    west = jnp.concatenate([first, values[:-1]], axis=0)
    east = jnp.concatenate([values[1:], last], axis=0)
    return west, east


def low_sum(values, weights):
    west, east = low_rows_beside(values)
    back, ahead = pltpu.roll(values, 1, 2), pltpu.roll(values, LANES - 1, 2)
    return six_sum(weights, 0, slice(0, LOW_TILES), west, values, east, back, ahead)


def pair_rows(values):
    rows = values.shape[0]
    return jnp.sum(values.reshape(rows // 2, 2, NZ, LANES), axis=1)


def twice_rows(values):
    rows = values.shape[0]
    wide = jnp.broadcast_to(values[:, None], (rows, 2, NZ, LANES))
    return wide.reshape(2 * rows, NZ, LANES)


def select_lanes(values, chosen):
    rows = values.shape[0]
    flat = jnp.dot(
        values.reshape(rows * NZ, LANES), chosen, precision=lax.Precision.HIGHEST,
        preferred_element_type=jnp.float32)
    return flat.reshape(rows, NZ, LANES)


def roll_lanes(tile, amount):
    amount = amount % LANES
    return tile if amount == 0 else pltpu.roll(tile, amount, 1)


def pack_edges(block, group, right_side):
    lane = lax.broadcasted_iota(jnp.int32, (NZ, LANES), 1)
    packed = None
    for j in range(8):
        moved = roll_lanes(block[8 * group + j], EDGE * j + (EDGE if right_side else 0))
        packed = moved if packed is None else jnp.where(lane // EDGE == j, moved, packed)
    return packed


def unpack_edges(left, right, j):
    lane = lax.broadcasted_iota(jnp.int32, (NZ, LANES), 1)
    from_right = roll_lanes(right, -EDGE * j)
    from_left = roll_lanes(left, -EDGE * (j + 1))
    return jnp.where(lane < EDGE, from_right, jnp.where(lane >= LANES - EDGE, from_left, 0.0))


def pack_low(rows):
    out = rows[0]
    for m in range(1, 4):
        out = out + roll_lanes(rows[m], LOW_OWN * m)
    return out


def unpack_low(get, scale_left, scale_right, scale_rows):
    lane = lax.broadcasted_iota(jnp.int32, (NZ, LANES), 1)
    rows = []
    far = LOW_HALO - OWN2
    parts = [(-2, 1, range(4 - far, 4)), (2, 0, range(far))]
    parts[1:1] = [(a, q, range(4)) for a in (-1, 0, 1) for q in (0, 1)]
    for a, q, members in parts:
        own = get(a, 0, q)
        left, right = roll_lanes(get(a, -1, q), -LOW_OWN), roll_lanes(get(a, 1, q), LOW_OWN)
        if scale_left is not None:
            left, right = left * scale_left, right * scale_right
        if scale_rows is not None and a != 0:
            scale = scale_rows[a]
            own, left, right = own * scale, left * scale, right * scale
        for m in members:
            row = len(rows)
            away = (lane - LOW_OWN * m) % LANES
            tile = jnp.where(
                away < LOW_OWN, own,
                jnp.where(away < LOW_OWN + LOW_LANE, right,
                          jnp.where(away >= LANES - LOW_LANE, left, 0.0)))
            half = HALF if row >= LOW_TILES else 0
            rows.append(roll_lanes(tile, half + LOW_LANE - LOW_OWN * m))
    return jnp.stack([rows[i] + rows[i + LOW_TILES] for i in range(LOW_TILES)])


def pack_mid(rows):
    lane = lax.broadcasted_iota(jnp.int32, (NZ, LANES), 1)
    return [
        jnp.where(lane < HALF, roll_lanes(rows[2 * j], -MID_LANE),
                  roll_lanes(rows[2 * j + 1], MID_LANE)) for j in range(MID_ROWS // 2)]


MID_AT, MID_TILES = {}, 0
for side in [(a, b) for a in (-1, 0, 1) for b in (-1, 0, 1) if (a, b) != (0, 0)]:
    MID_AT[side] = MID_TILES
    MID_TILES += MID_ROWS // 2 if side[0] == 0 else MID_ROWS // 4


LOW_AT, LOW_COUNT = {}, 0
for side in [(a, b) for a in (-2, 2, -1, 1, 0) for b in (-1, 1, 0) if (a, b) != (0, 0)]:
    LOW_AT[side] = LOW_COUNT
    LOW_COUNT += 1 if abs(side[0]) == 2 else 2


def start_low(send, got, send_sem, got_sem, near):
    for (a, b), at in LOW_AT.items():
        tiles, first = (1, 1 if a < 0 else 0) if abs(a) == 2 else (2, 0)
        pltpu.make_async_remote_copy(
            src_ref=send.at[pl.ds(first, tiles)],
            dst_ref=got.at[pl.ds(at, tiles)],
            send_sem=send_sem,
            recv_sem=got_sem,
            device_id=near(-a, -b),
            device_id_type=MESH,
        ).start()


def start_mid(send, got, send_sem, got_sem, near):
    for a, b in AROUND:
        count = MID_ROWS // 2 if a == 0 else MID_ROWS // 4
        pltpu.make_async_remote_copy(
            src_ref=send.at[pl.ds(MID_ROWS // 4 if a < 0 else 0, count)],
            dst_ref=got.at[pl.ds(MID_AT[a, b], count)],
            send_sem=send_sem,
            recv_sem=got_sem,
            device_id=near(-a, -b),
            device_id_type=MESH,
        ).start()


def unpack_mid(got, which, put):
    lane = lax.broadcasted_iota(jnp.int32, (NZ, LANES), 1)
    own = (lane >= MID_LANE) & (lane < MID_LANE + MID_OWN)
    for row in range(MID):
        a = -1 if row < MID_HALO else 0 if row < MID_HALO + MID_ROWS else 1
        source = row - MID_HALO - MID_ROWS * a
        tile, half = divmod(source - (MID_ROWS // 2 if a < 0 else 0), 2)
        turn = MID_LANE if half == 0 else -MID_LANE
        left, right = got[MID_AT[a, -1] + tile, which], got[MID_AT[a, 1] + tile, which]
        beside = roll_lanes(jnp.where(lane % HALF < MID_LANE, right, left), -turn)
        if a != 0:
            beside = jnp.where(own, roll_lanes(got[MID_AT[a, 0] + tile, which], turn), beside)
        put(row, a, own, beside)


class Exchange:
    def __init__(self, depth):
        self.depth = depth
        sizes = [depth] * 2 + [4] * 2 + [2] * 4
        self.at = [sum(sizes[:i]) for i in range(9)]

    def stage(self, edges, block):
        for side in (0, 1):
            for group in range(4):
                edges[side, group] = pack_edges(block, group, side == 1)

    def start(self, block, edges, got, send_sem, got_sem, near, rows):
        n, at = self.depth, self.at
        top, bottom = pl.ds(0, 2), pl.ds(2, 2)
        moves = [
            (block.at[pl.ds(ROWS - n, n)], 0, (1, 0)),
            (block.at[pl.ds(0, n)], 1, (-1, 0)),
            (edges.at[1], 2, (0, 1)),
            (edges.at[0], 3, (0, -1)),
            (edges.at[1, bottom], 4, (1, 1)),
            (edges.at[0, bottom], 5, (1, -1)),
            (edges.at[1, top], 6, (-1, 1)),
            (edges.at[0, top], 7, (-1, -1)),
        ]
        for source, slot, way in moves[:2] if rows else moves[:3:-1] + moves[2:4]:
            pltpu.make_async_remote_copy(
                src_ref=source,
                dst_ref=got.at[pl.ds(at[slot], at[slot + 1] - at[slot])],
                send_sem=send_sem,
                recv_sem=got_sem,
                device_id=near(*way),
                device_id_type=MESH,
            ).start()

    def unpack(self, got, put_rows, put_beside):
        n, at = self.depth, self.at
        put_rows(HALO - n, n, got[at[0]:at[0] + n])
        put_rows(HALO + ROWS, n, got[at[1]:at[1] + n])
        for i in range(FINE):
            if i < HALO:
                source = ROWS - HALO + i
                offset = at[4] - 2, at[5] - 2
            elif i < HALO + ROWS:
                source = i - HALO
                offset = at[2], at[3]
            else:
                source = i - HALO - ROWS
                offset = at[6], at[7]
            group, j = divmod(source, 8)
            put_beside(i, unpack_edges(got[offset[0] + group], got[offset[1] + group], j))


AROUND = [(a, b) for a in (-1, 1) for b in (-1, 1)] + [(-1, 0), (1, 0), (0, -1), (0, 1)]
FOR_K, FOR_F = Exchange(HALO), Exchange(HALO - 4)
THIN = HALO - FOR_F.depth


def kernel(strip_hbm, source_ref, coefficient_ref, out_ref,
           strip_ref, k_in, f_in, k_own, f_own, s_own, k_edge, f_edge, k_got, f_got,
           k0, c0, g0, d0, va, vb, k1, c1, i1, g1, d1, ua, ub, k2, c2, i2,
           weight, shifts, pick, l_own, l_send, l_got, m_send, m_got, n_send, n_got, one_send, one_got, two_send, two_got,
           picked, sems):
    px, py = lax.axis_index("px"), lax.axis_index("py")
    size_x, size_y = lax.axis_size("px"), lax.axis_size("py")
    strips = strip_ref.shape[0]

    def near(a, b):
        return (lax.rem(px + a + size_x, size_x), lax.rem(py + b + size_y, size_y))

    k_copy = pltpu.make_async_copy(coefficient_ref, k_in, sems.at[0])
    f_copy = pltpu.make_async_copy(source_ref, f_in, sems.at[1])
    strip_copy = pltpu.make_async_copy(strip_hbm, strip_ref, sems.at[26])
    k_copy.start()
    strip_copy.start()
    f_copy.start()
    def around_ring(offset, size):
        return min(offset % size, -offset % size)

    along_y = sorted(range(1, size_y), key=lambda b: -around_ring(b, size_y))
    along_x = sorted(
        range(1, size_x),
        key=lambda a: -around_ring(a % 4, 4) - around_ring((a + 1) // 4, size_x // 4))
    to_y, to_x = [(0, b) for b in along_y], [(a, 0) for a in along_x]
    peers = [(a, b) for a in (-2, 2) for b in (-1, 1)] + to_y + to_x
    peers += [way for way in AROUND if way[0] and way[1]]
    barrier = pltpu.get_barrier_semaphore()
    for way in peers:
        pl.semaphore_signal(barrier, inc=1, device_id=near(*way), device_id_type=MESH)

    def arrived(buffer, sem):
        pltpu.make_async_copy(buffer, buffer, sem).wait()

    def spread(source, got, sem, ways):
        for slot, way in enumerate(ways):
            pltpu.make_async_remote_copy(
                src_ref=source,
                dst_ref=got.at[slot],
                send_sem=sems.at[sem],
                recv_sem=sems.at[sem + 1],
                device_id=near(*way),
                device_id_type=MESH,
            ).start()

    one = lax.broadcasted_iota(jnp.int32, (LANES, LANES), 0)
    other = lax.broadcasted_iota(jnp.int32, (LANES, LANES), 1)

    def chosen(condition):
        return jnp.where(condition, 1.0, 0.0)

    def beside_pairs(wide, narrow):
        nearby = (wide < EDGE) & (narrow == MID_LANE + MID_OWN + wide // 2)
        return nearby | ((wide >= LANES - EDGE) & (narrow == MID_LANE - LANES // 2 + wide // 2))

    def low_of(mid, half):
        return half + LOW_LANE - MID_LANE // 2 + mid // 2

    mid_halo = EDGE
    mid_in = (other >= MID_LANE - mid_halo) & (other < MID_LANE + MID_OWN + mid_halo)
    tables = [
        chosen(other == MID_LANE + one // 2), chosen(beside_pairs(one, other)),
        chosen(one == MID_LANE + other // 2), chosen(beside_pairs(other, one)),
        chosen((one >= MID_LANE) & (one < MID_LANE + MID_OWN)
               & (other == (one - MID_LANE) // 2)),
        chosen(mid_in & (one == low_of(other, 0))), chosen(mid_in & (one == low_of(other, HALF))),
        chosen(other == one // 4),
    ]
    for at, table in enumerate(tables):
        picked[at] = table

    strip_copy.wait()
    ends, total = [], jnp.int32(0)
    for c in range(strips):
        total = total + strip_ref[c]
        ends.append(total)
    sub = lax.broadcasted_iota(jnp.int32, (8, LANES), 0)
    lane = lax.broadcasted_iota(jnp.int32, (8, LANES), 1)

    def strip_of(rows):
        found = jnp.zeros_like(rows)
        for end in ends:
            found = found + jnp.where(rows >= end, 1, 0)
        return found

    lane_strip = strip_of(lane)
    for tile in (0, 1):
        rows = jnp.clip(OWN2 * px - 4 + 8 * tile + sub, 0, OWN2 * size_x - 1)
        pick[tile] = jnp.where(strip_of(rows) == lane_strip, 1.0, 0.0)

    zero = jnp.zeros((NZ, LANES), jnp.float32)
    for ref, end in ((k0, FINE), (va, FINE), (vb, FINE), (k1, MID), (ua, MID), (ub, MID)):
        for t in range(ref.shape[0]):
            ref[t, 0] = zero
            ref[t, end + 1] = zero
    for i in range(THIN):
        va[0, 1 + i] = zero
        va[0, FINE - i] = zero
    for i in range(MID):
        ua[0, 1 + i] = zero

    k_copy.wait()
    for r in range(ROWS):
        k_own[r] = k_in[pl.ds(r, NZ, stride=ROWS), :]
    pl.semaphore_wait(barrier, len(peers))
    FOR_K.start(k_own, k_edge, k_got, sems.at[4], sems.at[5], near, True)
    lows = (1.0 / 16.0) * select_lanes(pair_rows(pair_rows(k_own[...])), picked[7])
    FOR_K.stage(k_edge, k_own)
    FOR_K.start(k_own, k_edge, k_got, sems.at[4], sems.at[5], near, False)
    for q in (0, 1):
        l_send[2, q] = pack_low([lows[4 * q + m] for m in range(4)])
    start_low(l_send.at[2], l_got.at[2], sems.at[2], sems.at[3], near)
    f_copy.wait()
    for r in range(ROWS):
        f_own[r] = f_in[pl.ds(r, NZ, stride=ROWS), :]
    FOR_F.start(f_own, f_edge, f_got, sems.at[6], sems.at[7], near, True)
    FOR_F.stage(f_edge, f_own)
    FOR_F.start(f_own, f_edge, f_got, sems.at[6], sems.at[7], near, False)

    wide_lane = lax.broadcasted_iota(jnp.int32, (NZ, LANES), 1)
    in_left, in_right = jnp.where(py > 0, 1.0, 0.0), jnp.where(py < size_y - 1, 1.0, 0.0)
    inner_y = jnp.where(wide_lane < LANES // 2, in_right, in_left)
    row_in = [jnp.where(px > 0, 1.0, 0.0), jnp.where(px < size_x - 1, 1.0, 0.0)]
    low_in = {-1: row_in[0], 1: row_in[1], -2: jnp.where(px > 1, 1.0, 0.0),
              2: jnp.where(px < size_x - 2, 1.0, 0.0)}

    kept = []
    for tile in range(4):
        rows = OWN2 * px - LOW_HALO + 8 * tile + sub
        flags = jnp.ones((8, LANES), jnp.float32)
        for end in ends:
            flags = jnp.where(rows == end, 0.0, flags)
        kept += [jnp.broadcast_to(flags[i:i + 1], (NZ, LANES)) for i in range(8)]
    lower_half = wide_lane < HALF
    keep = [
        jnp.stack([jnp.where(lower_half, kept[i + d], kept[i + d + LOW_TILES])
                   for i in range(LOW_TILES)]) for d in (0, 1)]

    def tiles_of(at):
        def get(a, b, q):
            if (a, b) == (0, 0):
                return l_send[at, q]
            return l_got[at, LOW_AT[a, b] + (0 if abs(a) == 2 else q)]

        return get

    arrived(l_got.at[2], sems.at[3])
    lows = unpack_low(tiles_of(2), in_left, in_right, low_in)
    k2[...] = lows
    west, east = low_rows_beside(lows)
    faces, inverse, diagonal = scaled_faces(
        lows, west, east, pltpu.roll(lows, 1, 2), pltpu.roll(lows, LANES - 1, 2),
        16.0 * z_coupling, keep)
    for side in range(6):
        c2[side, 0] = faces[side]
    i2[...] = inverse
    ones = jnp.where(lows > 0.0, 1.0, 0.0)
    for turn in range(COARSE_SWEEPS):
        ones = (1.0 - relaxation) * ones + low_sum(ones, c2)

    def own_low(values):
        out = []
        for r in range(LOW_HALO, LOW_HALO + OWN2):
            half = HALF if r >= LOW_TILES else 0
            moved = roll_lanes(values[r % LOW_TILES], -half - LOW_LANE)
            out.append(jnp.where(wide_lane < LOW_OWN, moved, 0.0))
        return jnp.stack(out)

    weight[...] = own_low(ones)

    def in_row(values):
        column = jnp.sum(jnp.sum(values, axis=1), axis=1, keepdims=True)
        return jnp.sum(jnp.where(lane == OWN2 * px + sub, column, 0.0), axis=0, keepdims=True)

    one_send[0, 1] = in_row(own_low(diagonal))

    def put_k_rows(first, rows, values):
        k0[0, 1 + first:1 + first + rows] = values * row_in[0 if first < HALO else 1]

    def put_k_beside(i, tile):
        tile = tile * inner_y
        if i < HALO or i >= HALO + ROWS:
            tile = tile * row_in[0 if i < HALO else 1]
        k0[1, 1 + i] = tile

    k0[0, 1 + HALO:1 + HALO + ROWS] = k_own[...]
    arrived(k_got, sems.at[5])
    FOR_K.unpack(k_got, put_k_rows, put_k_beside)

    def restrict(parts):
        total = select_lanes(pair_rows(parts[0]), picked[0])
        return total + select_lanes(pair_rows(parts[1]), picked[1])

    for row, rows in groups(0, FINE, 10):
        k1[0, row // 2 + 1:(row + rows) // 2 + 1] = 0.25 * restrict(
            [k0[t, row + 1:row + rows + 1] for t in (0, 1)])
    for row, rows in groups(THIN, FINE - THIN):
        inverse, diagonal = make_weights(k0, c0, row, rows, z_coupling)
        for t in (0, 1):
            g0[t, row:row + rows] = inverse[t]
            d0[t, row:row + rows] = (1.0 / relaxation) * diagonal[t]
    for row, rows in groups(0, MID, 10):
        inverse, diagonal = make_weights(k1, c1, row, rows, 4.0 * z_coupling)
        i1[0, row:row + rows] = inverse[0]
        d1[0, row:row + rows] = (1.0 / relaxation) * diagonal[0]

    va[0, 1 + HALO:1 + HALO + ROWS] = f_own[...]

    def put_f_rows(first, rows, values):
        va[0, 1 + first:1 + first + rows] = values

    def put_f_beside(i, tile):
        va[1, 1 + i] = tile

    arrived(f_got, sems.at[7])
    FOR_F.unpack(f_got, put_f_rows, put_f_beside)
    for row, rows in groups(THIN, FINE - THIN):
        for t in (0, 1):
            start = g0[t, row:row + rows] * va[t, row + 1:row + rows + 1]
            g0[t, row:row + rows] = start
            va[t, row + 1:row + rows + 1] = start

    def rows_0(halo):
        return HALO - halo, HALO + ROWS + halo

    def rows_1(halo):
        return MID_HALO - halo, MID_HALO + MID_ROWS + halo

    dens = None
    used = 8
    for cycle in range(CYCLES):
        if cycle > 0:
            sweep(va, vb, c0, g0, *rows_0(6))
            sweep(vb, va, c0, g0, *rows_0(6))
            fine, spare = va, vb
        else:
            sweep(va, vb, c0, g0, *rows_0(10))
            fine, spare = vb, va

        for row, rows in groups(*rows_0(4)):
            old, total = weighted(fine, c0, row, rows, (0, 1))
            here = slice(row, row + rows)
            rest = [
                d0[t, here] * (g0[t, here] - relaxation * old[t] + total[t]) for t in (0, 1)]
            half, count = row // 2, rows // 2
            start = i1[0, half:half + count] * restrict(rest)
            g1[0, half:half + count] = start
            ua[0, half + 1:half + count + 1] = start
        sweep(ua, ub, c1, g1, *rows_1(2))
        for part in (0, 1):
            row = MID_HALO + 8 * part
            old, total = weighted(ub, c1, row, 8, (0,))
            rest = d1[0, row:row + 8] * (
                g1[0, row:row + 8] - relaxation * old[0] + total[0])
            l_own[4 * part:4 * part + 4] = select_lanes(pair_rows(rest), picked[4])

        one_send[cycle, 0] = in_row(weight[...] * l_own[...])
        wide = 2 if cycle == 0 else 1
        one_out, one_in = one_send.at[cycle, pl.ds(0, wide)], one_got.at[cycle, :, pl.ds(0, wide)]
        two_out, two_in = two_send.at[cycle, pl.ds(0, wide)], two_got.at[cycle, :, pl.ds(0, wide)]
        spread(one_out, one_in, used, to_y)
        for q in (0, 1):
            l_send[cycle, q] = pack_low([l_own[4 * q + m] for m in range(4)])
        start_low(l_send.at[cycle], l_got.at[cycle], sems.at[used + 2], sems.at[used + 3], near)
        mids_out, mids_in = (m_send, m_got) if cycle == 0 else (n_send, n_got)
        for j, tile in enumerate(pack_mid(ub[0, 1 + MID_HALO:1 + MID_HALO + MID_ROWS])):
            mids_out[j, 0] = tile
        if cycle == 0:
            for j, tile in enumerate(pack_mid(g1[0, MID_HALO:MID_HALO + MID_ROWS])):
                mids_out[j, 1] = tile
        start_mid(mids_out, mids_in, sems.at[used + 6], sems.at[used + 7], near)
        arrived(one_in, sems.at[used + 1])
        for part in range(wide):
            two_send[cycle, part] = one_send[cycle, part] + jnp.sum(one_got[cycle, :, part], axis=0)
        spread(two_out, two_in, used + 4, to_x)

        arrived(l_got.at[cycle], sems.at[used + 3])
        right = i2[...] * unpack_low(tiles_of(cycle), None, None, None)
        low = right
        for turn in range(COARSE_SWEEPS - 1):
            low = right + (1.0 - relaxation) * low + low_sum(low, c2)
        def put_u(row, a, own, tile):
            tile = jnp.where(own, ub[0, 1 + row], tile) if a == 0 else tile
            ub[0, 1 + row] = jnp.where(k1[0, 1 + row] > 0.0, tile, 0.0)

        def put_g(row, a, own, tile):
            tile = jnp.where(own, g1[0, row], tile) if a == 0 else tile
            g1[0, row] = jnp.where(k1[0, 1 + row] > 0.0, tile, 0.0)

        arrived(mids_in, sems.at[used + 7])
        unpack_mid(mids_in, 0, put_u)
        if cycle == 0:
            unpack_mid(mids_in, 1, put_g)

        arrived(two_in, sems.at[used + 5])
        parts = []
        for part in range(wide):
            both = two_send[cycle, part] + jnp.sum(two_got[cycle, :, part], axis=0)
            row_sums = jnp.broadcast_to(both, (8, LANES))
            parts.append([jnp.sum(pick[tile] * row_sums, axis=1, keepdims=True) for tile in (0, 1)])
        if cycle == 0:
            dens = parts[1]
        for tile in (0, 1):
            shift = jnp.broadcast_to(parts[0][tile] / dens[tile], (8, LANES))
            for i in range(8):
                shifts[8 * tile + i] = jnp.broadcast_to(shift[i:i + 1], (NZ, LANES))

        for part in (0, 1):
            tiles = slice(LOW_TILES - 8, LOW_TILES) if part == 0 else slice(0, 8)
            moved = jnp.where(k2[tiles] > 0.0, shifts[8 * part:8 * part + 8], 0.0)
            wave = twice_rows(select_lanes(low[tiles] + moved, picked[5 + part]))
            at, count = (1, MID // 2) if part == 0 else (1 + MID // 2, MID // 2)
            ua[0, at:at + count] = ub[0, at:at + count] + (wave[1:] if part == 0 else wave[:-1])
        around = rows_1(6 if cycle == 0 else 2)
        sweep(ua, ub, c1, g1, *around)
        sweep(ub, ua, c1, g1, *around)

        for row, rows in groups(*rows_0(10 if cycle == 0 else 2)):
            wave = ua[0, row // 2 + 1:(row + rows) // 2 + 1]
            here = slice(row + 1, row + rows + 1)
            for t in (0, 1):
                spare[t, here] = fine[t, here] + twice_rows(select_lanes(wave, picked[2 + t]))
        if cycle < CYCLES - 1:
            sweep(spare, fine, c0, g0, *rows_0(8))
            sweep(fine, spare, c0, g0, *rows_0(8))
        else:
            sweep(spare, fine, c0, g0, *rows_0(1))
            for row, rows in groups(*rows_0(0)):
                old, total = weighted(fine, c0, row, rows, (0,))
                s_own[row - HALO:row - HALO + rows] = (
                    g0[0, row:row + rows] + (1.0 - relaxation) * old[0] + total[0])
        used += 8

    for r in range(ROWS):
        out_ref[pl.ds(r, NZ, stride=ROWS), :] = s_own[r]

    arrived(l_got.at[2], sems.at[2])
    arrived(k_got, sems.at[4])
    arrived(f_got, sems.at[6])
    arrived(m_got, sems.at[14])
    arrived(n_got, sems.at[22])
    for cycle, at in ((0, 8), (1, 16)):
        wide = pl.ds(0, 2 - cycle)
        arrived(one_got.at[cycle, :, wide], sems.at[at])
        arrived(l_got.at[cycle], sems.at[at + 2])
        arrived(two_got.at[cycle, :, wide], sems.at[at + 4])


def vmem(*shape):
    return pltpu.VMEM(shape + (NZ, LANES), jnp.float32)


def shards(source, coefficient, strip_rows):
    size_x, size_y = lax.axis_size("px"), lax.axis_size("py")
    flat = (NZ * ROWS, LANES)
    scratch = [pltpu.SMEM(strip_rows.shape, jnp.int32)] + [pltpu.VMEM(flat, jnp.float32)] * 2
    scratch += [vmem(ROWS), vmem(ROWS), vmem(ROWS), vmem(2, 4), vmem(2, 4)]
    scratch += [vmem(e.at[8]) for e in (FOR_K, FOR_F)]
    scratch += [vmem(2, FINE + 2), vmem(6, 2, FINE), vmem(2, FINE), vmem(2, FINE)]
    scratch += [vmem(2, FINE + 2), vmem(2, FINE + 2)]
    scratch += [vmem(1, MID + 2), vmem(6, 1, MID), vmem(1, MID), vmem(1, MID), vmem(1, MID)]
    scratch += [vmem(1, MID + 2), vmem(1, MID + 2)]
    scratch += [vmem(LOW_TILES), vmem(6, 1, LOW_TILES), vmem(LOW_TILES)]
    scratch += [vmem(OWN2), vmem(16), vmem(2), vmem(OWN2), vmem(3, 2), vmem(3, LOW_COUNT)]
    scratch += [vmem(MID_ROWS // 2, 2), vmem(MID_TILES, 2), vmem(MID_ROWS // 2, 1), vmem(MID_TILES, 1)]
    row = lambda *shape: pltpu.VMEM(shape + (1, LANES), jnp.float32)
    scratch += [row(2, 2), row(2, size_y - 1, 2), row(2, 2), row(2, size_x - 1, 2)]
    scratch += [pltpu.VMEM((8, LANES, LANES), jnp.float32), pltpu.SemaphoreType.DMA((27,))]
    hbm = pl.BlockSpec(memory_space=pltpu.HBM)
    done = pl.pallas_call(
        kernel,
        out_shape=jax.ShapeDtypeStruct(flat, jnp.float32),
        in_specs=[hbm, hbm, hbm],
        out_specs=pl.BlockSpec(memory_space=pltpu.VMEM),
        scratch_shapes=scratch,
        compiler_params=pltpu.CompilerParams(
            collective_id=0, has_side_effects=True, vmem_limit_bytes=60 << 20
        ),
        name="cycles",
    )(strip_rows, source.reshape(flat), coefficient.reshape(flat))
    return done.reshape(source.shape)


def solution(mesh):
    placed = (P(None, "px", "py"), P(None, "px", "py"), P())
    return jax.shard_map(
        shards, mesh=mesh, in_specs=placed, out_specs=P(None, "px", "py"), check_vma=False
    )
```

```python
import jax
import jax.numpy as jnp
from jax import lax
from jax.experimental import pallas as pl
from jax.experimental.pallas import tpu as pltpu
from jax.sharding import PartitionSpec as P

CYCLES = 2
COARSE_SWEEPS = 6
relaxation = 0.8
z_coupling = 0.25

MESH = pl.DeviceIdType.MESH

NZ = 8
ROWS = 32
LANES = 128
EDGE = 16
HALO = 14
FINE = ROWS + 2 * HALO
MID = FINE // 2
OWN2 = ROWS // 4
LOW_HALO = 10
LOW_TILES = (OWN2 + 2 * LOW_HALO) // 2
MID_LANE, MID_OWN = 32, 64
LOW_LANE, LOW_OWN, HALF = LOW_HALO, 32, 64
MID_HALO, MID_ROWS = HALO // 2, ROWS // 2


def lanes_of(rows):
    return lax.broadcasted_iota(jnp.int32, (rows, NZ, LANES), 2)


def layers_of(rows):
    return lax.broadcasted_iota(jnp.int32, (rows, NZ, LANES), 1)


def beside_lanes(parts, tiles):
    back = [pltpu.roll(part, 1, 2) for part in parts]
    ahead = [pltpu.roll(part, LANES - 1, 2) for part in parts]
    if len(parts) == 1:
        return back, ahead
    lane = lanes_of(parts[0].shape[0])
    before, after = lane < 1, lane >= LANES - 1
    south = [jnp.where(before, back[1 - t], back[t]) for t in tiles]
    north = [jnp.where(after, ahead[1 - t], ahead[t]) for t in tiles]
    return south, north


def six_sum(weights, t, here, west, own, east, south, north):
    total = weights[0, t, here] * west + weights[1, t, here] * east
    total += weights[4, t, here] * pltpu.roll(own, 1, 1)
    total += weights[5, t, here] * pltpu.roll(own, NZ - 1, 1)
    total += weights[2, t, here] * south
    total += weights[3, t, here] * north
    return total


def weighted(values, weights, row, rows, tiles):
    parts = [values[t, row + 1:row + 1 + rows] for t in range(values.shape[0])]
    south, north = beside_lanes(parts, tiles)
    totals = []
    for at, t in enumerate(tiles):
        west, east = values[t, row:row + rows], values[t, row + 2:row + 2 + rows]
        totals.append(six_sum(weights, t, slice(row, row + rows), west, parts[t], east,
                              south[at], north[at]))
    return [parts[t] for t in tiles], totals


def groups(first, end, rows=8):
    return [(row, min(rows, end - row)) for row in range(first, end, rows)]


def sweep(values, new, weights, right, first, end):
    tiles = range(values.shape[0])
    for row, rows in groups(first, end):
        old, total = weighted(values, weights, row, rows, tiles)
        for t in tiles:
            new[t, row + 1:row + 1 + rows] = (
                right[t, row:row + rows] + (1.0 - relaxation) * old[t] + total[t])


def scaled_faces(own, west, east, south, north, z_factor, keep=None):
    layer = layers_of(own.shape[0])
    half_z = 0.5 * z_factor
    faces = [
        0.5 * (own + west), 0.5 * (own + east), 0.5 * (own + south), 0.5 * (own + north),
        jnp.where(layer > 0, half_z * (own + pltpu.roll(own, 1, 1)), 0.0),
        jnp.where(layer < NZ - 1, half_z * (own + pltpu.roll(own, NZ - 1, 1)), 0.0),
    ]
    diagonal = faces[0] + faces[1] + faces[2] + faces[3] + faces[4] + faces[5]
    inside = own > 0.0
    inverse = jnp.where(inside, relaxation / jnp.where(inside, diagonal, 1.0), 0.0)
    if keep is not None:
        faces[0], faces[1] = faces[0] * keep[0], faces[1] * keep[1]
    return [inverse * face for face in faces], inverse, diagonal


def make_weights(conduct, weights, row, rows, z_factor):
    tiles = range(conduct.shape[0])
    parts = [conduct[t, row + 1:row + 1 + rows] for t in tiles]
    south, north = beside_lanes(parts, tiles)
    inverses, diagonals = [], []
    for t in tiles:
        west, east = conduct[t, row:row + rows], conduct[t, row + 2:row + 2 + rows]
        faces, inverse, diagonal = scaled_faces(
            parts[t], west, east, south[t], north[t], z_factor)
        for side in range(6):
            weights[side, t, row:row + rows] = faces[side]
        inverses.append(inverse)
        diagonals.append(diagonal)
    return inverses, diagonals


def low_rows_beside(values):
    first = pltpu.roll(values[LOW_TILES - 1:], HALF, 2)
    last = pltpu.roll(values[:1], HALF, 2)
    west = jnp.concatenate([first, values[:-1]], axis=0)
    east = jnp.concatenate([values[1:], last], axis=0)
    return west, east


def low_sum(values, weights):
    west, east = low_rows_beside(values)
    back, ahead = pltpu.roll(values, 1, 2), pltpu.roll(values, LANES - 1, 2)
    return six_sum(weights, 0, slice(0, LOW_TILES), west, values, east, back, ahead)


def pair_rows(values):
    rows = values.shape[0]
    return jnp.sum(values.reshape(rows // 2, 2, NZ, LANES), axis=1)


def twice_rows(values):
    rows = values.shape[0]
    wide = jnp.broadcast_to(values[:, None], (rows, 2, NZ, LANES))
    return wide.reshape(2 * rows, NZ, LANES)


def select_lanes(values, chosen):
    rows = values.shape[0]
    flat = jnp.dot(
        values.reshape(rows * NZ, LANES), chosen, precision=lax.Precision.HIGHEST,
        preferred_element_type=jnp.float32)
    return flat.reshape(rows, NZ, LANES)


def roll_lanes(tile, amount):
    amount = amount % LANES
    return tile if amount == 0 else pltpu.roll(tile, amount, 1)


def pack_edges(block, group, right_side):
    lane = lax.broadcasted_iota(jnp.int32, (NZ, LANES), 1)
    packed = None
    for j in range(8):
        moved = roll_lanes(block[8 * group + j], EDGE * j + (EDGE if right_side else 0))
        packed = moved if packed is None else jnp.where(lane // EDGE == j, moved, packed)
    return packed


def unpack_edges(left, right, j):
    lane = lax.broadcasted_iota(jnp.int32, (NZ, LANES), 1)
    from_right = roll_lanes(right, -EDGE * j)
    from_left = roll_lanes(left, -EDGE * (j + 1))
    return jnp.where(lane < EDGE, from_right, jnp.where(lane >= LANES - EDGE, from_left, 0.0))


def pack_low(rows):
    out = rows[0]
    for m in range(1, 4):
        out = out + roll_lanes(rows[m], LOW_OWN * m)
    return out


def unpack_low(get, scale_left, scale_right, scale_rows):
    lane = lax.broadcasted_iota(jnp.int32, (NZ, LANES), 1)
    rows = []
    far = LOW_HALO - OWN2
    parts = [(-2, 1, range(4 - far, 4)), (2, 0, range(far))]
    parts[1:1] = [(a, q, range(4)) for a in (-1, 0, 1) for q in (0, 1)]
    for a, q, members in parts:
        own = get(a, 0, q)
        left, right = roll_lanes(get(a, -1, q), -LOW_OWN), roll_lanes(get(a, 1, q), LOW_OWN)
        if scale_left is not None:
            left, right = left * scale_left, right * scale_right
        if scale_rows is not None and a != 0:
            scale = scale_rows[a]
            own, left, right = own * scale, left * scale, right * scale
        for m in members:
            row = len(rows)
            away = (lane - LOW_OWN * m) % LANES
            tile = jnp.where(
                away < LOW_OWN, own,
                jnp.where(away < LOW_OWN + LOW_LANE, right,
                          jnp.where(away >= LANES - LOW_LANE, left, 0.0)))
            half = HALF if row >= LOW_TILES else 0
            rows.append(roll_lanes(tile, half + LOW_LANE - LOW_OWN * m))
    return jnp.stack([rows[i] + rows[i + LOW_TILES] for i in range(LOW_TILES)])


def pack_mid(rows):
    lane = lax.broadcasted_iota(jnp.int32, (NZ, LANES), 1)
    return [
        jnp.where(lane < HALF, roll_lanes(rows[2 * j], -MID_LANE),
                  roll_lanes(rows[2 * j + 1], MID_LANE)) for j in range(MID_ROWS // 2)]


MID_AT, MID_TILES = {}, 0
for side in [(a, b) for a in (-1, 0, 1) for b in (-1, 0, 1) if (a, b) != (0, 0)]:
    MID_AT[side] = MID_TILES
    MID_TILES += MID_ROWS // 2 if side[0] == 0 else MID_ROWS // 4


LOW_AT, LOW_COUNT = {}, 0
for side in [(a, b) for a in (-2, 2, -1, 1, 0) for b in (-1, 1, 0) if (a, b) != (0, 0)]:
    LOW_AT[side] = LOW_COUNT
    LOW_COUNT += 1 if abs(side[0]) == 2 else 2


def start_low(send, got, send_sem, got_sem, near):
    for (a, b), at in LOW_AT.items():
        tiles, first = (1, 1 if a < 0 else 0) if abs(a) == 2 else (2, 0)
        pltpu.make_async_remote_copy(
            src_ref=send.at[pl.ds(first, tiles)],
            dst_ref=got.at[pl.ds(at, tiles)],
            send_sem=send_sem,
            recv_sem=got_sem,
            device_id=near(-a, -b),
            device_id_type=MESH,
        ).start()


def start_mid(send, got, send_sem, got_sem, near):
    for a, b in AROUND:
        count = MID_ROWS // 2 if a == 0 else MID_ROWS // 4
        pltpu.make_async_remote_copy(
            src_ref=send.at[pl.ds(MID_ROWS // 4 if a < 0 else 0, count)],
            dst_ref=got.at[pl.ds(MID_AT[a, b], count)],
            send_sem=send_sem,
            recv_sem=got_sem,
            device_id=near(-a, -b),
            device_id_type=MESH,
        ).start()


def unpack_mid(got, which, put):
    lane = lax.broadcasted_iota(jnp.int32, (NZ, LANES), 1)
    own = (lane >= MID_LANE) & (lane < MID_LANE + MID_OWN)
    for row in range(MID):
        a = -1 if row < MID_HALO else 0 if row < MID_HALO + MID_ROWS else 1
        source = row - MID_HALO - MID_ROWS * a
        tile, half = divmod(source - (MID_ROWS // 2 if a < 0 else 0), 2)
        turn = MID_LANE if half == 0 else -MID_LANE
        left, right = got[MID_AT[a, -1] + tile, which], got[MID_AT[a, 1] + tile, which]
        beside = roll_lanes(jnp.where(lane % HALF < MID_LANE, right, left), -turn)
        if a != 0:
            beside = jnp.where(own, roll_lanes(got[MID_AT[a, 0] + tile, which], turn), beside)
        put(row, a, own, beside)


class Exchange:
    def __init__(self, depth):
        self.depth = depth
        sizes = [depth] * 2 + [4] * 2 + [2] * 4
        self.at = [sum(sizes[:i]) for i in range(9)]

    def stage(self, edges, block):
        for side in (0, 1):
            for group in range(4):
                edges[side, group] = pack_edges(block, group, side == 1)

    def start(self, block, edges, got, send_sem, got_sem, near):
        n, at = self.depth, self.at
        top, bottom = pl.ds(0, 2), pl.ds(2, 2)
        moves = [
            (block.at[pl.ds(ROWS - n, n)], 0, (1, 0)),
            (block.at[pl.ds(0, n)], 1, (-1, 0)),
            (edges.at[1], 2, (0, 1)),
            (edges.at[0], 3, (0, -1)),
            (edges.at[1, bottom], 4, (1, 1)),
            (edges.at[0, bottom], 5, (1, -1)),
            (edges.at[1, top], 6, (-1, 1)),
            (edges.at[0, top], 7, (-1, -1)),
        ]
        for source, slot, way in moves[4:] + moves[:4]:
            pltpu.make_async_remote_copy(
                src_ref=source,
                dst_ref=got.at[pl.ds(at[slot], at[slot + 1] - at[slot])],
                send_sem=send_sem,
                recv_sem=got_sem,
                device_id=near(*way),
                device_id_type=MESH,
            ).start()

    def unpack(self, got, put_rows, put_beside):
        n, at = self.depth, self.at
        put_rows(HALO - n, n, got[at[0]:at[0] + n])
        put_rows(HALO + ROWS, n, got[at[1]:at[1] + n])
        for i in range(FINE):
            if i < HALO:
                source = ROWS - HALO + i
                offset = at[4] - 2, at[5] - 2
            elif i < HALO + ROWS:
                source = i - HALO
                offset = at[2], at[3]
            else:
                source = i - HALO - ROWS
                offset = at[6], at[7]
            group, j = divmod(source, 8)
            put_beside(i, unpack_edges(got[offset[0] + group], got[offset[1] + group], j))


AROUND = [(a, b) for a in (-1, 1) for b in (-1, 1)] + [(-1, 0), (1, 0), (0, -1), (0, 1)]
FOR_K, FOR_F = Exchange(HALO), Exchange(HALO - 4)
THIN = HALO - FOR_F.depth


def kernel(strip_hbm, source_ref, coefficient_ref, out_ref,
           strip_ref, k_in, f_in, k_own, f_own, s_own, k_edge, f_edge, k_got, f_got,
           k0, c0, g0, d0, va, vb, k1, c1, i1, g1, d1, ua, ub, k2, c2, i2,
           weight, shifts, pick, l_own, l_send, l_got, m_send, m_got, n_send, n_got, one_send, one_got, two_send, two_got,
           picked, sems):
    px, py = lax.axis_index("px"), lax.axis_index("py")
    size_x, size_y = lax.axis_size("px"), lax.axis_size("py")
    strips = strip_ref.shape[0]

    def near(a, b):
        return (lax.rem(px + a + size_x, size_x), lax.rem(py + b + size_y, size_y))

    k_copy = pltpu.make_async_copy(coefficient_ref, k_in, sems.at[0])
    f_copy = pltpu.make_async_copy(source_ref, f_in, sems.at[1])
    strip_copy = pltpu.make_async_copy(strip_hbm, strip_ref, sems.at[26])
    k_copy.start()
    strip_copy.start()
    f_copy.start()
    def around_ring(offset, size):
        return min(offset % size, -offset % size)

    along_y = sorted(range(1, size_y), key=lambda b: -around_ring(b, size_y))
    along_x = sorted(
        range(1, size_x),
        key=lambda a: -around_ring(a % 4, 4) - around_ring((a + 1) // 4, size_x // 4))
    to_y, to_x = [(0, b) for b in along_y], [(a, 0) for a in along_x]
    peers = [(a, b) for a in (-2, 2) for b in (-1, 1)] + to_y + to_x
    peers += [way for way in AROUND if way[0] and way[1]]
    barrier = pltpu.get_barrier_semaphore()
    for way in peers:
        pl.semaphore_signal(barrier, inc=1, device_id=near(*way), device_id_type=MESH)

    def arrived(buffer, sem):
        pltpu.make_async_copy(buffer, buffer, sem).wait()

    def spread(source, got, sem, ways):
        for slot, way in enumerate(ways):
            pltpu.make_async_remote_copy(
                src_ref=source,
                dst_ref=got.at[slot],
                send_sem=sems.at[sem],
                recv_sem=sems.at[sem + 1],
                device_id=near(*way),
                device_id_type=MESH,
            ).start()

    one = lax.broadcasted_iota(jnp.int32, (LANES, LANES), 0)
    other = lax.broadcasted_iota(jnp.int32, (LANES, LANES), 1)

    def chosen(condition):
        return jnp.where(condition, 1.0, 0.0)

    def beside_pairs(wide, narrow):
        nearby = (wide < EDGE) & (narrow == MID_LANE + MID_OWN + wide // 2)
        return nearby | ((wide >= LANES - EDGE) & (narrow == MID_LANE - LANES // 2 + wide // 2))

    def low_of(mid, half):
        return half + LOW_LANE - MID_LANE // 2 + mid // 2

    mid_halo = EDGE
    mid_in = (other >= MID_LANE - mid_halo) & (other < MID_LANE + MID_OWN + mid_halo)
    tables = [
        chosen(other == MID_LANE + one // 2), chosen(beside_pairs(one, other)),
        chosen(one == MID_LANE + other // 2), chosen(beside_pairs(other, one)),
        chosen((one >= MID_LANE) & (one < MID_LANE + MID_OWN)
               & (other == (one - MID_LANE) // 2)),
        chosen(mid_in & (one == low_of(other, 0))), chosen(mid_in & (one == low_of(other, HALF))),
        chosen(other == one // 4),
    ]
    for at, table in enumerate(tables):
        picked[at] = table

    strip_copy.wait()
    ends, total = [], jnp.int32(0)
    for c in range(strips):
        total = total + strip_ref[c]
        ends.append(total)
    sub = lax.broadcasted_iota(jnp.int32, (8, LANES), 0)
    lane = lax.broadcasted_iota(jnp.int32, (8, LANES), 1)

    def strip_of(rows):
        found = jnp.zeros_like(rows)
        for end in ends:
            found = found + jnp.where(rows >= end, 1, 0)
        return found

    lane_strip = strip_of(lane)
    for tile in (0, 1):
        rows = jnp.clip(OWN2 * px - 4 + 8 * tile + sub, 0, OWN2 * size_x - 1)
        pick[tile] = jnp.where(strip_of(rows) == lane_strip, 1.0, 0.0)

    zero = jnp.zeros((NZ, LANES), jnp.float32)
    for ref, end in ((k0, FINE), (va, FINE), (vb, FINE), (k1, MID), (ua, MID), (ub, MID)):
        for t in range(ref.shape[0]):
            ref[t, 0] = zero
            ref[t, end + 1] = zero
    for i in range(THIN):
        va[0, 1 + i] = zero
        va[0, FINE - i] = zero
    for i in range(MID):
        ua[0, 1 + i] = zero

    k_copy.wait()
    for r in range(ROWS):
        k_own[r] = k_in[pl.ds(r, NZ, stride=ROWS), :]
    lows = (1.0 / 16.0) * select_lanes(pair_rows(pair_rows(k_own[...])), picked[7])
    for q in (0, 1):
        l_send[2, q] = pack_low([lows[4 * q + m] for m in range(4)])
    FOR_K.stage(k_edge, k_own)
    f_copy.wait()
    for r in range(ROWS):
        f_own[r] = f_in[pl.ds(r, NZ, stride=ROWS), :]
    FOR_F.stage(f_edge, f_own)
    pl.semaphore_wait(barrier, len(peers))
    start_low(l_send.at[2], l_got.at[2], sems.at[2], sems.at[3], near)
    FOR_K.start(k_own, k_edge, k_got, sems.at[4], sems.at[5], near)
    FOR_F.start(f_own, f_edge, f_got, sems.at[6], sems.at[7], near)

    wide_lane = lax.broadcasted_iota(jnp.int32, (NZ, LANES), 1)
    in_left, in_right = jnp.where(py > 0, 1.0, 0.0), jnp.where(py < size_y - 1, 1.0, 0.0)
    inner_y = jnp.where(wide_lane < LANES // 2, in_right, in_left)
    row_in = [jnp.where(px > 0, 1.0, 0.0), jnp.where(px < size_x - 1, 1.0, 0.0)]
    low_in = {-1: row_in[0], 1: row_in[1], -2: jnp.where(px > 1, 1.0, 0.0),
              2: jnp.where(px < size_x - 2, 1.0, 0.0)}

    kept = []
    for tile in range(4):
        rows = OWN2 * px - LOW_HALO + 8 * tile + sub
        flags = jnp.ones((8, LANES), jnp.float32)
        for end in ends:
            flags = jnp.where(rows == end, 0.0, flags)
        kept += [jnp.broadcast_to(flags[i:i + 1], (NZ, LANES)) for i in range(8)]
    lower_half = wide_lane < HALF
    keep = [
        jnp.stack([jnp.where(lower_half, kept[i + d], kept[i + d + LOW_TILES])
                   for i in range(LOW_TILES)]) for d in (0, 1)]

    def tiles_of(at):
        def get(a, b, q):
            if (a, b) == (0, 0):
                return l_send[at, q]
            return l_got[at, LOW_AT[a, b] + (0 if abs(a) == 2 else q)]

        return get

    arrived(l_got.at[2], sems.at[3])
    lows = unpack_low(tiles_of(2), in_left, in_right, low_in)
    k2[...] = lows
    west, east = low_rows_beside(lows)
    faces, inverse, diagonal = scaled_faces(
        lows, west, east, pltpu.roll(lows, 1, 2), pltpu.roll(lows, LANES - 1, 2),
        16.0 * z_coupling, keep)
    for side in range(6):
        c2[side, 0] = faces[side]
    i2[...] = inverse
    ones = jnp.where(lows > 0.0, 1.0, 0.0)
    for turn in range(COARSE_SWEEPS):
        ones = (1.0 - relaxation) * ones + low_sum(ones, c2)

    def own_low(values):
        out = []
        for r in range(LOW_HALO, LOW_HALO + OWN2):
            half = HALF if r >= LOW_TILES else 0
            moved = roll_lanes(values[r % LOW_TILES], -half - LOW_LANE)
            out.append(jnp.where(wide_lane < LOW_OWN, moved, 0.0))
        return jnp.stack(out)

    weight[...] = own_low(ones)

    def in_row(values):
        column = jnp.sum(jnp.sum(values, axis=1), axis=1, keepdims=True)
        return jnp.sum(jnp.where(lane == OWN2 * px + sub, column, 0.0), axis=0, keepdims=True)

    one_send[0, 1] = in_row(own_low(diagonal))

    def put_k_rows(first, rows, values):
        k0[0, 1 + first:1 + first + rows] = values * row_in[0 if first < HALO else 1]

    def put_k_beside(i, tile):
        tile = tile * inner_y
        if i < HALO or i >= HALO + ROWS:
            tile = tile * row_in[0 if i < HALO else 1]
        k0[1, 1 + i] = tile

    k0[0, 1 + HALO:1 + HALO + ROWS] = k_own[...]
    arrived(k_got, sems.at[5])
    FOR_K.unpack(k_got, put_k_rows, put_k_beside)

    def restrict(parts):
        total = select_lanes(pair_rows(parts[0]), picked[0])
        return total + select_lanes(pair_rows(parts[1]), picked[1])

    for row, rows in groups(0, FINE, 10):
        k1[0, row // 2 + 1:(row + rows) // 2 + 1] = 0.25 * restrict(
            [k0[t, row + 1:row + rows + 1] for t in (0, 1)])
    for row, rows in groups(THIN, FINE - THIN):
        inverse, diagonal = make_weights(k0, c0, row, rows, z_coupling)
        for t in (0, 1):
            g0[t, row:row + rows] = inverse[t]
            d0[t, row:row + rows] = (1.0 / relaxation) * diagonal[t]
    for row, rows in groups(0, MID, 10):
        inverse, diagonal = make_weights(k1, c1, row, rows, 4.0 * z_coupling)
        i1[0, row:row + rows] = inverse[0]
        d1[0, row:row + rows] = (1.0 / relaxation) * diagonal[0]

    va[0, 1 + HALO:1 + HALO + ROWS] = f_own[...]

    def put_f_rows(first, rows, values):
        va[0, 1 + first:1 + first + rows] = values

    def put_f_beside(i, tile):
        va[1, 1 + i] = tile

    arrived(f_got, sems.at[7])
    FOR_F.unpack(f_got, put_f_rows, put_f_beside)
    for row, rows in groups(THIN, FINE - THIN):
        for t in (0, 1):
            start = g0[t, row:row + rows] * va[t, row + 1:row + rows + 1]
            g0[t, row:row + rows] = start
            va[t, row + 1:row + rows + 1] = start

    def rows_0(halo):
        return HALO - halo, HALO + ROWS + halo

    def rows_1(halo):
        return MID_HALO - halo, MID_HALO + MID_ROWS + halo

    dens = None
    used = 8
    for cycle in range(CYCLES):
        if cycle > 0:
            sweep(va, vb, c0, g0, *rows_0(6))
            sweep(vb, va, c0, g0, *rows_0(6))
            fine, spare = va, vb
        else:
            sweep(va, vb, c0, g0, *rows_0(10))
            fine, spare = vb, va

        for row, rows in groups(*rows_0(4)):
            old, total = weighted(fine, c0, row, rows, (0, 1))
            here = slice(row, row + rows)
            rest = [
                d0[t, here] * (g0[t, here] - relaxation * old[t] + total[t]) for t in (0, 1)]
            half, count = row // 2, rows // 2
            start = i1[0, half:half + count] * restrict(rest)
            g1[0, half:half + count] = start
            ua[0, half + 1:half + count + 1] = start
        sweep(ua, ub, c1, g1, *rows_1(2))
        for part in (0, 1):
            row = MID_HALO + 8 * part
            old, total = weighted(ub, c1, row, 8, (0,))
            rest = d1[0, row:row + 8] * (
                g1[0, row:row + 8] - relaxation * old[0] + total[0])
            l_own[4 * part:4 * part + 4] = select_lanes(pair_rows(rest), picked[4])

        one_send[cycle, 0] = in_row(weight[...] * l_own[...])
        wide = 2 if cycle == 0 else 1
        one_out, one_in = one_send.at[cycle, pl.ds(0, wide)], one_got.at[cycle, :, pl.ds(0, wide)]
        two_out, two_in = two_send.at[cycle, pl.ds(0, wide)], two_got.at[cycle, :, pl.ds(0, wide)]
        spread(one_out, one_in, used, to_y)
        for q in (0, 1):
            l_send[cycle, q] = pack_low([l_own[4 * q + m] for m in range(4)])
        start_low(l_send.at[cycle], l_got.at[cycle], sems.at[used + 2], sems.at[used + 3], near)
        mids_out, mids_in = (m_send, m_got) if cycle == 0 else (n_send, n_got)
        for j, tile in enumerate(pack_mid(ub[0, 1 + MID_HALO:1 + MID_HALO + MID_ROWS])):
            mids_out[j, 0] = tile
        if cycle == 0:
            for j, tile in enumerate(pack_mid(g1[0, MID_HALO:MID_HALO + MID_ROWS])):
                mids_out[j, 1] = tile
        start_mid(mids_out, mids_in, sems.at[used + 6], sems.at[used + 7], near)
        arrived(one_in, sems.at[used + 1])
        for part in range(wide):
            two_send[cycle, part] = one_send[cycle, part] + jnp.sum(one_got[cycle, :, part], axis=0)
        spread(two_out, two_in, used + 4, to_x)

        arrived(l_got.at[cycle], sems.at[used + 3])
        right = i2[...] * unpack_low(tiles_of(cycle), None, None, None)
        low = right
        for turn in range(COARSE_SWEEPS - 1):
            low = right + (1.0 - relaxation) * low + low_sum(low, c2)
        def put_u(row, a, own, tile):
            tile = jnp.where(own, ub[0, 1 + row], tile) if a == 0 else tile
            ub[0, 1 + row] = jnp.where(k1[0, 1 + row] > 0.0, tile, 0.0)

        def put_g(row, a, own, tile):
            tile = jnp.where(own, g1[0, row], tile) if a == 0 else tile
            g1[0, row] = jnp.where(k1[0, 1 + row] > 0.0, tile, 0.0)

        arrived(mids_in, sems.at[used + 7])
        unpack_mid(mids_in, 0, put_u)
        if cycle == 0:
            unpack_mid(mids_in, 1, put_g)

        arrived(two_in, sems.at[used + 5])
        parts = []
        for part in range(wide):
            both = two_send[cycle, part] + jnp.sum(two_got[cycle, :, part], axis=0)
            row_sums = jnp.broadcast_to(both, (8, LANES))
            parts.append([jnp.sum(pick[tile] * row_sums, axis=1, keepdims=True) for tile in (0, 1)])
        if cycle == 0:
            dens = parts[1]
        for tile in (0, 1):
            shift = jnp.broadcast_to(parts[0][tile] / dens[tile], (8, LANES))
            for i in range(8):
                shifts[8 * tile + i] = jnp.broadcast_to(shift[i:i + 1], (NZ, LANES))

        for part in (0, 1):
            tiles = slice(LOW_TILES - 8, LOW_TILES) if part == 0 else slice(0, 8)
            moved = jnp.where(k2[tiles] > 0.0, shifts[8 * part:8 * part + 8], 0.0)
            wave = twice_rows(select_lanes(low[tiles] + moved, picked[5 + part]))
            at, count = (1, MID // 2) if part == 0 else (1 + MID // 2, MID // 2)
            ua[0, at:at + count] = ub[0, at:at + count] + (wave[1:] if part == 0 else wave[:-1])
        around = rows_1(6 if cycle == 0 else 2)
        sweep(ua, ub, c1, g1, *around)
        sweep(ub, ua, c1, g1, *around)

        for row, rows in groups(*rows_0(10 if cycle == 0 else 2)):
            wave = ua[0, row // 2 + 1:(row + rows) // 2 + 1]
            here = slice(row + 1, row + rows + 1)
            for t in (0, 1):
                spare[t, here] = fine[t, here] + twice_rows(select_lanes(wave, picked[2 + t]))
        if cycle < CYCLES - 1:
            sweep(spare, fine, c0, g0, *rows_0(8))
            sweep(fine, spare, c0, g0, *rows_0(8))
        else:
            sweep(spare, fine, c0, g0, *rows_0(1))
            for row, rows in groups(*rows_0(0)):
                old, total = weighted(fine, c0, row, rows, (0,))
                s_own[row - HALO:row - HALO + rows] = (
                    g0[0, row:row + rows] + (1.0 - relaxation) * old[0] + total[0])
        used += 8

    for r in range(ROWS):
        out_ref[pl.ds(r, NZ, stride=ROWS), :] = s_own[r]

    arrived(l_got.at[2], sems.at[2])
    arrived(k_got, sems.at[4])
    arrived(f_got, sems.at[6])
    arrived(m_got, sems.at[14])
    arrived(n_got, sems.at[22])
    for cycle, at in ((0, 8), (1, 16)):
        wide = pl.ds(0, 2 - cycle)
        arrived(one_got.at[cycle, :, wide], sems.at[at])
        arrived(l_got.at[cycle], sems.at[at + 2])
        arrived(two_got.at[cycle, :, wide], sems.at[at + 4])


def vmem(*shape):
    return pltpu.VMEM(shape + (NZ, LANES), jnp.float32)


def shards(source, coefficient, strip_rows):
    size_x, size_y = lax.axis_size("px"), lax.axis_size("py")
    flat = (NZ * ROWS, LANES)
    scratch = [pltpu.SMEM(strip_rows.shape, jnp.int32)] + [pltpu.VMEM(flat, jnp.float32)] * 2
    scratch += [vmem(ROWS), vmem(ROWS), vmem(ROWS), vmem(2, 4), vmem(2, 4)]
    scratch += [vmem(e.at[8]) for e in (FOR_K, FOR_F)]
    scratch += [vmem(2, FINE + 2), vmem(6, 2, FINE), vmem(2, FINE), vmem(2, FINE)]
    scratch += [vmem(2, FINE + 2), vmem(2, FINE + 2)]
    scratch += [vmem(1, MID + 2), vmem(6, 1, MID), vmem(1, MID), vmem(1, MID), vmem(1, MID)]
    scratch += [vmem(1, MID + 2), vmem(1, MID + 2)]
    scratch += [vmem(LOW_TILES), vmem(6, 1, LOW_TILES), vmem(LOW_TILES)]
    scratch += [vmem(OWN2), vmem(16), vmem(2), vmem(OWN2), vmem(3, 2), vmem(3, LOW_COUNT)]
    scratch += [vmem(MID_ROWS // 2, 2), vmem(MID_TILES, 2), vmem(MID_ROWS // 2, 1), vmem(MID_TILES, 1)]
    row = lambda *shape: pltpu.VMEM(shape + (1, LANES), jnp.float32)
    scratch += [row(2, 2), row(2, size_y - 1, 2), row(2, 2), row(2, size_x - 1, 2)]
    scratch += [pltpu.VMEM((8, LANES, LANES), jnp.float32), pltpu.SemaphoreType.DMA((27,))]
    hbm = pl.BlockSpec(memory_space=pltpu.HBM)
    done = pl.pallas_call(
        kernel,
        out_shape=jax.ShapeDtypeStruct(flat, jnp.float32),
        in_specs=[hbm, hbm, hbm],
        out_specs=pl.BlockSpec(memory_space=pltpu.VMEM),
        scratch_shapes=scratch,
        compiler_params=pltpu.CompilerParams(
            collective_id=0, has_side_effects=True, vmem_limit_bytes=60 << 20
        ),
        name="cycles",
    )(strip_rows, source.reshape(flat), coefficient.reshape(flat))
    return done.reshape(source.shape)


def solution(mesh):
    placed = (P(None, "px", "py"), P(None, "px", "py"), P())
    return jax.shard_map(
        shards, mesh=mesh, in_specs=placed, out_specs=P(None, "px", "py"), check_vma=False
    )
```

```python
import jax
import jax.numpy as jnp
from jax import lax
from jax.experimental import pallas as pl
from jax.experimental.pallas import tpu as pltpu
from jax.sharding import PartitionSpec as P

CYCLES = 2
COARSE_SWEEPS = 6
relaxation = 0.8
z_coupling = 0.25

MESH = pl.DeviceIdType.MESH

NZ = 8
ROWS = 32
LANES = 128
EDGE = 16
HALO = 14
FINE = ROWS + 2 * HALO
MID = FINE // 2
OWN2 = ROWS // 4
LOW_HALO = 10
LOW_TILES = (OWN2 + 2 * LOW_HALO) // 2
MID_LANE, MID_OWN = 32, 64
LOW_LANE, LOW_OWN, HALF = LOW_HALO, 32, 64
MID_HALO, MID_ROWS = HALO // 2, ROWS // 2


def lanes_of(rows):
    return lax.broadcasted_iota(jnp.int32, (rows, NZ, LANES), 2)


def layers_of(rows):
    return lax.broadcasted_iota(jnp.int32, (rows, NZ, LANES), 1)


def beside_lanes(parts, tiles):
    back = [pltpu.roll(part, 1, 2) for part in parts]
    ahead = [pltpu.roll(part, LANES - 1, 2) for part in parts]
    if len(parts) == 1:
        return back, ahead
    lane = lanes_of(parts[0].shape[0])
    before, after = lane < 1, lane >= LANES - 1
    south = [jnp.where(before, back[1 - t], back[t]) for t in tiles]
    north = [jnp.where(after, ahead[1 - t], ahead[t]) for t in tiles]
    return south, north


def six_sum(weights, t, here, west, own, east, south, north):
    total = weights[0, t, here] * west + weights[1, t, here] * east
    total += weights[4, t, here] * pltpu.roll(own, 1, 1)
    total += weights[5, t, here] * pltpu.roll(own, NZ - 1, 1)
    total += weights[2, t, here] * south
    total += weights[3, t, here] * north
    return total


def weighted(values, weights, row, rows, tiles):
    parts = [values[t, row + 1:row + 1 + rows] for t in range(values.shape[0])]
    south, north = beside_lanes(parts, tiles)
    totals = []
    for at, t in enumerate(tiles):
        west, east = values[t, row:row + rows], values[t, row + 2:row + 2 + rows]
        totals.append(six_sum(weights, t, slice(row, row + rows), west, parts[t], east,
                              south[at], north[at]))
    return [parts[t] for t in tiles], totals


def groups(first, end, rows=8):
    return [(row, min(rows, end - row)) for row in range(first, end, rows)]


def sweep(values, new, weights, right, first, end):
    tiles = range(values.shape[0])
    for row, rows in groups(first, end):
        old, total = weighted(values, weights, row, rows, tiles)
        for t in tiles:
            new[t, row + 1:row + 1 + rows] = (
                right[t, row:row + rows] + (1.0 - relaxation) * old[t] + total[t])


def scaled_faces(own, west, east, south, north, z_factor, keep=None):
    layer = layers_of(own.shape[0])
    half_z = 0.5 * z_factor
    faces = [
        0.5 * (own + west), 0.5 * (own + east), 0.5 * (own + south), 0.5 * (own + north),
        jnp.where(layer > 0, half_z * (own + pltpu.roll(own, 1, 1)), 0.0),
        jnp.where(layer < NZ - 1, half_z * (own + pltpu.roll(own, NZ - 1, 1)), 0.0),
    ]
    diagonal = faces[0] + faces[1] + faces[2] + faces[3] + faces[4] + faces[5]
    inside = own > 0.0
    inverse = jnp.where(inside, relaxation / jnp.where(inside, diagonal, 1.0), 0.0)
    if keep is not None:
        faces[0], faces[1] = faces[0] * keep[0], faces[1] * keep[1]
    return [inverse * face for face in faces], inverse, diagonal


def make_weights(conduct, weights, row, rows, z_factor):
    tiles = range(conduct.shape[0])
    parts = [conduct[t, row + 1:row + 1 + rows] for t in tiles]
    south, north = beside_lanes(parts, tiles)
    inverses, diagonals = [], []
    for t in tiles:
        west, east = conduct[t, row:row + rows], conduct[t, row + 2:row + 2 + rows]
        faces, inverse, diagonal = scaled_faces(
            parts[t], west, east, south[t], north[t], z_factor)
        for side in range(6):
            weights[side, t, row:row + rows] = faces[side]
        inverses.append(inverse)
        diagonals.append(diagonal)
    return inverses, diagonals


def low_rows_beside(values):
    first = pltpu.roll(values[LOW_TILES - 1:], HALF, 2)
    last = pltpu.roll(values[:1], HALF, 2)
    west = jnp.concatenate([first, values[:-1]], axis=0)
    east = jnp.concatenate([values[1:], last], axis=0)
    return west, east


def low_sum(values, weights):
    west, east = low_rows_beside(values)
    back, ahead = pltpu.roll(values, 1, 2), pltpu.roll(values, LANES - 1, 2)
    return six_sum(weights, 0, slice(0, LOW_TILES), west, values, east, back, ahead)


def pair_rows(values):
    rows = values.shape[0]
    return jnp.sum(values.reshape(rows // 2, 2, NZ, LANES), axis=1)


def twice_rows(values):
    rows = values.shape[0]
    wide = jnp.broadcast_to(values[:, None], (rows, 2, NZ, LANES))
    return wide.reshape(2 * rows, NZ, LANES)


def select_lanes(values, chosen):
    rows = values.shape[0]
    flat = jnp.dot(
        values.reshape(rows * NZ, LANES), chosen, precision=lax.Precision.HIGHEST,
        preferred_element_type=jnp.float32)
    return flat.reshape(rows, NZ, LANES)


def roll_lanes(tile, amount):
    amount = amount % LANES
    return tile if amount == 0 else pltpu.roll(tile, amount, 1)


def pack_edges(block, group, right_side):
    lane = lax.broadcasted_iota(jnp.int32, (NZ, LANES), 1)
    packed = None
    for j in range(8):
        moved = roll_lanes(block[8 * group + j], EDGE * j + (EDGE if right_side else 0))
        packed = moved if packed is None else jnp.where(lane // EDGE == j, moved, packed)
    return packed


def unpack_edges(left, right, j):
    lane = lax.broadcasted_iota(jnp.int32, (NZ, LANES), 1)
    from_right = roll_lanes(right, -EDGE * j)
    from_left = roll_lanes(left, -EDGE * (j + 1))
    return jnp.where(lane < EDGE, from_right, jnp.where(lane >= LANES - EDGE, from_left, 0.0))


def pack_low(rows):
    out = rows[0]
    for m in range(1, 4):
        out = out + roll_lanes(rows[m], LOW_OWN * m)
    return out


def unpack_low(get, scale_left, scale_right, scale_rows):
    lane = lax.broadcasted_iota(jnp.int32, (NZ, LANES), 1)
    rows = []
    far = LOW_HALO - OWN2
    parts = [(-2, 1, range(4 - far, 4)), (2, 0, range(far))]
    parts[1:1] = [(a, q, range(4)) for a in (-1, 0, 1) for q in (0, 1)]
    for a, q, members in parts:
        own = get(a, 0, q)
        left, right = roll_lanes(get(a, -1, q), -LOW_OWN), roll_lanes(get(a, 1, q), LOW_OWN)
        if scale_left is not None:
            left, right = left * scale_left, right * scale_right
        if scale_rows is not None and a != 0:
            scale = scale_rows[a]
            own, left, right = own * scale, left * scale, right * scale
        for m in members:
            row = len(rows)
            away = (lane - LOW_OWN * m) % LANES
            tile = jnp.where(
                away < LOW_OWN, own,
                jnp.where(away < LOW_OWN + LOW_LANE, right,
                          jnp.where(away >= LANES - LOW_LANE, left, 0.0)))
            half = HALF if row >= LOW_TILES else 0
            rows.append(roll_lanes(tile, half + LOW_LANE - LOW_OWN * m))
    return jnp.stack([rows[i] + rows[i + LOW_TILES] for i in range(LOW_TILES)])


def pack_mid(rows):
    lane = lax.broadcasted_iota(jnp.int32, (NZ, LANES), 1)
    return [
        jnp.where(lane < HALF, roll_lanes(rows[2 * j], -MID_LANE),
                  roll_lanes(rows[2 * j + 1], MID_LANE)) for j in range(MID_ROWS // 2)]


MID_AT, MID_TILES = {}, 0
for side in [(a, b) for a in (-1, 0, 1) for b in (-1, 0, 1) if (a, b) != (0, 0)]:
    MID_AT[side] = MID_TILES
    MID_TILES += MID_ROWS // 2 if side[0] == 0 else MID_ROWS // 4


LOW_AT, LOW_COUNT = {}, 0
for side in [(a, b) for a in (-2, 2, -1, 1, 0) for b in (-1, 1, 0) if (a, b) != (0, 0)]:
    LOW_AT[side] = LOW_COUNT
    LOW_COUNT += 1 if abs(side[0]) == 2 else 2


def start_low(send, got, send_sem, got_sem, near):
    for (a, b), at in LOW_AT.items():
        tiles, first = (1, 1 if a < 0 else 0) if abs(a) == 2 else (2, 0)
        pltpu.make_async_remote_copy(
            src_ref=send.at[pl.ds(first, tiles)],
            dst_ref=got.at[pl.ds(at, tiles)],
            send_sem=send_sem,
            recv_sem=got_sem,
            device_id=near(-a, -b),
            device_id_type=MESH,
        ).start()


def start_mid(send, got, send_sem, got_sem, near):
    for a, b in AROUND:
        count = MID_ROWS // 2 if a == 0 else MID_ROWS // 4
        pltpu.make_async_remote_copy(
            src_ref=send.at[pl.ds(MID_ROWS // 4 if a < 0 else 0, count)],
            dst_ref=got.at[pl.ds(MID_AT[a, b], count)],
            send_sem=send_sem,
            recv_sem=got_sem,
            device_id=near(-a, -b),
            device_id_type=MESH,
        ).start()


def unpack_mid(got, which, put):
    lane = lax.broadcasted_iota(jnp.int32, (NZ, LANES), 1)
    own = (lane >= MID_LANE) & (lane < MID_LANE + MID_OWN)
    for row in range(MID):
        a = -1 if row < MID_HALO else 0 if row < MID_HALO + MID_ROWS else 1
        source = row - MID_HALO - MID_ROWS * a
        tile, half = divmod(source - (MID_ROWS // 2 if a < 0 else 0), 2)
        turn = MID_LANE if half == 0 else -MID_LANE
        left, right = got[MID_AT[a, -1] + tile, which], got[MID_AT[a, 1] + tile, which]
        beside = roll_lanes(jnp.where(lane % HALF < MID_LANE, right, left), -turn)
        if a != 0:
            beside = jnp.where(own, roll_lanes(got[MID_AT[a, 0] + tile, which], turn), beside)
        put(row, a, own, beside)


class Exchange:
    def __init__(self, depth):
        self.depth = depth
        sizes = [depth] * 2 + [4] * 2 + [2] * 4
        self.at = [sum(sizes[:i]) for i in range(9)]

    def stage(self, edges, block):
        for side in (0, 1):
            for group in range(4):
                edges[side, group] = pack_edges(block, group, side == 1)

    def start(self, block, edges, got, send_sem, got_sem, near):
        n, at = self.depth, self.at
        top, bottom = pl.ds(0, 2), pl.ds(2, 2)
        moves = [
            (block.at[pl.ds(ROWS - n, n)], 0, (1, 0)),
            (block.at[pl.ds(0, n)], 1, (-1, 0)),
            (edges.at[1], 2, (0, 1)),
            (edges.at[0], 3, (0, -1)),
            (edges.at[1, bottom], 4, (1, 1)),
            (edges.at[0, bottom], 5, (1, -1)),
            (edges.at[1, top], 6, (-1, 1)),
            (edges.at[0, top], 7, (-1, -1)),
        ]
        for source, slot, way in moves[4:] + moves[:4]:
            pltpu.make_async_remote_copy(
                src_ref=source,
                dst_ref=got.at[pl.ds(at[slot], at[slot + 1] - at[slot])],
                send_sem=send_sem,
                recv_sem=got_sem,
                device_id=near(*way),
                device_id_type=MESH,
            ).start()

    def unpack(self, got, put_rows, put_beside):
        n, at = self.depth, self.at
        put_rows(HALO - n, n, got[at[0]:at[0] + n])
        put_rows(HALO + ROWS, n, got[at[1]:at[1] + n])
        for i in range(FINE):
            if i < HALO:
                source = ROWS - HALO + i
                offset = at[4] - 2, at[5] - 2
            elif i < HALO + ROWS:
                source = i - HALO
                offset = at[2], at[3]
            else:
                source = i - HALO - ROWS
                offset = at[6], at[7]
            group, j = divmod(source, 8)
            put_beside(i, unpack_edges(got[offset[0] + group], got[offset[1] + group], j))


AROUND = [(a, b) for a in (-1, 1) for b in (-1, 1)] + [(-1, 0), (1, 0), (0, -1), (0, 1)]
FOR_K, FOR_F = Exchange(HALO), Exchange(HALO - 4)
THIN = HALO - FOR_F.depth


def kernel(strip_hbm, source_ref, coefficient_ref, out_ref,
           strip_ref, k_in, f_in, k_own, f_own, s_own, k_edge, f_edge, k_got, f_got,
           k0, c0, g0, d0, va, vb, k1, c1, i1, g1, d1, ua, ub, k2, c2, i2,
           weight, shifts, pick, l_own, l_send, l_got, m_send, m_got, n_send, n_got, one_send, one_got, two_send, two_got,
           picked, sems):
    px, py = lax.axis_index("px"), lax.axis_index("py")
    size_x, size_y = lax.axis_size("px"), lax.axis_size("py")
    strips = strip_ref.shape[0]

    def near(a, b):
        return (lax.rem(px + a + size_x, size_x), lax.rem(py + b + size_y, size_y))

    k_copy = pltpu.make_async_copy(coefficient_ref, k_in, sems.at[0])
    f_copy = pltpu.make_async_copy(source_ref, f_in, sems.at[1])
    strip_copy = pltpu.make_async_copy(strip_hbm, strip_ref, sems.at[26])
    k_copy.start()
    strip_copy.start()
    f_copy.start()
    def around_ring(offset, size):
        return min(offset % size, -offset % size)

    along_y = sorted(range(1, size_y), key=lambda b: -around_ring(b, size_y))
    along_x = sorted(
        range(1, size_x),
        key=lambda a: -around_ring(a % 4, 4) - around_ring((a + 1) // 4, size_x // 4))
    to_y, to_x = [(0, b) for b in along_y], [(a, 0) for a in along_x]
    peers = [(a, b) for a in (-2, 2) for b in (-1, 1)] + to_y + to_x
    peers += [way for way in AROUND if way[0] and way[1]]
    barrier = pltpu.get_barrier_semaphore()
    for way in peers:
        pl.semaphore_signal(barrier, inc=1, device_id=near(*way), device_id_type=MESH)

    def arrived(buffer, sem):
        pltpu.make_async_copy(buffer, buffer, sem).wait()

    def spread(source, got, sem, ways):
        for slot, way in enumerate(ways):
            pltpu.make_async_remote_copy(
                src_ref=source,
                dst_ref=got.at[slot],
                send_sem=sems.at[sem],
                recv_sem=sems.at[sem + 1],
                device_id=near(*way),
                device_id_type=MESH,
            ).start()

    one = lax.broadcasted_iota(jnp.int32, (LANES, LANES), 0)
    other = lax.broadcasted_iota(jnp.int32, (LANES, LANES), 1)

    def chosen(condition):
        return jnp.where(condition, 1.0, 0.0)

    def beside_pairs(wide, narrow):
        nearby = (wide < EDGE) & (narrow == MID_LANE + MID_OWN + wide // 2)
        return nearby | ((wide >= LANES - EDGE) & (narrow == MID_LANE - LANES // 2 + wide // 2))

    def low_of(mid, half):
        return half + LOW_LANE - MID_LANE // 2 + mid // 2

    mid_halo = EDGE
    mid_in = (other >= MID_LANE - mid_halo) & (other < MID_LANE + MID_OWN + mid_halo)
    tables = [
        chosen(other == MID_LANE + one // 2), chosen(beside_pairs(one, other)),
        chosen(one == MID_LANE + other // 2), chosen(beside_pairs(other, one)),
        chosen((one >= MID_LANE) & (one < MID_LANE + MID_OWN)
               & (other == (one - MID_LANE) // 2)),
        chosen(mid_in & (one == low_of(other, 0))), chosen(mid_in & (one == low_of(other, HALF))),
        chosen(other == one // 4),
    ]
    for at, table in enumerate(tables):
        picked[at] = table

    strip_copy.wait()
    ends, total = [], jnp.int32(0)
    for c in range(strips):
        total = total + strip_ref[c]
        ends.append(total)
    sub = lax.broadcasted_iota(jnp.int32, (8, LANES), 0)
    lane = lax.broadcasted_iota(jnp.int32, (8, LANES), 1)

    def strip_of(rows):
        found = jnp.zeros_like(rows)
        for end in ends:
            found = found + jnp.where(rows >= end, 1, 0)
        return found

    lane_strip = strip_of(lane)
    for tile in (0, 1):
        rows = jnp.clip(OWN2 * px - 4 + 8 * tile + sub, 0, OWN2 * size_x - 1)
        pick[tile] = jnp.where(strip_of(rows) == lane_strip, 1.0, 0.0)

    zero = jnp.zeros((NZ, LANES), jnp.float32)
    for ref, end in ((k0, FINE), (va, FINE), (vb, FINE), (k1, MID), (ua, MID), (ub, MID)):
        for t in range(ref.shape[0]):
            ref[t, 0] = zero
            ref[t, end + 1] = zero
    for i in range(THIN):
        va[0, 1 + i] = zero
        va[0, FINE - i] = zero
    for i in range(MID):
        ua[0, 1 + i] = zero

    k_copy.wait()
    for r in range(ROWS):
        k_own[r] = k_in[pl.ds(r, NZ, stride=ROWS), :]
    lows = (1.0 / 16.0) * select_lanes(pair_rows(pair_rows(k_own[...])), picked[7])
    for q in (0, 1):
        l_send[2, q] = pack_low([lows[4 * q + m] for m in range(4)])
    FOR_K.stage(k_edge, k_own)
    f_copy.wait()
    for r in range(ROWS):
        f_own[r] = f_in[pl.ds(r, NZ, stride=ROWS), :]
    FOR_F.stage(f_edge, f_own)
    pl.semaphore_wait(barrier, len(peers))
    start_low(l_send.at[2], l_got.at[2], sems.at[2], sems.at[3], near)
    FOR_K.start(k_own, k_edge, k_got, sems.at[4], sems.at[5], near)
    FOR_F.start(f_own, f_edge, f_got, sems.at[6], sems.at[7], near)

    wide_lane = lax.broadcasted_iota(jnp.int32, (NZ, LANES), 1)
    in_left, in_right = jnp.where(py > 0, 1.0, 0.0), jnp.where(py < size_y - 1, 1.0, 0.0)
    inner_y = jnp.where(wide_lane < LANES // 2, in_right, in_left)
    row_in = [jnp.where(px > 0, 1.0, 0.0), jnp.where(px < size_x - 1, 1.0, 0.0)]
    low_in = {-1: row_in[0], 1: row_in[1], -2: jnp.where(px > 1, 1.0, 0.0),
              2: jnp.where(px < size_x - 2, 1.0, 0.0)}

    kept = []
    for tile in range(4):
        rows = OWN2 * px - LOW_HALO + 8 * tile + sub
        flags = jnp.ones((8, LANES), jnp.float32)
        for end in ends:
            flags = jnp.where(rows == end, 0.0, flags)
        kept += [jnp.broadcast_to(flags[i:i + 1], (NZ, LANES)) for i in range(8)]
    lower_half = wide_lane < HALF
    keep = [
        jnp.stack([jnp.where(lower_half, kept[i + d], kept[i + d + LOW_TILES])
                   for i in range(LOW_TILES)]) for d in (0, 1)]

    def tiles_of(at):
        def get(a, b, q):
            if (a, b) == (0, 0):
                return l_send[at, q]
            return l_got[at, LOW_AT[a, b] + (0 if abs(a) == 2 else q)]

        return get

    arrived(l_got.at[2], sems.at[3])
    lows = unpack_low(tiles_of(2), in_left, in_right, low_in)
    k2[...] = lows
    west, east = low_rows_beside(lows)
    faces, inverse, diagonal = scaled_faces(
        lows, west, east, pltpu.roll(lows, 1, 2), pltpu.roll(lows, LANES - 1, 2),
        16.0 * z_coupling, keep)
    for side in range(6):
        c2[side, 0] = faces[side]
    i2[...] = inverse
    ones = jnp.where(lows > 0.0, 1.0, 0.0)
    for turn in range(COARSE_SWEEPS):
        ones = (1.0 - relaxation) * ones + low_sum(ones, c2)

    def own_low(values):
        out = []
        for r in range(LOW_HALO, LOW_HALO + OWN2):
            half = HALF if r >= LOW_TILES else 0
            moved = roll_lanes(values[r % LOW_TILES], -half - LOW_LANE)
            out.append(jnp.where(wide_lane < LOW_OWN, moved, 0.0))
        return jnp.stack(out)

    weight[...] = own_low(ones)

    def in_row(values):
        column = jnp.sum(jnp.sum(values, axis=1), axis=1, keepdims=True)
        return jnp.sum(jnp.where(lane == OWN2 * px + sub, column, 0.0), axis=0, keepdims=True)

    one_send[0, 1] = in_row(own_low(diagonal))

    def put_k_rows(first, rows, values):
        k0[0, 1 + first:1 + first + rows] = values * row_in[0 if first < HALO else 1]

    def put_k_beside(i, tile):
        tile = tile * inner_y
        if i < HALO or i >= HALO + ROWS:
            tile = tile * row_in[0 if i < HALO else 1]
        k0[1, 1 + i] = tile

    k0[0, 1 + HALO:1 + HALO + ROWS] = k_own[...]
    arrived(k_got, sems.at[5])
    FOR_K.unpack(k_got, put_k_rows, put_k_beside)

    def restrict(parts):
        total = select_lanes(pair_rows(parts[0]), picked[0])
        return total + select_lanes(pair_rows(parts[1]), picked[1])

    for row, rows in groups(0, FINE, 10):
        k1[0, row // 2 + 1:(row + rows) // 2 + 1] = 0.25 * restrict(
            [k0[t, row + 1:row + rows + 1] for t in (0, 1)])
    for row, rows in groups(THIN, FINE - THIN):
        inverse, diagonal = make_weights(k0, c0, row, rows, z_coupling)
        for t in (0, 1):
            g0[t, row:row + rows] = inverse[t]
            d0[t, row:row + rows] = (1.0 / relaxation) * diagonal[t]
    for row, rows in groups(0, MID, 10):
        inverse, diagonal = make_weights(k1, c1, row, rows, 4.0 * z_coupling)
        i1[0, row:row + rows] = inverse[0]
        d1[0, row:row + rows] = (1.0 / relaxation) * diagonal[0]

    va[0, 1 + HALO:1 + HALO + ROWS] = f_own[...]

    def put_f_rows(first, rows, values):
        va[0, 1 + first:1 + first + rows] = values

    def put_f_beside(i, tile):
        va[1, 1 + i] = tile

    arrived(f_got, sems.at[7])
    FOR_F.unpack(f_got, put_f_rows, put_f_beside)
    for row, rows in groups(THIN, FINE - THIN):
        for t in (0, 1):
            start = g0[t, row:row + rows] * va[t, row + 1:row + rows + 1]
            g0[t, row:row + rows] = start
            va[t, row + 1:row + rows + 1] = start

    def rows_0(halo):
        return HALO - halo, HALO + ROWS + halo

    def rows_1(halo):
        return MID_HALO - halo, MID_HALO + MID_ROWS + halo

    dens = None
    used = 8
    for cycle in range(CYCLES):
        if cycle > 0:
            sweep(va, vb, c0, g0, *rows_0(6))
            sweep(vb, va, c0, g0, *rows_0(6))
            fine, spare = va, vb
        else:
            sweep(va, vb, c0, g0, *rows_0(10))
            fine, spare = vb, va

        for row, rows in groups(*rows_0(4)):
            old, total = weighted(fine, c0, row, rows, (0, 1))
            here = slice(row, row + rows)
            rest = [
                d0[t, here] * (g0[t, here] - relaxation * old[t] + total[t]) for t in (0, 1)]
            half, count = row // 2, rows // 2
            start = i1[0, half:half + count] * restrict(rest)
            g1[0, half:half + count] = start
            ua[0, half + 1:half + count + 1] = start
        sweep(ua, ub, c1, g1, *rows_1(2))
        for part in (0, 1):
            row = MID_HALO + 8 * part
            old, total = weighted(ub, c1, row, 8, (0,))
            rest = d1[0, row:row + 8] * (
                g1[0, row:row + 8] - relaxation * old[0] + total[0])
            l_own[4 * part:4 * part + 4] = select_lanes(pair_rows(rest), picked[4])

        one_send[cycle, 0] = in_row(weight[...] * l_own[...])
        wide = 2 if cycle == 0 else 1
        one_out, one_in = one_send.at[cycle, pl.ds(0, wide)], one_got.at[cycle, :, pl.ds(0, wide)]
        two_out, two_in = two_send.at[cycle, pl.ds(0, wide)], two_got.at[cycle, :, pl.ds(0, wide)]
        spread(one_out, one_in, used, to_y)
        for q in (0, 1):
            l_send[cycle, q] = pack_low([l_own[4 * q + m] for m in range(4)])
        start_low(l_send.at[cycle], l_got.at[cycle], sems.at[used + 2], sems.at[used + 3], near)
        mids_out, mids_in = (m_send, m_got) if cycle == 0 else (n_send, n_got)
        for j, tile in enumerate(pack_mid(ub[0, 1 + MID_HALO:1 + MID_HALO + MID_ROWS])):
            mids_out[j, 0] = tile
        if cycle == 0:
            for j, tile in enumerate(pack_mid(g1[0, MID_HALO:MID_HALO + MID_ROWS])):
                mids_out[j, 1] = tile
        start_mid(mids_out, mids_in, sems.at[used + 6], sems.at[used + 7], near)
        arrived(one_in, sems.at[used + 1])
        for part in range(wide):
            two_send[cycle, part] = one_send[cycle, part] + jnp.sum(one_got[cycle, :, part], axis=0)
        spread(two_out, two_in, used + 4, to_x)

        arrived(l_got.at[cycle], sems.at[used + 3])
        right = i2[...] * unpack_low(tiles_of(cycle), None, None, None)
        low = right
        for turn in range(COARSE_SWEEPS - 1):
            low = right + (1.0 - relaxation) * low + low_sum(low, c2)
        def put_u(row, a, own, tile):
            tile = jnp.where(own, ub[0, 1 + row], tile) if a == 0 else tile
            ub[0, 1 + row] = jnp.where(k1[0, 1 + row] > 0.0, tile, 0.0)

        def put_g(row, a, own, tile):
            tile = jnp.where(own, g1[0, row], tile) if a == 0 else tile
            g1[0, row] = jnp.where(k1[0, 1 + row] > 0.0, tile, 0.0)

        arrived(mids_in, sems.at[used + 7])
        unpack_mid(mids_in, 0, put_u)
        if cycle == 0:
            unpack_mid(mids_in, 1, put_g)

        arrived(two_in, sems.at[used + 5])
        parts = []
        for part in range(wide):
            both = two_send[cycle, part] + jnp.sum(two_got[cycle, :, part], axis=0)
            row_sums = jnp.broadcast_to(both, (8, LANES))
            parts.append([jnp.sum(pick[tile] * row_sums, axis=1, keepdims=True) for tile in (0, 1)])
        if cycle == 0:
            dens = parts[1]
        for tile in (0, 1):
            shift = jnp.broadcast_to(parts[0][tile] / dens[tile], (8, LANES))
            for i in range(8):
                shifts[8 * tile + i] = jnp.broadcast_to(shift[i:i + 1], (NZ, LANES))

        for part in (0, 1):
            tiles = slice(LOW_TILES - 8, LOW_TILES) if part == 0 else slice(0, 8)
            moved = jnp.where(k2[tiles] > 0.0, shifts[8 * part:8 * part + 8], 0.0)
            wave = twice_rows(select_lanes(low[tiles] + moved, picked[5 + part]))
            at, count = (1, MID // 2) if part == 0 else (1 + MID // 2, MID // 2)
            ua[0, at:at + count] = ub[0, at:at + count] + (wave[1:] if part == 0 else wave[:-1])
        around = rows_1(6 if cycle == 0 else 2)
        sweep(ua, ub, c1, g1, *around)
        sweep(ub, ua, c1, g1, *around)

        for row, rows in groups(*rows_0(10 if cycle == 0 else 2)):
            wave = ua[0, row // 2 + 1:(row + rows) // 2 + 1]
            here = slice(row + 1, row + rows + 1)
            for t in (0, 1):
                spare[t, here] = fine[t, here] + twice_rows(select_lanes(wave, picked[2 + t]))
        if cycle < CYCLES - 1:
            sweep(spare, fine, c0, g0, *rows_0(8))
            sweep(fine, spare, c0, g0, *rows_0(8))
        else:
            sweep(spare, fine, c0, g0, *rows_0(1))
            for row, rows in groups(*rows_0(0)):
                old, total = weighted(fine, c0, row, rows, (0,))
                s_own[row - HALO:row - HALO + rows] = (
                    g0[0, row:row + rows] + (1.0 - relaxation) * old[0] + total[0])
        used += 8

    for r in range(ROWS):
        out_ref[pl.ds(r, NZ, stride=ROWS), :] = s_own[r]

    arrived(l_got.at[2], sems.at[2])
    arrived(k_got, sems.at[4])
    arrived(f_got, sems.at[6])
    arrived(m_got, sems.at[14])
    arrived(n_got, sems.at[22])
    for cycle, at in ((0, 8), (1, 16)):
        wide = pl.ds(0, 2 - cycle)
        arrived(one_got.at[cycle, :, wide], sems.at[at])
        arrived(l_got.at[cycle], sems.at[at + 2])
        arrived(two_got.at[cycle, :, wide], sems.at[at + 4])


def vmem(*shape):
    return pltpu.VMEM(shape + (NZ, LANES), jnp.float32)


def shards(source, coefficient, strip_rows):
    size_x, size_y = lax.axis_size("px"), lax.axis_size("py")
    flat = (NZ * ROWS, LANES)
    scratch = [pltpu.SMEM(strip_rows.shape, jnp.int32)] + [pltpu.VMEM(flat, jnp.float32)] * 2
    scratch += [vmem(ROWS), vmem(ROWS), vmem(ROWS), vmem(2, 4), vmem(2, 4)]
    scratch += [vmem(e.at[8]) for e in (FOR_K, FOR_F)]
    scratch += [vmem(2, FINE + 2), vmem(6, 2, FINE), vmem(2, FINE), vmem(2, FINE)]
    scratch += [vmem(2, FINE + 2), vmem(2, FINE + 2)]
    scratch += [vmem(1, MID + 2), vmem(6, 1, MID), vmem(1, MID), vmem(1, MID), vmem(1, MID)]
    scratch += [vmem(1, MID + 2), vmem(1, MID + 2)]
    scratch += [vmem(LOW_TILES), vmem(6, 1, LOW_TILES), vmem(LOW_TILES)]
    scratch += [vmem(OWN2), vmem(16), vmem(2), vmem(OWN2), vmem(3, 2), vmem(3, LOW_COUNT)]
    scratch += [vmem(MID_ROWS // 2, 2), vmem(MID_TILES, 2), vmem(MID_ROWS // 2, 1), vmem(MID_TILES, 1)]
    row = lambda *shape: pltpu.VMEM(shape + (1, LANES), jnp.float32)
    scratch += [row(2, 2), row(2, size_y - 1, 2), row(2, 2), row(2, size_x - 1, 2)]
    scratch += [pltpu.VMEM((8, LANES, LANES), jnp.float32), pltpu.SemaphoreType.DMA((27,))]
    hbm = pl.BlockSpec(memory_space=pltpu.HBM)
    done = pl.pallas_call(
        kernel,
        out_shape=pltpu.VMEM(flat, jnp.float32),
        in_specs=[hbm, hbm, hbm],
        out_specs=pl.BlockSpec(memory_space=pltpu.VMEM),
        scratch_shapes=scratch,
        compiler_params=pltpu.CompilerParams(
            collective_id=0, has_side_effects=True, vmem_limit_bytes=60 << 20
        ),
        name="cycles",
    )(strip_rows, source.reshape(flat), coefficient.reshape(flat))
    return done.reshape(source.shape)


def solution(mesh):
    placed = (P(None, "px", "py"), P(None, "px", "py"), P())
    return jax.shard_map(
        shards, mesh=mesh, in_specs=placed, out_specs=P(None, "px", "py"), check_vma=False
    )
```

```python
import jax
import jax.numpy as jnp
from jax import lax
from jax.experimental import pallas as pl
from jax.experimental.pallas import tpu as pltpu
from jax.sharding import PartitionSpec as P

CYCLES = 2
COARSE_SWEEPS = 6
relaxation = 0.8
z_coupling = 0.25

MESH = pl.DeviceIdType.MESH

NZ = 8
ROWS = 32
LANES = 128
EDGE = 16
HALO = 14
FINE = ROWS + 2 * HALO
MID = FINE // 2
OWN2 = ROWS // 4
LOW_HALO = 10
LOW_TILES = (OWN2 + 2 * LOW_HALO) // 2
MID_LANE, MID_OWN = 32, 64
LOW_LANE, LOW_OWN, HALF = LOW_HALO, 32, 64
MID_HALO, MID_ROWS = HALO // 2, ROWS // 2


def lanes_of(rows):
    return lax.broadcasted_iota(jnp.int32, (rows, NZ, LANES), 2)


def layers_of(rows):
    return lax.broadcasted_iota(jnp.int32, (rows, NZ, LANES), 1)


def beside_lanes(parts, tiles):
    back = [pltpu.roll(part, 1, 2) for part in parts]
    ahead = [pltpu.roll(part, LANES - 1, 2) for part in parts]
    if len(parts) == 1:
        return back, ahead
    lane = lanes_of(parts[0].shape[0])
    before, after = lane < 1, lane >= LANES - 1
    south = [jnp.where(before, back[1 - t], back[t]) for t in tiles]
    north = [jnp.where(after, ahead[1 - t], ahead[t]) for t in tiles]
    return south, north


def six_sum(weights, t, here, west, own, east, south, north):
    total = weights[0, t, here] * west + weights[1, t, here] * east
    total += weights[4, t, here] * pltpu.roll(own, 1, 1)
    total += weights[5, t, here] * pltpu.roll(own, NZ - 1, 1)
    total += weights[2, t, here] * south
    total += weights[3, t, here] * north
    return total


def weighted(values, weights, row, rows, tiles):
    parts = [values[t, row + 1:row + 1 + rows] for t in range(values.shape[0])]
    south, north = beside_lanes(parts, tiles)
    totals = []
    for at, t in enumerate(tiles):
        west, east = values[t, row:row + rows], values[t, row + 2:row + 2 + rows]
        totals.append(six_sum(weights, t, slice(row, row + rows), west, parts[t], east,
                              south[at], north[at]))
    return [parts[t] for t in tiles], totals


def groups(first, end, rows=8):
    return [(row, min(rows, end - row)) for row in range(first, end, rows)]


def sweep(values, new, weights, right, first, end):
    tiles = range(values.shape[0])
    for row, rows in groups(first, end):
        old, total = weighted(values, weights, row, rows, tiles)
        for t in tiles:
            new[t, row + 1:row + 1 + rows] = (
                right[t, row:row + rows] + (1.0 - relaxation) * old[t] + total[t])


def scaled_faces(own, west, east, south, north, z_factor, keep=None):
    layer = layers_of(own.shape[0])
    half_z = 0.5 * z_factor
    faces = [
        0.5 * (own + west), 0.5 * (own + east), 0.5 * (own + south), 0.5 * (own + north),
        jnp.where(layer > 0, half_z * (own + pltpu.roll(own, 1, 1)), 0.0),
        jnp.where(layer < NZ - 1, half_z * (own + pltpu.roll(own, NZ - 1, 1)), 0.0),
    ]
    diagonal = faces[0] + faces[1] + faces[2] + faces[3] + faces[4] + faces[5]
    inside = own > 0.0
    inverse = jnp.where(inside, relaxation / jnp.where(inside, diagonal, 1.0), 0.0)
    if keep is not None:
        faces[0], faces[1] = faces[0] * keep[0], faces[1] * keep[1]
    return [inverse * face for face in faces], inverse, diagonal


def make_weights(conduct, weights, row, rows, z_factor):
    tiles = range(conduct.shape[0])
    parts = [conduct[t, row + 1:row + 1 + rows] for t in tiles]
    south, north = beside_lanes(parts, tiles)
    inverses, diagonals = [], []
    for t in tiles:
        west, east = conduct[t, row:row + rows], conduct[t, row + 2:row + 2 + rows]
        faces, inverse, diagonal = scaled_faces(
            parts[t], west, east, south[t], north[t], z_factor)
        for side in range(6):
            weights[side, t, row:row + rows] = faces[side]
        inverses.append(inverse)
        diagonals.append(diagonal)
    return inverses, diagonals


def low_rows_beside(values):
    first = pltpu.roll(values[LOW_TILES - 1:], HALF, 2)
    last = pltpu.roll(values[:1], HALF, 2)
    west = jnp.concatenate([first, values[:-1]], axis=0)
    east = jnp.concatenate([values[1:], last], axis=0)
    return west, east


def low_sum(values, weights):
    west, east = low_rows_beside(values)
    back, ahead = pltpu.roll(values, 1, 2), pltpu.roll(values, LANES - 1, 2)
    return six_sum(weights, 0, slice(0, LOW_TILES), west, values, east, back, ahead)


def pair_rows(values):
    rows = values.shape[0]
    return jnp.sum(values.reshape(rows // 2, 2, NZ, LANES), axis=1)


def twice_rows(values):
    rows = values.shape[0]
    wide = jnp.broadcast_to(values[:, None], (rows, 2, NZ, LANES))
    return wide.reshape(2 * rows, NZ, LANES)


def select_lanes(values, chosen):
    rows = values.shape[0]
    flat = jnp.dot(
        values.reshape(rows * NZ, LANES), chosen, precision=lax.Precision.HIGHEST,
        preferred_element_type=jnp.float32)
    return flat.reshape(rows, NZ, LANES)


def roll_lanes(tile, amount):
    amount = amount % LANES
    return tile if amount == 0 else pltpu.roll(tile, amount, 1)


def pack_edges(block, group, right_side):
    lane = lax.broadcasted_iota(jnp.int32, (NZ, LANES), 1)
    packed = None
    for j in range(8):
        moved = roll_lanes(block[8 * group + j], EDGE * j + (EDGE if right_side else 0))
        packed = moved if packed is None else jnp.where(lane // EDGE == j, moved, packed)
    return packed


def unpack_edges(left, right, j):
    lane = lax.broadcasted_iota(jnp.int32, (NZ, LANES), 1)
    from_right = roll_lanes(right, -EDGE * j)
    from_left = roll_lanes(left, -EDGE * (j + 1))
    return jnp.where(lane < EDGE, from_right, jnp.where(lane >= LANES - EDGE, from_left, 0.0))


def pack_low(rows):
    out = rows[0]
    for m in range(1, 4):
        out = out + roll_lanes(rows[m], LOW_OWN * m)
    return out


def unpack_low(get, scale_left, scale_right, scale_rows):
    lane = lax.broadcasted_iota(jnp.int32, (NZ, LANES), 1)
    rows = []
    far = LOW_HALO - OWN2
    parts = [(-2, 1, range(4 - far, 4)), (2, 0, range(far))]
    parts[1:1] = [(a, q, range(4)) for a in (-1, 0, 1) for q in (0, 1)]
    for a, q, members in parts:
        own = get(a, 0, q)
        left, right = roll_lanes(get(a, -1, q), -LOW_OWN), roll_lanes(get(a, 1, q), LOW_OWN)
        if scale_left is not None:
            left, right = left * scale_left, right * scale_right
        if scale_rows is not None and a != 0:
            scale = scale_rows[a]
            own, left, right = own * scale, left * scale, right * scale
        for m in members:
            row = len(rows)
            away = (lane - LOW_OWN * m) % LANES
            tile = jnp.where(
                away < LOW_OWN, own,
                jnp.where(away < LOW_OWN + LOW_LANE, right,
                          jnp.where(away >= LANES - LOW_LANE, left, 0.0)))
            half = HALF if row >= LOW_TILES else 0
            rows.append(roll_lanes(tile, half + LOW_LANE - LOW_OWN * m))
    return jnp.stack([rows[i] + rows[i + LOW_TILES] for i in range(LOW_TILES)])


def pack_mid(rows):
    lane = lax.broadcasted_iota(jnp.int32, (NZ, LANES), 1)
    return [
        jnp.where(lane < HALF, roll_lanes(rows[2 * j], -MID_LANE),
                  roll_lanes(rows[2 * j + 1], MID_LANE)) for j in range(MID_ROWS // 2)]


MID_AT, MID_TILES = {}, 0
for side in [(a, b) for a in (-1, 0, 1) for b in (-1, 0, 1) if (a, b) != (0, 0)]:
    MID_AT[side] = MID_TILES
    MID_TILES += MID_ROWS // 2 if side[0] == 0 else MID_ROWS // 4


LOW_AT, LOW_COUNT = {}, 0
for side in [(a, b) for a in (-2, 2, -1, 1, 0) for b in (-1, 1, 0) if (a, b) != (0, 0)]:
    LOW_AT[side] = LOW_COUNT
    LOW_COUNT += 1 if abs(side[0]) == 2 else 2


def start_low(send, got, send_sem, got_sem, near):
    for (a, b), at in LOW_AT.items():
        tiles, first = (1, 1 if a < 0 else 0) if abs(a) == 2 else (2, 0)
        pltpu.make_async_remote_copy(
            src_ref=send.at[pl.ds(first, tiles)],
            dst_ref=got.at[pl.ds(at, tiles)],
            send_sem=send_sem,
            recv_sem=got_sem,
            device_id=near(-a, -b),
            device_id_type=MESH,
        ).start()


def start_mid(send, got, send_sem, got_sem, near):
    for a, b in AROUND:
        count = MID_ROWS // 2 if a == 0 else MID_ROWS // 4
        pltpu.make_async_remote_copy(
            src_ref=send.at[pl.ds(MID_ROWS // 4 if a < 0 else 0, count)],
            dst_ref=got.at[pl.ds(MID_AT[a, b], count)],
            send_sem=send_sem,
            recv_sem=got_sem,
            device_id=near(-a, -b),
            device_id_type=MESH,
        ).start()


def unpack_mid(got, which, put):
    lane = lax.broadcasted_iota(jnp.int32, (NZ, LANES), 1)
    own = (lane >= MID_LANE) & (lane < MID_LANE + MID_OWN)
    for row in range(MID):
        a = -1 if row < MID_HALO else 0 if row < MID_HALO + MID_ROWS else 1
        source = row - MID_HALO - MID_ROWS * a
        tile, half = divmod(source - (MID_ROWS // 2 if a < 0 else 0), 2)
        turn = MID_LANE if half == 0 else -MID_LANE
        left, right = got[MID_AT[a, -1] + tile, which], got[MID_AT[a, 1] + tile, which]
        beside = roll_lanes(jnp.where(lane % HALF < MID_LANE, right, left), -turn)
        if a != 0:
            beside = jnp.where(own, roll_lanes(got[MID_AT[a, 0] + tile, which], turn), beside)
        put(row, a, own, beside)


class Exchange:
    def __init__(self, depth):
        self.depth = depth
        sizes = [depth] * 2 + [4] * 2 + [2] * 4
        self.at = [sum(sizes[:i]) for i in range(9)]

    def stage(self, edges, block):
        for side in (0, 1):
            for group in range(4):
                edges[side, group] = pack_edges(block, group, side == 1)

    def start(self, block, edges, got, send_sem, got_sem, near):
        n, at = self.depth, self.at
        top, bottom = pl.ds(0, 2), pl.ds(2, 2)
        moves = [
            (block.at[pl.ds(ROWS - n, n)], 0, (1, 0)),
            (block.at[pl.ds(0, n)], 1, (-1, 0)),
            (edges.at[1], 2, (0, 1)),
            (edges.at[0], 3, (0, -1)),
            (edges.at[1, bottom], 4, (1, 1)),
            (edges.at[0, bottom], 5, (1, -1)),
            (edges.at[1, top], 6, (-1, 1)),
            (edges.at[0, top], 7, (-1, -1)),
        ]
        for source, slot, way in moves[4:] + moves[:4]:
            pltpu.make_async_remote_copy(
                src_ref=source,
                dst_ref=got.at[pl.ds(at[slot], at[slot + 1] - at[slot])],
                send_sem=send_sem,
                recv_sem=got_sem,
                device_id=near(*way),
                device_id_type=MESH,
            ).start()

    def unpack(self, got, put_rows, put_beside):
        n, at = self.depth, self.at
        put_rows(HALO - n, n, got[at[0]:at[0] + n])
        put_rows(HALO + ROWS, n, got[at[1]:at[1] + n])
        for i in range(FINE):
            if i < HALO:
                source = ROWS - HALO + i
                offset = at[4] - 2, at[5] - 2
            elif i < HALO + ROWS:
                source = i - HALO
                offset = at[2], at[3]
            else:
                source = i - HALO - ROWS
                offset = at[6], at[7]
            group, j = divmod(source, 8)
            put_beside(i, unpack_edges(got[offset[0] + group], got[offset[1] + group], j))


AROUND = [(a, b) for a in (-1, 1) for b in (-1, 1)] + [(-1, 0), (1, 0), (0, -1), (0, 1)]
FOR_K, FOR_F = Exchange(HALO), Exchange(HALO - 4)
THIN = HALO - FOR_F.depth


def kernel(strip_hbm, source_ref, coefficient_ref, out_ref,
           strip_ref, k_in, f_in, k_own, f_own, k_edge, f_edge, k_got, f_got,
           k0, c0, g0, d0, va, vb, k1, c1, i1, g1, d1, ua, ub, k2, c2, i2,
           weight, shifts, pick, l_own, l_send, l_got, m_send, m_got, n_send, n_got, one_send, one_got, two_send, two_got,
           picked, sems):
    px, py = lax.axis_index("px"), lax.axis_index("py")
    size_x, size_y = lax.axis_size("px"), lax.axis_size("py")
    strips = strip_ref.shape[0]

    def near(a, b):
        return (lax.rem(px + a + size_x, size_x), lax.rem(py + b + size_y, size_y))

    k_copy = pltpu.make_async_copy(coefficient_ref, k_in, sems.at[0])
    f_copy = pltpu.make_async_copy(source_ref, f_in, sems.at[1])
    strip_copy = pltpu.make_async_copy(strip_hbm, strip_ref, sems.at[26])
    k_copy.start()
    strip_copy.start()
    f_copy.start()
    def around_ring(offset, size):
        return min(offset % size, -offset % size)

    along_y = sorted(range(1, size_y), key=lambda b: -around_ring(b, size_y))
    along_x = sorted(
        range(1, size_x),
        key=lambda a: -around_ring(a % 4, 4) - around_ring((a + 1) // 4, size_x // 4))
    to_y, to_x = [(0, b) for b in along_y], [(a, 0) for a in along_x]
    peers = [(a, b) for a in (-2, 2) for b in (-1, 1)] + to_y + to_x
    peers += [way for way in AROUND if way[0] and way[1]]
    barrier = pltpu.get_barrier_semaphore()
    for way in peers:
        pl.semaphore_signal(barrier, inc=1, device_id=near(*way), device_id_type=MESH)

    def arrived(buffer, sem):
        pltpu.make_async_copy(buffer, buffer, sem).wait()

    def spread(source, got, sem, ways):
        for slot, way in enumerate(ways):
            pltpu.make_async_remote_copy(
                src_ref=source,
                dst_ref=got.at[slot],
                send_sem=sems.at[sem],
                recv_sem=sems.at[sem + 1],
                device_id=near(*way),
                device_id_type=MESH,
            ).start()

    one = lax.broadcasted_iota(jnp.int32, (LANES, LANES), 0)
    other = lax.broadcasted_iota(jnp.int32, (LANES, LANES), 1)

    def chosen(condition):
        return jnp.where(condition, 1.0, 0.0)

    def beside_pairs(wide, narrow):
        nearby = (wide < EDGE) & (narrow == MID_LANE + MID_OWN + wide // 2)
        return nearby | ((wide >= LANES - EDGE) & (narrow == MID_LANE - LANES // 2 + wide // 2))

    def low_of(mid, half):
        return half + LOW_LANE - MID_LANE // 2 + mid // 2

    mid_halo = EDGE
    mid_in = (other >= MID_LANE - mid_halo) & (other < MID_LANE + MID_OWN + mid_halo)
    tables = [
        chosen(other == MID_LANE + one // 2), chosen(beside_pairs(one, other)),
        chosen(one == MID_LANE + other // 2), chosen(beside_pairs(other, one)),
        chosen((one >= MID_LANE) & (one < MID_LANE + MID_OWN)
               & (other == (one - MID_LANE) // 2)),
        chosen(mid_in & (one == low_of(other, 0))), chosen(mid_in & (one == low_of(other, HALF))),
        chosen(other == one // 4),
    ]
    for at, table in enumerate(tables):
        picked[at] = table

    strip_copy.wait()
    ends, total = [], jnp.int32(0)
    for c in range(strips):
        total = total + strip_ref[c]
        ends.append(total)
    sub = lax.broadcasted_iota(jnp.int32, (8, LANES), 0)
    lane = lax.broadcasted_iota(jnp.int32, (8, LANES), 1)

    def strip_of(rows):
        found = jnp.zeros_like(rows)
        for end in ends:
            found = found + jnp.where(rows >= end, 1, 0)
        return found

    lane_strip = strip_of(lane)
    for tile in (0, 1):
        rows = jnp.clip(OWN2 * px - 4 + 8 * tile + sub, 0, OWN2 * size_x - 1)
        pick[tile] = jnp.where(strip_of(rows) == lane_strip, 1.0, 0.0)

    zero = jnp.zeros((NZ, LANES), jnp.float32)
    for ref, end in ((k0, FINE), (va, FINE), (vb, FINE), (k1, MID), (ua, MID), (ub, MID)):
        for t in range(ref.shape[0]):
            ref[t, 0] = zero
            ref[t, end + 1] = zero
    for i in range(THIN):
        va[0, 1 + i] = zero
        va[0, FINE - i] = zero
    for i in range(MID):
        ua[0, 1 + i] = zero

    k_copy.wait()
    for r in range(ROWS):
        k_own[r] = k_in[pl.ds(r, NZ, stride=ROWS), :]
    lows = (1.0 / 16.0) * select_lanes(pair_rows(pair_rows(k_own[...])), picked[7])
    for q in (0, 1):
        l_send[2, q] = pack_low([lows[4 * q + m] for m in range(4)])
    FOR_K.stage(k_edge, k_own)
    f_copy.wait()
    for r in range(ROWS):
        f_own[r] = f_in[pl.ds(r, NZ, stride=ROWS), :]
    FOR_F.stage(f_edge, f_own)
    pl.semaphore_wait(barrier, len(peers))
    start_low(l_send.at[2], l_got.at[2], sems.at[2], sems.at[3], near)
    FOR_K.start(k_own, k_edge, k_got, sems.at[4], sems.at[5], near)
    FOR_F.start(f_own, f_edge, f_got, sems.at[6], sems.at[7], near)

    wide_lane = lax.broadcasted_iota(jnp.int32, (NZ, LANES), 1)
    in_left, in_right = jnp.where(py > 0, 1.0, 0.0), jnp.where(py < size_y - 1, 1.0, 0.0)
    inner_y = jnp.where(wide_lane < LANES // 2, in_right, in_left)
    row_in = [jnp.where(px > 0, 1.0, 0.0), jnp.where(px < size_x - 1, 1.0, 0.0)]
    low_in = {-1: row_in[0], 1: row_in[1], -2: jnp.where(px > 1, 1.0, 0.0),
              2: jnp.where(px < size_x - 2, 1.0, 0.0)}

    kept = []
    for tile in range(4):
        rows = OWN2 * px - LOW_HALO + 8 * tile + sub
        flags = jnp.ones((8, LANES), jnp.float32)
        for end in ends:
            flags = jnp.where(rows == end, 0.0, flags)
        kept += [jnp.broadcast_to(flags[i:i + 1], (NZ, LANES)) for i in range(8)]
    lower_half = wide_lane < HALF
    keep = [
        jnp.stack([jnp.where(lower_half, kept[i + d], kept[i + d + LOW_TILES])
                   for i in range(LOW_TILES)]) for d in (0, 1)]

    def tiles_of(at):
        def get(a, b, q):
            if (a, b) == (0, 0):
                return l_send[at, q]
            return l_got[at, LOW_AT[a, b] + (0 if abs(a) == 2 else q)]

        return get

    arrived(l_got.at[2], sems.at[3])
    lows = unpack_low(tiles_of(2), in_left, in_right, low_in)
    k2[...] = lows
    west, east = low_rows_beside(lows)
    faces, inverse, diagonal = scaled_faces(
        lows, west, east, pltpu.roll(lows, 1, 2), pltpu.roll(lows, LANES - 1, 2),
        16.0 * z_coupling, keep)
    for side in range(6):
        c2[side, 0] = faces[side]
    i2[...] = inverse
    ones = jnp.where(lows > 0.0, 1.0, 0.0)
    def own_low(values):
        out = []
        for r in range(LOW_HALO, LOW_HALO + OWN2):
            half = HALF if r >= LOW_TILES else 0
            moved = roll_lanes(values[r % LOW_TILES], -half - LOW_LANE)
            out.append(jnp.where(wide_lane < LOW_OWN, moved, 0.0))
        return jnp.stack(out)

    def in_row(values):
        column = jnp.sum(jnp.sum(values, axis=1), axis=1, keepdims=True)
        return jnp.sum(jnp.where(lane == OWN2 * px + sub, column, 0.0), axis=0, keepdims=True)

    one_send[0, 1] = in_row(own_low(diagonal))

    def put_k_rows(first, rows, values):
        k0[0, 1 + first:1 + first + rows] = values * row_in[0 if first < HALO else 1]

    def put_k_beside(i, tile):
        tile = tile * inner_y
        if i < HALO or i >= HALO + ROWS:
            tile = tile * row_in[0 if i < HALO else 1]
        k0[1, 1 + i] = tile

    k0[0, 1 + HALO:1 + HALO + ROWS] = k_own[...]
    arrived(k_got, sems.at[5])
    FOR_K.unpack(k_got, put_k_rows, put_k_beside)

    def restrict(parts):
        total = select_lanes(pair_rows(parts[0]), picked[0])
        return total + select_lanes(pair_rows(parts[1]), picked[1])

    for row, rows in groups(0, FINE, 10):
        k1[0, row // 2 + 1:(row + rows) // 2 + 1] = 0.25 * restrict(
            [k0[t, row + 1:row + rows + 1] for t in (0, 1)])
    turns = COARSE_SWEEPS
    for row, rows in groups(THIN, FINE - THIN):
        if turns > 0:
            ones = (1.0 - relaxation) * ones + low_sum(ones, c2)
            turns -= 1
        inverse, diagonal = make_weights(k0, c0, row, rows, z_coupling)
        for t in (0, 1):
            g0[t, row:row + rows] = inverse[t]
            d0[t, row:row + rows] = (1.0 / relaxation) * diagonal[t]
    weight[...] = own_low(ones)
    for row, rows in groups(0, MID, 10):
        inverse, diagonal = make_weights(k1, c1, row, rows, 4.0 * z_coupling)
        i1[0, row:row + rows] = inverse[0]
        d1[0, row:row + rows] = (1.0 / relaxation) * diagonal[0]

    va[0, 1 + HALO:1 + HALO + ROWS] = f_own[...]

    def put_f_rows(first, rows, values):
        va[0, 1 + first:1 + first + rows] = values

    def put_f_beside(i, tile):
        va[1, 1 + i] = tile

    arrived(f_got, sems.at[7])
    FOR_F.unpack(f_got, put_f_rows, put_f_beside)
    for row, rows in groups(THIN, FINE - THIN):
        for t in (0, 1):
            start = g0[t, row:row + rows] * va[t, row + 1:row + rows + 1]
            g0[t, row:row + rows] = start
            va[t, row + 1:row + rows + 1] = start

    def rows_0(halo):
        return HALO - halo, HALO + ROWS + halo

    def rows_1(halo):
        return MID_HALO - halo, MID_HALO + MID_ROWS + halo

    dens = None
    used = 8
    for cycle in range(CYCLES):
        if cycle > 0:
            sweep(va, vb, c0, g0, *rows_0(6))
            sweep(vb, va, c0, g0, *rows_0(6))
            fine, spare = va, vb
        else:
            sweep(va, vb, c0, g0, *rows_0(10))
            fine, spare = vb, va

        for row, rows in groups(*rows_0(4)):
            old, total = weighted(fine, c0, row, rows, (0, 1))
            here = slice(row, row + rows)
            rest = [
                d0[t, here] * (g0[t, here] - relaxation * old[t] + total[t]) for t in (0, 1)]
            half, count = row // 2, rows // 2
            start = i1[0, half:half + count] * restrict(rest)
            g1[0, half:half + count] = start
            ua[0, half + 1:half + count + 1] = start
        sweep(ua, ub, c1, g1, *rows_1(2))
        for part in (0, 1):
            row = MID_HALO + 8 * part
            old, total = weighted(ub, c1, row, 8, (0,))
            rest = d1[0, row:row + 8] * (
                g1[0, row:row + 8] - relaxation * old[0] + total[0])
            l_own[4 * part:4 * part + 4] = select_lanes(pair_rows(rest), picked[4])

        one_send[cycle, 0] = in_row(weight[...] * l_own[...])
        wide = 2 if cycle == 0 else 1
        one_out, one_in = one_send.at[cycle, pl.ds(0, wide)], one_got.at[cycle, :, pl.ds(0, wide)]
        two_out, two_in = two_send.at[cycle, pl.ds(0, wide)], two_got.at[cycle, :, pl.ds(0, wide)]
        spread(one_out, one_in, used, to_y)
        for q in (0, 1):
            l_send[cycle, q] = pack_low([l_own[4 * q + m] for m in range(4)])
        start_low(l_send.at[cycle], l_got.at[cycle], sems.at[used + 2], sems.at[used + 3], near)
        mids_out, mids_in = (m_send, m_got) if cycle == 0 else (n_send, n_got)
        for j, tile in enumerate(pack_mid(ub[0, 1 + MID_HALO:1 + MID_HALO + MID_ROWS])):
            mids_out[j, 0] = tile
        if cycle == 0:
            for j, tile in enumerate(pack_mid(g1[0, MID_HALO:MID_HALO + MID_ROWS])):
                mids_out[j, 1] = tile
        start_mid(mids_out, mids_in, sems.at[used + 6], sems.at[used + 7], near)
        arrived(one_in, sems.at[used + 1])
        for part in range(wide):
            two_send[cycle, part] = one_send[cycle, part] + jnp.sum(one_got[cycle, :, part], axis=0)
        spread(two_out, two_in, used + 4, to_x)

        arrived(l_got.at[cycle], sems.at[used + 3])
        right = i2[...] * unpack_low(tiles_of(cycle), None, None, None)
        low = right
        for turn in range(COARSE_SWEEPS - 1):
            low = right + (1.0 - relaxation) * low + low_sum(low, c2)
        def put_u(row, a, own, tile):
            tile = jnp.where(own, ub[0, 1 + row], tile) if a == 0 else tile
            ub[0, 1 + row] = jnp.where(k1[0, 1 + row] > 0.0, tile, 0.0)

        def put_g(row, a, own, tile):
            tile = jnp.where(own, g1[0, row], tile) if a == 0 else tile
            g1[0, row] = jnp.where(k1[0, 1 + row] > 0.0, tile, 0.0)

        arrived(mids_in, sems.at[used + 7])
        unpack_mid(mids_in, 0, put_u)
        if cycle == 0:
            unpack_mid(mids_in, 1, put_g)

        arrived(two_in, sems.at[used + 5])
        parts = []
        for part in range(wide):
            both = two_send[cycle, part] + jnp.sum(two_got[cycle, :, part], axis=0)
            row_sums = jnp.broadcast_to(both, (8, LANES))
            parts.append([jnp.sum(pick[tile] * row_sums, axis=1, keepdims=True) for tile in (0, 1)])
        if cycle == 0:
            dens = parts[1]
        for tile in (0, 1):
            shift = jnp.broadcast_to(parts[0][tile] / dens[tile], (8, LANES))
            for i in range(8):
                shifts[8 * tile + i] = jnp.broadcast_to(shift[i:i + 1], (NZ, LANES))

        for part in (0, 1):
            tiles = slice(LOW_TILES - 8, LOW_TILES) if part == 0 else slice(0, 8)
            moved = jnp.where(k2[tiles] > 0.0, shifts[8 * part:8 * part + 8], 0.0)
            wave = twice_rows(select_lanes(low[tiles] + moved, picked[5 + part]))
            at, count = (1, MID // 2) if part == 0 else (1 + MID // 2, MID // 2)
            ua[0, at:at + count] = ub[0, at:at + count] + (wave[1:] if part == 0 else wave[:-1])
        around = rows_1(6 if cycle == 0 else 2)
        sweep(ua, ub, c1, g1, *around)
        sweep(ub, ua, c1, g1, *around)

        for row, rows in groups(*rows_0(10 if cycle == 0 else 2)):
            wave = ua[0, row // 2 + 1:(row + rows) // 2 + 1]
            here = slice(row + 1, row + rows + 1)
            for t in (0, 1):
                spare[t, here] = fine[t, here] + twice_rows(select_lanes(wave, picked[2 + t]))
        if cycle < CYCLES - 1:
            sweep(spare, fine, c0, g0, *rows_0(8))
            sweep(fine, spare, c0, g0, *rows_0(8))
        else:
            sweep(spare, fine, c0, g0, *rows_0(1))
            for row, rows in groups(*rows_0(0)):
                old, total = weighted(fine, c0, row, rows, (0,))
                done = g0[0, row:row + rows] + (1.0 - relaxation) * old[0] + total[0]
                for r in range(rows):
                    out_ref[pl.ds(row - HALO + r, NZ, stride=ROWS), :] = done[r]
        used += 8

    arrived(l_got.at[2], sems.at[2])
    arrived(k_got, sems.at[4])
    arrived(f_got, sems.at[6])
    arrived(m_got, sems.at[14])
    arrived(n_got, sems.at[22])
    for cycle, at in ((0, 8), (1, 16)):
        wide = pl.ds(0, 2 - cycle)
        arrived(one_got.at[cycle, :, wide], sems.at[at])
        arrived(l_got.at[cycle], sems.at[at + 2])
        arrived(two_got.at[cycle, :, wide], sems.at[at + 4])


def vmem(*shape):
    return pltpu.VMEM(shape + (NZ, LANES), jnp.float32)


def shards(source, coefficient, strip_rows):
    size_x, size_y = lax.axis_size("px"), lax.axis_size("py")
    flat = (NZ * ROWS, LANES)
    scratch = [pltpu.SMEM(strip_rows.shape, jnp.int32)] + [pltpu.VMEM(flat, jnp.float32)] * 2
    scratch += [vmem(ROWS), vmem(ROWS), vmem(2, 4), vmem(2, 4)]
    scratch += [vmem(e.at[8]) for e in (FOR_K, FOR_F)]
    scratch += [vmem(2, FINE + 2), vmem(6, 2, FINE), vmem(2, FINE), vmem(2, FINE)]
    scratch += [vmem(2, FINE + 2), vmem(2, FINE + 2)]
    scratch += [vmem(1, MID + 2), vmem(6, 1, MID), vmem(1, MID), vmem(1, MID), vmem(1, MID)]
    scratch += [vmem(1, MID + 2), vmem(1, MID + 2)]
    scratch += [vmem(LOW_TILES), vmem(6, 1, LOW_TILES), vmem(LOW_TILES)]
    scratch += [vmem(OWN2), vmem(16), vmem(2), vmem(OWN2), vmem(3, 2), vmem(3, LOW_COUNT)]
    scratch += [vmem(MID_ROWS // 2, 2), vmem(MID_TILES, 2), vmem(MID_ROWS // 2, 1), vmem(MID_TILES, 1)]
    row = lambda *shape: pltpu.VMEM(shape + (1, LANES), jnp.float32)
    scratch += [row(2, 2), row(2, size_y - 1, 2), row(2, 2), row(2, size_x - 1, 2)]
    scratch += [pltpu.VMEM((8, LANES, LANES), jnp.float32), pltpu.SemaphoreType.DMA((27,))]
    hbm = pl.BlockSpec(memory_space=pltpu.HBM)
    done = pl.pallas_call(
        kernel,
        out_shape=pltpu.VMEM(flat, jnp.float32),
        in_specs=[hbm, hbm, hbm],
        out_specs=pl.BlockSpec(memory_space=pltpu.VMEM),
        scratch_shapes=scratch,
        compiler_params=pltpu.CompilerParams(
            collective_id=0, has_side_effects=True, vmem_limit_bytes=60 << 20
        ),
        name="cycles",
    )(strip_rows, source.reshape(flat), coefficient.reshape(flat))
    return done.reshape(source.shape)


def solution(mesh):
    placed = (P(None, "px", "py"), P(None, "px", "py"), P())
    return jax.shard_map(
        shards, mesh=mesh, in_specs=placed, out_specs=P(None, "px", "py"), check_vma=False
    )
```
